32 devices in a mesh: ctx: 8 (over z, x), fsdp: 4 (over y, core).
Axes of the slice: x: 2, y: 2, z: 4, core: 2. Of those that a mesh axis runs over, the one named last changes fastest.
Arguments:
- tokens: bfloat16 [4, 8192, 512], P('fsdp', 'ctx'), may hold values from -6 to 6
- ln1_gain: bfloat16 [512], P('fsdp'), may hold values from 0.5 to 1.5
- ln1_shift: bfloat16 [512], P('fsdp'), may hold values from -1.1953125 to 1.1953125
- qkv_weight: bfloat16 [512, 1536], P('fsdp'), may hold values from -0.25 to 0.25
- qkv_bias: bfloat16 [1536], P('fsdp'), may hold values from -0.59765625 to 0.59765625
- out_weight: bfloat16 [512, 512], P('fsdp'), may hold values from -3 to 3
- out_bias: bfloat16 [512], P('fsdp'), may hold values from -1.1953125 to 1.1953125
- ln2_gain: bfloat16 [512], P('fsdp'), may hold values from 0.5 to 1.5
- ln2_shift: bfloat16 [512], P('fsdp'), may hold values from -1.1953125 to 1.1953125
- up_weight: bfloat16 [512, 2048], P('fsdp'), may hold values from -0.25 to 0.25
- up_bias: bfloat16 [2048], P('fsdp'), may hold values from -1.1953125 to 1.1953125
- down_weight: bfloat16 [2048, 512], P('fsdp'), may hold values from -0.125 to 0.125
- down_bias: bfloat16 [512], P('fsdp'), may hold values from -4 to 4
- seq_lengths: int32 [4, 9], P('fsdp'), may hold values from 128 to 4096, as said below
- span_order: int32 [4, 64], P('fsdp'), may hold values from 0 to 63, each once within a row
- cotangent: bfloat16 [4, 8192, 512], P('fsdp', 'ctx'), may hold values from -6 to 6
Outputs:
- mixed: bfloat16 [4, 8192, 512], P('fsdp', 'ctx')
- tokens_grad: float32 [4, 8192, 512], P('fsdp', 'ctx')
- ln1_gain_grad: float32 [512], P('fsdp')
- ln1_shift_grad: float32 [512], P('fsdp')
- qkv_weight_grad: float32 [512, 1536], P('fsdp')
- qkv_bias_grad: float32 [1536], P('fsdp')
- out_weight_grad: float32 [512, 512], P('fsdp')
- out_bias_grad: float32 [512], P('fsdp')
- ln2_gain_grad: float32 [512], P('fsdp')
- ln2_shift_grad: float32 [512], P('fsdp')
- up_weight_grad: float32 [512, 2048], P('fsdp')
- up_bias_grad: float32 [2048], P('fsdp')
- down_weight_grad: float32 [2048, 512], P('fsdp')
- down_bias_grad: float32 [512], P('fsdp')
The draws below stay inside these ranges and needn't reach their ends.
Inputs may be any that keep to these rules, and one draw needn't show every extreme that they name: `seq_lengths`: row g holds the lengths of group g's prompt and then of its 8 continuations, which follow one another in that order from the group's first position; each is a multiple of 128, and together they fill 8192 positions. The prompt holds 4096 positions; the continuations hold the other half, each between 128 and 896 positions. `span_order`: row g gives, for each slot of 128 rows of tokens[g] in row order, the span of the group that it holds (span b covers positions b * 128 to (b + 1) * 128 - 1); each span once.
All inputs are finite; a program needn't handle non-finite values.
Results may differ from the reference program's by a relative error of at most 0.013.
Values may be sent and summed in bfloat16 or wider, within the bound.
No kernel may reach another device: no remote copies, remote signals or barrier semaphores. Data moves between devices by JAX's collectives and lax.ppermute only.
A program may use at most 128 MiB of HBM per device.

```python
import jax
import jax.numpy as jnp
from jax import lax

D = 512
HEADS = 8
HEAD = 64
FF = 2048
SPAN = 128
CONTS = 8
GROUP_TOK = 8192
NSPAN = 64
GROUPS = 4


def group_lengths(group_key):
    half_spans = NSPAN // 2
    base_spans = half_spans // CONTS
    pairs = CONTS // 2
    first_key, second_key, third_key = jax.random.split(group_key, 3)
    deltas = jax.random.randint(first_key, (pairs,), 0, base_spans)
    chosen = jax.random.randint(second_key, (), 0, pairs)
    deltas = jnp.where(jnp.arange(pairs) == chosen, base_spans - 1, deltas)
    cont_spans = jnp.concatenate([base_spans + deltas, base_spans - deltas])
    cont_spans = jax.random.permutation(third_key, cont_spans)
    prompt_spans = jnp.full((1,), half_spans, jnp.int32)
    return jnp.concatenate([prompt_spans, cont_spans.astype(jnp.int32)]) * SPAN


def draw_seq_lengths(key, part):
    group_keys = jax.random.split(jax.random.fold_in(key, 7), GROUPS)
    return jax.vmap(group_lengths)(group_keys).astype(jnp.int32)


def draw_down_bias(key, part):
    size_key = jax.random.fold_in(jax.random.fold_in(key, 11), 1)
    values = 1.5 * jax.random.normal(size_key, (D,), jnp.float32)
    return jnp.clip(values, -4.0, 4.0).astype(jnp.bfloat16)


def block_scale(stream_key, shape, pieces, smallest, high):
    def one(position, blocks):
        steps = jax.random.uniform(jax.random.fold_in(jax.random.fold_in(stream_key, 6), position), (blocks,), jnp.float32, smallest / len(pieces), high / len(pieces))
        return jnp.repeat(jnp.exp(steps), shape[position] // blocks).reshape((-1,) + (1,) * (len(shape) - position - 1))

    loudness = one(*pieces[0])
    for cut in pieces[1:]:
        loudness = loudness * one(*cut)
    return loudness


def centred(stream_key, extent, scale, limit, cuts=(), dtype=jnp.bfloat16):
    result = scale * jax.random.normal(stream_key, extent, jnp.float32)
    if cuts:
        result = result * block_scale(stream_key, extent, cuts, -0.22, 0.18)
    return jnp.clip(result, -limit, limit).astype(dtype)


def setup_inputs(seed: int = 0) -> dict:
    streams_of = jax.random.split(jax.random.key(seed), 17)
    return {
        "tokens": centred(streams_of[0], (GROUPS, GROUP_TOK, D), 1.0, 6.0, ((0, 4), (1, 8))),
        "ln1_gain": jnp.clip(1.0 + 0.1 * jax.random.normal(streams_of[1], (D,), jnp.float32), 0.5, 1.5).astype(jnp.bfloat16),
        "ln1_shift": centred(streams_of[2], (D,), 0.2, 1.1953125, ((0, 4),)),
        "qkv_weight": centred(streams_of[3], (D, 3 * D), D ** -0.5, 0.25, ((0, 4),)),
        "qkv_bias": centred(streams_of[4], (3 * D,), 0.1, 0.59765625, ((0, 4),)),
        "out_weight": centred(streams_of[5], (D, D), (max(D // 128, 1)) ** -0.5, 3.0, ((0, 4),)),
        "out_bias": centred(streams_of[6], (D,), 0.2, 1.1953125, ((0, 4),)),
        "ln2_gain": jnp.clip(1.0 + 0.1 * jax.random.normal(streams_of[7], (D,), jnp.float32), 0.5, 1.5).astype(jnp.bfloat16),
        "ln2_shift": centred(streams_of[8], (D,), 0.2, 1.1953125, ((0, 4),)),
        "up_weight": centred(streams_of[9], (D, FF), D ** -0.5, 0.25, ((0, 4),)),
        "up_bias": centred(streams_of[10], (FF,), 0.2, 1.1953125, ((0, 4),)),
        "down_weight": centred(streams_of[11], (FF, D), FF ** -0.5, 0.125, ((0, 4),)),
        "down_bias": draw_down_bias(jax.random.fold_in(streams_of[16], 71), 0),
        "seq_lengths": draw_seq_lengths(jax.random.fold_in(streams_of[16], 71), 0),
        "span_order": jax.vmap(lambda own: jax.random.permutation(own, NSPAN))(jax.random.split(streams_of[14], GROUPS)).reshape((GROUPS, NSPAN)).astype(jnp.int32),
        "cotangent": centred(streams_of[15], (GROUPS, GROUP_TOK, D), 1.0, 6.0, ((0, 4), (1, 8))),
    }


EPSILON = 1e-05
MASKED = -1e+30
HIGHEST = lax.Precision.HIGHEST

@jax.custom_vjp
def low(v):
    return lax.optimization_barrier(v.astype(jnp.bfloat16)).astype(jnp.float32)

@jax.custom_vjp
def low_back(v):
    return v

def low_keep(v):
    return (low(v), None)

def low_pass(kept, grad):
    return (grad,)

def back_keep(v):
    return (v, None)

def back_low(kept, grad):
    return (low(grad),)
low.defvjp(low_keep, low_pass)
low_back.defvjp(back_keep, back_low)

def layer_norm(values, gain, shift):
    centre = values - lax.optimization_barrier(jnp.mean(values, axis=-1, keepdims=True))
    spread = lax.optimization_barrier(jnp.mean(centre * centre, axis=-1, keepdims=True))
    return centre * lax.rsqrt(spread + EPSILON) * gain + shift

def gelu_tanh(values):
    return jax.nn.gelu(values, approximate=True)

def exact_dot(left, right):
    return jnp.dot(left, right, precision=HIGHEST, preferred_element_type=jnp.float32)

def span_begins(lengths_row, span_ids):
    lengths_int = lengths_row.astype(jnp.int32)
    seq_ends = jnp.cumsum(lengths_int).astype(jnp.int32) // SPAN
    seq_starts = (seq_ends - lengths_int // SPAN).astype(jnp.int32)
    started = seq_starts[None, :] <= span_ids[:, None]
    return lax.optimization_barrier(jnp.max(jnp.where(started, seq_starts[None, :], 0), axis=1)).astype(jnp.int32)

def attend_block(packed_rows, row_spans, row_begins, span_keys, span_values, all_spans, prompt_spans):
    span_count = row_spans.shape[0]
    row_count = span_count * SPAN
    score_scale = HEAD ** (-0.5)
    shaped = packed_rows.reshape(span_count, SPAN, 3, HEADS, HEAD)
    queries = shaped[:, :, 0]
    key_rows = shaped[:, :, 1]
    value_rows = shaped[:, :, 2]
    nearby = low_back(jnp.einsum('sqhd,skhd->hsqk', queries, key_rows, precision=HIGHEST) * score_scale)
    offset = jnp.arange(SPAN)
    causal = offset[None, :] <= offset[:, None]
    nearby = jnp.where(causal, nearby, MASKED).reshape(HEADS, row_count, SPAN)
    flat_queries = queries.reshape(row_count, HEADS, HEAD)
    distant = low_back(jnp.einsum('rhd,jhd->hrj', flat_queries, span_keys.reshape(-1, HEADS, HEAD), precision=HIGHEST) * score_scale)
    query_span = jnp.repeat(row_spans, SPAN)
    query_begin = jnp.repeat(row_begins, SPAN)
    allowed = (all_spans[None, :] < query_span[:, None]) & ((all_spans[None, :] >= query_begin[:, None]) | (all_spans[None, :] < prompt_spans))
    distant = jnp.where(allowed[None], distant, MASKED)
    row_peak = jnp.maximum(lax.optimization_barrier(jnp.max(nearby, axis=-1)), lax.optimization_barrier(jnp.max(distant, axis=-1)))
    nearby_exp = jnp.exp(nearby - row_peak[..., None])
    distant_exp = jnp.exp(distant - row_peak[..., None])
    row_total = lax.optimization_barrier(jnp.sum(nearby_exp, axis=-1)) + lax.optimization_barrier(jnp.sum(distant_exp, axis=-1))
    near_weights = low(nearby_exp / row_total[..., None]).reshape(HEADS, span_count, SPAN, SPAN)
    far_weights = low(distant_exp / row_total[..., None])
    mixed_near = jnp.einsum('hsqk,skhd->sqhd', near_weights, value_rows, precision=HIGHEST).reshape(row_count, D)
    mixed_far = jnp.einsum('hrj,jhd->rhd', far_weights, span_values.reshape(-1, HEADS, HEAD), precision=HIGHEST).reshape(row_count, D)
    return low(low_back(mixed_near + mixed_far))

def group_forward(params, tokens_group, span_ids, lengths_row):
    ln1_gain, ln1_shift, qkv_weight, qkv_bias, out_weight, out_bias, ln2_gain, ln2_shift, up_weight, up_bias, down_weight, down_bias = params
    row_block = min(512, GROUP_TOK)
    blocks = GROUP_TOK // row_block
    per_block = row_block // SPAN

    def project(tokens_block):
        normed = low(layer_norm(tokens_block, ln1_gain, ln1_shift))
        return low(low_back(exact_dot(normed, qkv_weight) + qkv_bias))
    packed = lax.map(jax.checkpoint(project), tokens_group.reshape(blocks, row_block, D)).reshape(GROUP_TOK, 3 * D)
    inv_root = SPAN ** (-0.5)
    span_keys = low(lax.optimization_barrier(jnp.sum(packed[:, D:2 * D].reshape(NSPAN, SPAN, D), axis=1)) * inv_root)
    span_values = low(lax.optimization_barrier(jnp.sum(packed[:, 2 * D:].reshape(NSPAN, SPAN, D), axis=1)) * inv_root)
    begins = span_begins(lengths_row, span_ids)
    prompt_spans = lengths_row[0].astype(jnp.int32) // SPAN

    def attend(members):
        packed_rows, row_spans, row_begins = members
        return attend_block(packed_rows, row_spans, row_begins, span_keys, span_values, span_ids, prompt_spans)
    attended = lax.map(jax.checkpoint(attend), (packed.reshape(blocks, row_block, 3 * D), span_ids.reshape(blocks, per_block), begins.reshape(blocks, per_block)))

    def finish(members):
        tokens_block, heads_out = members
        residual = tokens_block + low_back(exact_dot(heads_out, out_weight) + out_bias)
        normed = low(layer_norm(residual, ln2_gain, ln2_shift))
        hidden = low_back(exact_dot(normed, up_weight) + up_bias)
        return residual + exact_dot(low(gelu_tanh(hidden)), down_weight) + down_bias
    finished = lax.map(jax.checkpoint(finish), (tokens_group.reshape(blocks, row_block, D), attended))
    return finished.reshape(GROUP_TOK, D)

def reference(tokens, ln1_gain, ln1_shift, qkv_weight, qkv_bias, out_weight, out_bias, ln2_gain, ln2_shift, up_weight, up_bias, down_weight, down_bias, seq_lengths, span_order, cotangent):
    params = tuple((p.astype(jnp.float32) for p in (ln1_gain, ln1_shift, qkv_weight, qkv_bias, out_weight, out_bias, ln2_gain, ln2_shift, up_weight, up_bias, down_weight, down_bias)))
    order_int = span_order.astype(jnp.int32)
    lengths_int = seq_lengths.astype(jnp.int32)

    def whole_layer(inputs, *weights):

        def step(carry, members):
            tokens_group, span_ids, lengths_row = members
            return (carry, jax.checkpoint(group_forward)(weights, tokens_group, span_ids, lengths_row))
        carry, outputs = lax.scan(step, jnp.zeros((), jnp.float32), (inputs, order_int, lengths_int))
        return outputs
    outputs, pull_back = jax.vjp(whole_layer, tokens.astype(jnp.float32), *params)
    grads = pull_back(cotangent.astype(jnp.float32))
    return (outputs.astype(jnp.bfloat16), grads[0], grads[1], grads[2], grads[3], grads[4], grads[5], grads[6], grads[7], grads[8], grads[9], grads[10], grads[11], grads[12])
```

```python
import functools

import jax
import jax.numpy as jnp
from jax import lax
from jax.experimental import pallas as pl
from jax.experimental.pallas import tpu as pltpu
from jax.sharding import PartitionSpec as P

D = 512
HEADS = 8
HEAD = 64
SPAN = 128
LANE = 128
PAIRS = D // LANE
ROWS = 256
EPSILON = 1e-05
MASKED = -1e30
SCALE = HEAD**-0.5
INV_ROOT = SPAN**-0.5
F32 = jnp.float32
BF16 = jnp.bfloat16
VMEM_LIMIT = 56 * 1024 * 1024

G1, S1, OB, G2, S2, DB, QB, UB = range(8)
SC_F, SC_SLOT, SC_LEN = 0, 1, 2


def dot(a, b):
    return lax.dot_general(a, b, (((1,), (0,)), ((), ())), preferred_element_type=F32)


def dot_bt(a, b):
    return lax.dot_general(a, b, (((1,), (1,)), ((), ())), preferred_element_type=F32)


def dot_at(a, b):
    return lax.dot_general(a, b, (((0,), (0,)), ((), ())), preferred_element_type=F32)


def normalize(values):
    centre = values - jnp.mean(values, axis=-1, keepdims=True)
    spread = jnp.mean(centre * centre, axis=-1, keepdims=True)
    rstd = lax.rsqrt(spread + EPSILON)
    return centre * rstd, rstd


def norm_back(e, n, rstd):
    return rstd * (
        e - jnp.mean(e, axis=-1, keepdims=True) - n * jnp.mean(e * n, axis=-1, keepdims=True)
    )


def params(steps, semantics=True):
    return pltpu.CompilerParams(
        dimension_semantics=("arbitrary",), vmem_limit_bytes=VMEM_LIMIT
    )


def full(shape):
    return pl.BlockSpec(shape, lambda i, *_: (0,) * len(shape))


def rows_of(shape):
    return pl.BlockSpec(shape, lambda i, *_: (i,) + (0,) * (len(shape) - 1))


def sums_kernel(x_ref, o_ref):
    spans = x_ref.shape[0] // SPAN
    sums = []
    for s in range(spans):
        n, _ = normalize(x_ref[s * SPAN : (s + 1) * SPAN, :].astype(F32))
        sums.append(jnp.sum(n, axis=0, keepdims=True))
    table = jnp.concatenate(sums, axis=0)
    for k in range(o_ref.shape[0]):
        o_ref[k] = table


def span_sums(x, copies):
    spans = x.shape[0] // SPAN
    return pl.pallas_call(
        sums_kernel,
        out_shape=jax.ShapeDtypeStruct((copies, spans, D), F32),
        compiler_params=pltpu.CompilerParams(vmem_limit_bytes=VMEM_LIMIT),
        name="span_sums",
    )(x)


def attend_kernel(
    sc, x_ref, order_ref, nsum_ref, *refs, nf, seqs
):
    qkv_refs, out_refs, small_refs = refs[:nf], refs[nf : 2 * nf], refs[2 * nf : 3 * nf]
    (packed_ref, p_ref, att_ref, r1_ref, h1_ref, h2_ref, wqkv, wout, vec, tabs) = refs[3 * nf :]
    i = pl.program_id(0)
    nspan = nsum_ref.shape[0]
    block = D // nf

    @pl.when(i == 0)
    def _():
        vec[...] = jnp.zeros_like(vec)
        for q in range(nf):
            fq = sc[SC_F] ^ q
            at = pl.ds(pl.multiple_of(fq * block, block), block)
            wqkv[at, :] = qkv_refs[q][...]
            wout[at, :] = out_refs[q][...]
            sm = small_refs[q][...].astype(F32)
            for row, src in ((G1, 0), (S1, 1), (OB, 5), (G2, 6), (S2, 7), (DB, 12)):
                vec[row : row + 1, at] = sm[src : src + 1]
            for t in range(3):
                at3 = pl.ds(pl.multiple_of(fq * 3 * block + t * block, block), block)
                vec[QB : QB + 1, at3] = sm[2 + t : 3 + t]
            for t in range(4):
                at4 = pl.ds(pl.multiple_of(fq * 4 * block + t * block, block), block)
                vec[UB : UB + 1, at4] = sm[8 + t : 9 + t]
        hs = nsum_ref[...] * vec[G1 : G1 + 1, :D] + SPAN * vec[S1 : S1 + 1, :D]
        hi = hs.astype(BF16)
        lo = (hs - hi.astype(F32)).astype(BF16)
        wkv = wqkv[:, D:]
        t = dot(hi, wkv) + dot(lo, wkv) + SPAN * vec[QB : QB + 1, D : 3 * D]
        tabs[...] = (t * INV_ROOT).astype(BF16)

    x = x_ref[...].astype(F32)
    n1, _ = normalize(x)
    h1 = (n1 * vec[G1 : G1 + 1, :D] + vec[S1 : S1 + 1, :D]).astype(BF16)
    h1_ref[...] = h1
    packed_ref[...] = (dot(h1, wqkv[...]) + vec[QB : QB + 1, : 3 * D]).astype(BF16)

    lane = lax.broadcasted_iota(jnp.int32, (SPAN, LANE), 1)
    low = lane < HEAD
    causal = jnp.where(
        lane <= lax.broadcasted_iota(jnp.int32, (SPAN, LANE), 0), 0.0, MASKED
    ).astype(F32)
    order = order_ref[...]
    prompt = lax.div(sc[SC_LEN], SPAN)
    spans = ROWS // SPAN
    for s in range(spans):
        a = sc[SC_LEN + seqs + sc[SC_SLOT] + i * spans + s]
        start, begin = 0, 0
        for k in range(seqs):
            begin = jnp.where(start <= a, start, begin)
            start = start + lax.div(sc[SC_LEN + k], SPAN)
        seen = (order < a) & ((order >= begin) | (order < prompt))
        far = jnp.where(seen, 0.0, MASKED).astype(F32)
        bias = jnp.concatenate([causal, jnp.broadcast_to(far, (SPAN, nspan))], axis=1)
        bias = jnp.concatenate([bias, bias], axis=0)
        at = slice(s * SPAN, (s + 1) * SPAN)
        for p in range(PAIRS):
            cols = slice(p * LANE, (p + 1) * LANE)
            q = packed_ref[at, cols] * SCALE
            k = packed_ref[at, D + p * LANE : D + (p + 1) * LANE]
            v = packed_ref[at, 2 * D + p * LANE : 2 * D + (p + 1) * LANE]
            zero = jnp.zeros_like(q)
            q2 = jnp.concatenate([jnp.where(low, q, zero), jnp.where(low, zero, q)], axis=0)
            kc = jnp.concatenate([k, tabs[:, cols]], axis=0)
            vc = jnp.concatenate([v, tabs[:, D + p * LANE : D + (p + 1) * LANE]], axis=0)
            scores = dot_bt(q2, kc) + bias
            peak = jnp.max(scores, axis=1, keepdims=True)
            e = jnp.exp(scores - peak)
            w = (e * (1.0 / jnp.sum(e, axis=1, keepdims=True))).astype(BF16)
            p_ref[s * PAIRS + p] = w
            o2 = dot(w, vc)
            att_ref[at, cols] = jnp.where(low, o2[:SPAN], o2[SPAN:]).astype(BF16)

    r1 = x + (dot(att_ref[...], wout[...]) + vec[OB : OB + 1, :D])
    r1_ref[...] = r1
    n2, _ = normalize(r1)
    h2_ref[...] = (n2 * vec[G2 : G2 + 1, :D] + vec[S2 : S2 + 1, :D]).astype(BF16)


def attend(sc, x, order, nsum, qkv, out, small, seqs):
    nf = len(qkv)
    rows = x.shape[0]
    nspan = nsum.shape[0]
    keys = SPAN + nspan
    per = ROWS // SPAN * PAIRS
    return pl.pallas_call(
        functools.partial(attend_kernel, nf=nf, seqs=seqs),
        grid_spec=pltpu.PrefetchScalarGridSpec(
            num_scalar_prefetch=1,
            grid=(rows // ROWS,),
            in_specs=[rows_of((ROWS, D)), full((1, nspan)), full((nspan, D))]
            + [full(a.shape) for a in (*qkv, *out, *small)],
            out_specs=[
                rows_of((ROWS, 3 * D)),
                rows_of((per, 2 * SPAN, keys)),
                rows_of((ROWS, D)),
                rows_of((ROWS, D)),
                rows_of((ROWS, D)),
                rows_of((ROWS, D)),
                full((D, 3 * D)),
                full((D, D)),
                full((8, 4 * D)),
                full((nspan, 2 * D)),
            ],
        ),
        out_shape=[
            jax.ShapeDtypeStruct((rows, 3 * D), BF16),
            jax.ShapeDtypeStruct((rows // SPAN * PAIRS, 2 * SPAN, keys), BF16),
            jax.ShapeDtypeStruct((rows, D), BF16),
            jax.ShapeDtypeStruct((rows, D), F32),
            jax.ShapeDtypeStruct((rows, D), BF16),
            jax.ShapeDtypeStruct((rows, D), BF16),
            jax.ShapeDtypeStruct((D, 3 * D), BF16),
            jax.ShapeDtypeStruct((D, D), BF16),
            jax.ShapeDtypeStruct((8, 4 * D), F32),
            jax.ShapeDtypeStruct((nspan, 2 * D), BF16),
        ],
        compiler_params=params(1),
        name="attend",
    )(sc, x, order, nsum, *qkv, *out, *small)


def relative(step, nf):
    half = nf // 2
    return jnp.where(step < half, 2 * step + 1, 2 * (step - half))


def up_kernel(sc, h2_ref, c_ref, vec_ref, *refs, nf):
    up_refs = refs[:nf]
    g_ref, gp_ref, w_ref, send_ref, keep_ref = refs[nf:]
    s = pl.program_id(0)
    f = sc[SC_F] ^ relative(s, nf)
    block = D // nf
    for q in range(nf):
        at = pl.ds(pl.multiple_of((sc[SC_F] ^ q) * block, block), block)
        w_ref[at, :] = up_refs[q][...]
    width = w_ref.shape[1]
    bias = vec_ref[UB : UB + 1, pl.ds(pl.multiple_of(f * width, width), width)]
    w = w_ref[...]
    k0 = 0.7978845608028654
    for r in range(0, h2_ref.shape[0], ROWS):
        u = dot(h2_ref[r : r + ROWS, :], w) + bias
        u2 = u * u
        t = jnp.tanh(u * (k0 + (k0 * 0.044715) * u2))
        half = 0.5 + 0.5 * t
        g_ref[r : r + ROWS, :] = (u * half).astype(BF16)
        slope = u * (k0 + (3 * k0 * 0.044715) * u2)
        gp_ref[r : r + ROWS, :] = (half + (0.5 - 0.5 * t * t) * slope).astype(BF16)
    grad = dot_at(g_ref[...], c_ref[...]).astype(BF16)

    def store(ref):
        for j in range(D // LANE):
            ref[0, j * width : (j + 1) * width, :] = grad[:, j * LANE : (j + 1) * LANE]

    @pl.when(s < nf // 2)
    def _():
        store(send_ref)

    @pl.when(s >= nf // 2)
    def _():
        store(keep_ref)


def ffn_up(sc, h2, c, vec, up):
    nf = len(up)
    rows = h2.shape[0]
    ff = up[0].shape[1]
    width = ff // nf
    half = nf // 2
    at = lambda s, sc: (0, sc[SC_F] ^ relative(s, nf))
    piece = width * D // LANE
    return pl.pallas_call(
        functools.partial(up_kernel, nf=nf),
        grid_spec=pltpu.PrefetchScalarGridSpec(
            num_scalar_prefetch=1,
            grid=(nf,),
            in_specs=[full((rows, D)), full((rows, D)), full(vec.shape)]
            + [pl.BlockSpec((D // nf, width), at) for _ in up],
            out_specs=[
                pl.BlockSpec((rows, width), at),
                pl.BlockSpec((rows, width), at),
                pl.BlockSpec((D, width), at),
                pl.BlockSpec((1, piece, LANE), lambda s, sc: (jnp.minimum(s, half - 1), 0, 0)),
                pl.BlockSpec((1, piece, LANE), lambda s, sc: (jnp.maximum(s - half, 0), 0, 0)),
            ],
        ),
        out_shape=[
            jax.ShapeDtypeStruct((rows, ff), BF16),
            jax.ShapeDtypeStruct((rows, ff), BF16),
            jax.ShapeDtypeStruct((D, ff), BF16),
            jax.ShapeDtypeStruct((half, piece, LANE), BF16),
            jax.ShapeDtypeStruct((half, piece, LANE), BF16),
        ],
        compiler_params=params(1),
        name="ffn_up",
    )(sc, h2, c, vec, *up)


def down_kernel(sc, h2_ref, c_ref, gp_ref, w_ref, *refs, nf):
    down_refs = refs[:nf]
    dh2_ref, dub_ref, wd_ref, send_ref, keep_ref, du_ref, grad_ref = refs[nf:]
    s = pl.program_id(0)
    for q in range(nf):

        @pl.when(s == q)
        def _():
            wd_ref[...] = down_refs[q][...]

    @pl.when(s == 0)
    def _():
        dh2_ref[...] = jnp.zeros_like(dh2_ref)

    wd = wd_ref[...]
    w = w_ref[...]
    total = jnp.zeros((1, w.shape[1]), F32)
    for r in range(0, h2_ref.shape[0], ROWS):
        at = slice(r, r + ROWS)
        dg = dot_bt(c_ref[at, :], wd)
        du = (dg * gp_ref[at, :].astype(F32)).astype(BF16)
        du_ref[at, :] = du
        total = total + jnp.sum(du.astype(F32), axis=0, keepdims=True)
        dh2_ref[at, :] += dot_bt(du, w)
    dub_ref[...] = total
    grad_ref[...] = dot_at(h2_ref[...], du_ref[...])
    block = D // nf
    for q in range(nf):
        ref = send_ref if q % 2 else keep_ref
        piece = grad_ref[pl.ds(pl.multiple_of((sc[SC_F] ^ q) * block, block), block), :]
        piece = piece.astype(BF16)
        for j in range(w.shape[1] // LANE):
            ref[q // 2, j * block : (j + 1) * block, :] = piece[:, j * LANE : (j + 1) * LANE]


def ffn_down(sc, h2, c, gp, w, down):
    nf = len(down)
    rows = h2.shape[0]
    ff = w.shape[1]
    width = ff // nf
    half = nf // 2
    block = D // nf
    part = width // LANE * block
    cols = lambda s, sc: (0, sc[SC_F] ^ s)
    return pl.pallas_call(
        functools.partial(down_kernel, nf=nf),
        grid_spec=pltpu.PrefetchScalarGridSpec(
            num_scalar_prefetch=1,
            grid=(nf,),
            in_specs=[
                full((rows, D)),
                full((rows, D)),
                pl.BlockSpec((rows, width), cols),
                pl.BlockSpec((D, width), cols),
            ]
            + [full(a.shape) for a in down],
            out_specs=[
                full((rows, D)),
                pl.BlockSpec((1, width), cols),
                pl.BlockSpec((width, D), lambda s, sc: (sc[SC_F] ^ s, 0)),
                pl.BlockSpec((half, part, LANE), lambda s, sc: (0, sc[SC_F] ^ s, 0)),
                pl.BlockSpec((half, part, LANE), lambda s, sc: (0, sc[SC_F] ^ s, 0)),
            ],
            scratch_shapes=[pltpu.VMEM((rows, width), BF16), pltpu.VMEM((D, width), F32)],
        ),
        out_shape=[
            jax.ShapeDtypeStruct((rows, D), F32),
            jax.ShapeDtypeStruct((1, ff), F32),
            jax.ShapeDtypeStruct((ff, D), BF16),
            jax.ShapeDtypeStruct((half, part * nf, LANE), BF16),
            jax.ShapeDtypeStruct((half, part * nf, LANE), BF16),
        ],
        compiler_params=params(1),
        name="ffn_down",
    )(sc, h2, c, gp, w, *down)


def back_kernel(
    sc, x_ref, c_ref, dh2_ref, r1_ref, att_ref, h1_ref, packed_ref, p_ref,
    tabs, wqkv, wout, vec, nsum_ref, dub_ref,
    dr1_ref, dh1_ref, dspan_ref, send_ref, keep_ref,
    acc_qkv, acc_out, acc_span, accv, dp_ref, *, nf
):
    i = pl.program_id(0)
    last = pl.num_programs(0) - 1

    @pl.when(i == 0)
    def _():
        for ref in (acc_qkv, acc_out, acc_span, accv):
            ref[...] = jnp.zeros_like(ref)

    def add(row, values):
        accv[row : row + 1, : values.shape[1]] += jnp.sum(values, axis=0, keepdims=True)

    c = c_ref[...].astype(F32)
    dh2 = dh2_ref[...]
    n2, rstd2 = normalize(r1_ref[...])
    add(G2, dh2 * n2)
    add(S2, dh2)
    add(DB, c)
    dr1 = c + norm_back(dh2 * vec[G2 : G2 + 1, :D], n2, rstd2)
    dr1_ref[...] = dr1
    dy = dr1.astype(BF16)
    add(OB, dy.astype(F32))
    att = att_ref[...]
    acc_out[...] += dot_at(att, dy)
    da = dot_bt(dy, wout[...]).astype(BF16)

    low = lax.broadcasted_iota(jnp.int32, (SPAN, LANE), 1) < HEAD
    for s in range(ROWS // SPAN):
        at = slice(s * SPAN, (s + 1) * SPAN)
        for p in range(PAIRS):
            cq, ck, cv = (slice(t * D + p * LANE, t * D + (p + 1) * LANE) for t in range(3))
            cp = slice(D + p * LANE, D + (p + 1) * LANE)
            q = packed_ref[at, cq] * SCALE
            do = da[at, cq]
            zero = jnp.zeros_like(q)
            q2 = jnp.concatenate([jnp.where(low, q, zero), jnp.where(low, zero, q)], axis=0)
            do2 = jnp.concatenate([jnp.where(low, do, zero), jnp.where(low, zero, do)], axis=0)
            kc = jnp.concatenate([packed_ref[at, ck], tabs[:, cq]], axis=0)
            vc = jnp.concatenate([packed_ref[at, cv], tabs[:, cp]], axis=0)
            w = p_ref[s * PAIRS + p]
            wf = w.astype(F32)
            dp = dot_bt(do2, vc)
            delta = jnp.sum(wf * dp, axis=1, keepdims=True)
            ds = (wf * (dp - delta)).astype(BF16)
            dq2 = dot(ds, kc)
            dq = jnp.where(low, dq2[:SPAN], dq2[SPAN:]) * SCALE
            dk = dot_at(ds, q2)
            dv = dot_at(w, do2)
            acc_span[:, cq] += dk[SPAN:]
            acc_span[:, cp] += dv[SPAN:]
            dp_ref[at, cq] = dq.astype(BF16)
            dp_ref[at, ck] = dk[:SPAN].astype(BF16)
            dp_ref[at, cv] = dv[:SPAN].astype(BF16)
    dpk = dp_ref[...]
    add(QB, dpk.astype(F32))
    acc_qkv[...] += dot_at(h1_ref[...], dpk)
    dh1 = dot_bt(dpk, wqkv[...])
    dh1_ref[...] = dh1
    n1, _ = normalize(x_ref[...].astype(F32))
    add(G1, dh1 * n1)
    add(S1, dh1)

    @pl.when(i == last)
    def _():
        span = acc_span[...]
        copies, own = dspan_ref.shape[0], dspan_ref.shape[1]
        for k in range(copies):
            dspan_ref[k] = span[k * own : (k + 1) * own].astype(BF16)
        span = span * INV_ROOT
        low_span = span.astype(BF16)
        nsum = nsum_ref[...]
        hs = (nsum * vec[G1 : G1 + 1, :D] + SPAN * vec[S1 : S1 + 1, :D]).astype(BF16)
        acc_qkv[:, D:] += dot_at(hs, low_span)
        accv[QB : QB + 1, D : 3 * D] += SPAN * jnp.sum(span, axis=0, keepdims=True)
        de = dot_bt(low_span, wqkv[:, D:])
        add(G1, de * nsum)
        accv[S1 : S1 + 1, :D] += SPAN * jnp.sum(de, axis=0, keepdims=True)
        block = D // nf
        for q in range(nf):
            ref = send_ref if q % 2 else keep_ref
            fq = sc[SC_F] ^ q
            at = pl.ds(pl.multiple_of(fq * block, block), block)
            piece = acc_qkv[at, :].astype(BF16)
            for j in range(3 * D // LANE):
                ref[q // 2, j * block : (j + 1) * block, :] = piece[:, j * LANE : (j + 1) * LANE]
            base = 3 * D // LANE * block
            piece = acc_out[at, :].astype(BF16)
            for j in range(D // LANE):
                ref[q // 2, base + j * block : base + (j + 1) * block, :] = piece[
                    :, j * LANE : (j + 1) * LANE
                ]
            base += D // LANE * block
            three = [
                accv[QB : QB + 1, pl.ds(pl.multiple_of(fq * 3 * block + t * block, block), block)]
                for t in range(3)
            ]
            four = [
                dub_ref[0:1, pl.ds(pl.multiple_of(fq * 4 * block + t * block, block), block)]
                for t in range(4)
            ]
            small = jnp.concatenate(
                [accv[G1 : G1 + 1, at], accv[S1 : S1 + 1, at]]
                + three
                + [accv[OB : OB + 1, at], accv[G2 : G2 + 1, at], accv[S2 : S2 + 1, at]]
                + four
                + [accv[DB : DB + 1, at], jnp.zeros((3, LANE), F32)],
                axis=0,
            ).astype(BF16)
            ref[q // 2, base : base + 16, :] = small
            ref[q // 2, base + 16 : base + block, :] = jnp.zeros((block - 16, LANE), BF16)


def back(sc, x, c, dh2, r1, att, h1, packed, p, tabs, wqkv, wout, vec, nsum, dub, nf, copies):
    rows = x.shape[0]
    nspan = nsum.shape[0]
    per = ROWS // SPAN * PAIRS
    half = nf // 2
    piece = (4 * D // LANE + 1) * (D // nf)
    return pl.pallas_call(
        functools.partial(back_kernel, nf=nf),
        grid_spec=pltpu.PrefetchScalarGridSpec(
            num_scalar_prefetch=1,
            grid=(rows // ROWS,),
            in_specs=[rows_of((ROWS, D))] * 6
            + [rows_of((ROWS, 3 * D)), rows_of((per,) + p.shape[1:])]
            + [full(a.shape) for a in (tabs, wqkv, wout, vec, nsum, dub)],
            out_specs=[
                rows_of((ROWS, D)),
                rows_of((ROWS, D)),
                full((copies, nspan // copies, 2 * D)),
                full((half, piece, LANE)),
                full((half, piece, LANE)),
            ],
            scratch_shapes=[
                pltpu.VMEM((D, 3 * D), F32),
                pltpu.VMEM((D, D), F32),
                pltpu.VMEM((nspan, 2 * D), F32),
                pltpu.VMEM((8, 3 * D), F32),
                pltpu.VMEM((ROWS, 3 * D), BF16),
            ],
        ),
        out_shape=[
            jax.ShapeDtypeStruct((rows, D), F32),
            jax.ShapeDtypeStruct((rows, D), F32),
            jax.ShapeDtypeStruct((copies, nspan // copies, 2 * D), BF16),
            jax.ShapeDtypeStruct((half, piece, LANE), BF16),
            jax.ShapeDtypeStruct((half, piece, LANE), BF16),
        ],
        compiler_params=params(1),
        name="back",
    )(sc, x, c, dh2, r1, att, h1, packed, p, tabs, wqkv, wout, vec, nsum, dub)


def first_kernel(x_ref, dr1_ref, dh1_ref, got_ref, wqkv, vec, o_ref, e_ref):
    i = pl.program_id(0)

    @pl.when(i == 0)
    def _():
        total = jnp.sum(got_ref[...].astype(F32), axis=0) * INV_ROOT
        e_ref[...] = dot_bt(total.astype(BF16), wqkv[:, D:])

    n1, rstd1 = normalize(x_ref[...].astype(F32))
    spans = ROWS // SPAN
    extra = jnp.concatenate(
        [
            jnp.broadcast_to(e_ref[pl.ds(i * spans + s, 1), :], (SPAN, D))
            for s in range(spans)
        ],
        axis=0,
    )
    dh1 = dh1_ref[...] + extra
    o_ref[...] = dr1_ref[...] + norm_back(dh1 * vec[G1 : G1 + 1, :D], n1, rstd1)


def first_back(x, dr1, dh1, got, wqkv, vec):
    rows = x.shape[0]
    return pl.pallas_call(
        first_kernel,
        grid=(rows // ROWS,),
        in_specs=[rows_of((ROWS, D))] * 3 + [full(a.shape) for a in (got, wqkv, vec)],
        out_specs=rows_of((ROWS, D)),
        out_shape=jax.ShapeDtypeStruct((rows, D), F32),
        scratch_shapes=[pltpu.VMEM((rows // SPAN, D), F32)],
        compiler_params=params(1),
        name="first_back",
    )(x, dr1, dh1, got, wqkv, vec)


def mixed_kernel(r1_ref, g_ref, w_ref, vec, o_ref):
    o_ref[...] = (r1_ref[...] + dot(g_ref[...], w_ref[...]) + vec[DB : DB + 1, :D]).astype(BF16)


def block_output(r1, g, w, vec):
    rows = r1.shape[0]
    return pl.pallas_call(
        mixed_kernel,
        grid=(rows // ROWS,),
        in_specs=[rows_of((ROWS, D)), rows_of((ROWS, g.shape[1])), full(w.shape), full(vec.shape)],
        out_specs=rows_of((ROWS, D)),
        out_shape=jax.ShapeDtypeStruct((rows, D), BF16),
        compiler_params=params(1),
        name="block_output",
    )(r1, g, w, vec)


def swap(array, axis, bit):
    n = lax.axis_size(axis)
    return lax.ppermute(array, axis, [(k, k ^ bit) for k in range(n)])


def gathered(array, axis):
    n = lax.axis_size(axis)
    held = {0: array}
    bit = n // 2
    while bit:
        for r in sorted(held):
            held[r ^ bit] = swap(held[r], axis, bit)
        bit //= 2
    return [held[r] for r in range(n)]


def add_low(a, b):
    return (a.astype(F32) + b.astype(F32)).astype(BF16)


def to_owner(keep, send, axis):
    n = lax.axis_size(axis)
    bit = 1
    while True:
        keep = add_low(keep, swap(send, axis, bit))
        bit *= 2
        if bit == n:
            return keep[0]
        keep, send = keep[0::2], keep[1::2]


def over_all(piece, axis):
    n = lax.axis_size(axis)
    split = piece.reshape(n, piece.shape[0] // n, LANE)
    got = lax.all_to_all(split, axis, 0, 0, tiled=True)
    own = got.astype(F32).sum(axis=0).astype(BF16)
    wide = jnp.broadcast_to(own[None], (n,) + own.shape)
    return lax.all_to_all(wide, axis, 0, 0, tiled=True).reshape(piece.shape).astype(F32)


def unblocked(rows, height):
    blocks = rows.reshape(-1, height, LANE)
    return jnp.swapaxes(blocks, 0, 1).reshape(height, -1)


def local(
    tokens, ln1_gain, ln1_shift, qkv_weight, qkv_bias, out_weight, out_bias, ln2_gain, ln2_shift,
    up_weight, up_bias, down_weight, down_bias, seq_lengths, span_order, cotangent,
):
    nf = lax.axis_size("fsdp")
    nc = lax.axis_size("ctx")
    x, c = tokens[0], cotangent[0]
    spans = x.shape[0] // SPAN
    seqs = seq_lengths.shape[1]
    small = jnp.concatenate(
        [ln1_gain, ln1_shift, qkv_bias, out_bias, ln2_gain, ln2_shift, up_bias, down_bias]
    )
    small = jnp.pad(small, (0, 16 * LANE - small.shape[0])).reshape(16, LANE)
    scalars = jnp.concatenate(
        [
            lax.axis_index("fsdp").reshape(1),
            (lax.axis_index("ctx") * spans).reshape(1),
            seq_lengths[0],
            span_order[0],
        ]
    ).astype(jnp.int32)
    qkv = gathered(qkv_weight, "fsdp")
    smalls = gathered(small, "fsdp")
    out = gathered(out_weight, "fsdp")
    up = gathered(up_weight, "fsdp")
    down = gathered(down_weight, "fsdp")
    nsum = lax.all_to_all(span_sums(x, nc), "ctx", 0, 0, tiled=True).reshape(nc * spans, D)

    packed, p, att, r1, h1, h2, wqkv, wout, vec, tabs = attend(
        scalars, x, span_order, nsum, qkv, out, smalls, seqs
    )
    g, gp, wup, dsend, dkeep = ffn_up(scalars, h2, c, vec, up)
    dh2, dub, wdown, usend, ukeep = ffn_down(scalars, h2, c, gp, wup, down)
    dr1, dh1, dspan, bsend, bkeep = back(
        scalars, x, c, dh2, r1, att, h1, packed, p, tabs, wqkv, wout, vec, nsum, dub, nf, nc
    )
    got = lax.all_to_all(dspan, "ctx", 0, 0, tiled=True)
    tokens_grad = first_back(x, dr1, dh1, got, wqkv, vec)
    mixed = block_output(r1, g, wdown, vec)

    grad_down = unblocked(over_all(to_owner(dkeep, dsend, "fsdp"), "ctx"), down_weight.shape[0])
    grad_up = unblocked(over_all(to_owner(ukeep, usend, "fsdp"), "ctx"), D // nf)
    rest = over_all(to_owner(bkeep, bsend, "fsdp"), "ctx")
    block = D // nf
    at_out = 3 * D // LANE * block
    at_small = 4 * D // LANE * block
    grad_qkv = unblocked(rest[:at_out], block)
    grad_out = unblocked(rest[at_out:at_small], block)
    tail = rest[at_small : at_small + 16].reshape(-1)
    pieces, at = [], 0
    for width in (block, block, 3 * block, block, block, block, 4 * block, block):
        pieces.append(tail[at : at + width])
        at += width
    g1, s1, qb, ob, g2, s2, ub, db = pieces
    return (
        mixed[None], tokens_grad[None], g1, s1, grad_qkv, qb, grad_out, ob, g2, s2,
        grad_up, ub, grad_down, db,
    )


def solution(mesh):
    rows, one, two = P("fsdp", "ctx", None), P("fsdp"), P("fsdp", None)
    return jax.shard_map(
        local,
        mesh=mesh,
        in_specs=(
            rows, one, one, two, one, two, one, one, one, two, one, two, one, two, two, rows,
        ),
        out_specs=(rows, rows, one, one, two, one, two, one, one, one, two, one, two, one),
        check_vma=False,
    )
```

```python
import functools

import jax
import jax.numpy as jnp
from jax import lax
from jax.experimental import pallas as pl
from jax.experimental.pallas import tpu as pltpu
from jax.sharding import PartitionSpec as P

D = 512
HEADS = 8
HEAD = 64
SPAN = 128
LANE = 128
PAIRS = D // LANE
ROWS = 256
EPSILON = 1e-05
MASKED = -1e30
SCALE = HEAD**-0.5
INV_ROOT = SPAN**-0.5
F32 = jnp.float32
BF16 = jnp.bfloat16

G1, S1, OB, G2, S2, DB, QB, UB = range(8)
SC_F, SC_C, SC_SLOT, SC_LEN = range(4)


def dot(a, b):
    return lax.dot_general(a, b, (((1,), (0,)), ((), ())), preferred_element_type=F32)


def dot_bt(a, b):
    return lax.dot_general(a, b, (((1,), (1,)), ((), ())), preferred_element_type=F32)


def dot_at(a, b):
    return lax.dot_general(a, b, (((0,), (0,)), ((), ())), preferred_element_type=F32)


def normalize(values):
    centre = values - jnp.mean(values, axis=-1, keepdims=True)
    spread = jnp.mean(centre * centre, axis=-1, keepdims=True)
    rstd = lax.rsqrt(spread + EPSILON)
    return centre * rstd, rstd


def norm_back(e, n, rstd):
    return rstd * (
        e - jnp.mean(e, axis=-1, keepdims=True) - n * jnp.mean(e * n, axis=-1, keepdims=True)
    )


def params(mib):
    return pltpu.CompilerParams(vmem_limit_bytes=mib * 1024 * 1024)


def in_vmem(count):
    return [pl.BlockSpec(memory_space=pltpu.VMEM) for _ in range(count)]


def cost(micros):
    return pl.CostEstimate(
        flops=int(micros * 1e9), transcendentals=0, bytes_accessed=int(micros * 1e6)
    )


def resident(kernel, name, micros, mib, scalars, arrays, outs, scratch=()):
    return pl.pallas_call(
        kernel,
        in_specs=[pl.BlockSpec(memory_space=pltpu.SMEM)] * len(scalars) + in_vmem(len(arrays)),
        out_specs=in_vmem(len(outs)),
        out_shape=[jax.ShapeDtypeStruct(shape, dtype) for shape, dtype in outs],
        scratch_shapes=list(scratch),
        compiler_params=params(mib),
        name=name,
        cost_estimate=cost(micros),
    )(*scalars, *arrays)


def block_rows(i, size=ROWS):
    return pl.ds(pl.multiple_of(i * size, size), size)


def each_block(rows, body):
    def step(i, carry):
        body(i)
        return carry

    lax.fori_loop(0, rows // ROWS, step, 0)


def sums_kernel(x_ref, o_ref):
    spans = x_ref.shape[0] // SPAN
    sums = []
    for s in range(spans):
        n, _ = normalize(x_ref[s * SPAN : (s + 1) * SPAN, :].astype(F32))
        sums.append(jnp.sum(n, axis=0, keepdims=True))
    table = jnp.concatenate(sums, axis=0)
    for k in range(o_ref.shape[0]):
        o_ref[k] = table


def span_sums(x, copies):
    spans = x.shape[0] // SPAN
    return resident(sums_kernel, "span_sums", 3, 16, (), (x,), [((copies, spans, D), F32)])[0]


def pack_kernel(qkv_ref, out_ref, *refs):
    o_ref = refs[-1]
    rows, width = qkv_ref.shape
    o_ref[:rows, :width] = qkv_ref[...]
    o_ref[:rows, width:] = out_ref[...]
    parts = [ref[...].astype(F32) for ref in refs[:-1]]
    used = sum(part.shape[0] for part in parts)
    parts.append(jnp.zeros((16 - used, LANE), F32))
    o_ref[rows:, :LANE] = jnp.concatenate(parts, axis=0).astype(BF16)
    o_ref[rows:, LANE:] = jnp.zeros((16, o_ref.shape[1] - LANE), BF16)


def packed_params(qkv, out, vectors):
    shape = (qkv.shape[0] + 16, qkv.shape[1] + out.shape[1])
    vectors = [v.reshape(-1, LANE) for v in vectors]
    arrays = [qkv, out] + vectors
    return pl.pallas_call(
        pack_kernel,
        out_shape=jax.ShapeDtypeStruct(shape, BF16),
        compiler_params=params(58),
        name="pack",
        cost_estimate=cost(1),
    )(*arrays)


def attend_kernel(sc, x_ref, order_ref, nsum_ref, *refs, nf, seqs):
    param_refs = refs[:nf]
    (packed_ref, p_ref, att_ref, h1_ref, wqkv, wout, vec, tabs) = refs[nf:]
    nspan = nsum_ref.shape[0]
    block = D // nf

    vec[...] = jnp.zeros_like(vec)
    for q in range(nf):
        fq = sc[SC_F] ^ q
        at = pl.ds(pl.multiple_of(fq * block, block), block)
        wqkv[at, :] = param_refs[q][:block, : 3 * D]
        wout[at, :] = param_refs[q][:block, 3 * D :]
        sm = param_refs[q][block:, :LANE].astype(F32)
        for row, src in ((G1, 0), (S1, 1), (OB, 5), (G2, 6), (S2, 7), (DB, 12)):
            vec[row : row + 1, at] = sm[src : src + 1]
        for t in range(3):
            at3 = pl.ds(pl.multiple_of(fq * 3 * block + t * block, block), block)
            vec[QB : QB + 1, at3] = sm[2 + t : 3 + t]
        for t in range(4):
            at4 = pl.ds(pl.multiple_of(fq * 4 * block + t * block, block), block)
            vec[UB : UB + 1, at4] = sm[8 + t : 9 + t]
    hs = nsum_ref[...] * vec[G1 : G1 + 1, :D] + SPAN * vec[S1 : S1 + 1, :D]
    hi = hs.astype(BF16)
    lo = (hs - hi.astype(F32)).astype(BF16)
    t = dot(hi, wqkv[:, D:]) + dot(lo, wqkv[:, D:]) + SPAN * vec[QB : QB + 1, D : 3 * D]
    tabs[...] = (t * INV_ROOT).astype(BF16)
    prompt = lax.div(sc[SC_LEN], SPAN)
    spans = ROWS // SPAN

    def body(i):
        rows = block_rows(i)
        n1, _ = normalize(x_ref[rows, :].astype(F32))
        h1 = (n1 * vec[G1 : G1 + 1, :D] + vec[S1 : S1 + 1, :D]).astype(BF16)
        h1_ref[rows, :] = h1
        packed_ref[rows, :] = (dot(h1, wqkv[...]) + vec[QB : QB + 1, : 3 * D]).astype(BF16)

        lane = lax.broadcasted_iota(jnp.int32, (SPAN, LANE), 1)
        low = lane < HEAD
        causal = jnp.where(
            lane <= lax.broadcasted_iota(jnp.int32, (SPAN, LANE), 0), 0.0, MASKED
        ).astype(F32)
        order = order_ref[...]
        for s in range(spans):
            a = sc[SC_LEN + seqs + sc[SC_SLOT] + i * spans + s]
            start, begin = 0, 0
            for k in range(seqs):
                begin = jnp.where(start <= a, start, begin)
                start = start + lax.div(sc[SC_LEN + k], SPAN)
            seen = (order < a) & ((order >= begin) | (order < prompt))
            far = jnp.where(seen, 0.0, MASKED).astype(F32)
            bias = jnp.concatenate([causal, jnp.broadcast_to(far, (SPAN, nspan))], axis=1)
            bias = jnp.concatenate([bias, bias], axis=0)
            at = block_rows(i * spans + s, SPAN)
            for p in range(PAIRS):
                cq, ck, cv = (slice(t * D + p * LANE, t * D + (p + 1) * LANE) for t in range(3))
                q = packed_ref[at, cq] * SCALE
                zero = jnp.zeros_like(q)
                q2 = jnp.concatenate([jnp.where(low, q, zero), jnp.where(low, zero, q)], axis=0)
                kc = jnp.concatenate([packed_ref[at, ck], tabs[:, cq]], axis=0)
                vc = jnp.concatenate([packed_ref[at, cv], tabs[:, ck]], axis=0)
                scores = dot_bt(q2, kc) + bias
                peak = jnp.max(scores, axis=1, keepdims=True)
                e = jnp.exp(scores - peak)
                w = (e * (1.0 / jnp.sum(e, axis=1, keepdims=True))).astype(BF16)
                p_ref[(i * spans + s) * PAIRS + p] = w
                o2 = dot(w, vc)
                att_ref[at, cq] = jnp.where(low, o2[:SPAN], o2[SPAN:]).astype(BF16)

    each_block(x_ref.shape[0], body)


def proj_kernel(x_ref, att_ref, wout, vec, r1_ref, h2_ref):
    def body(i):
        at = block_rows(i)
        r1 = x_ref[at, :].astype(F32) + (dot(att_ref[at, :], wout[...]) + vec[OB : OB + 1, :D])
        r1_ref[at, :] = r1
        n2, _ = normalize(r1)
        h2_ref[at, :] = (n2 * vec[G2 : G2 + 1, :D] + vec[S2 : S2 + 1, :D]).astype(BF16)

    each_block(x_ref.shape[0], body)


def proj(x, att, wout, vec):
    outs = [(x.shape, F32), (x.shape, BF16)]
    return resident(proj_kernel, "proj", 3, 8, (), (x, att, wout, vec), outs)


def attend(sc, x, order, nsum, weights, seqs):
    rows = x.shape[0]
    nspan = nsum.shape[0]
    outs = [
        ((rows, 3 * D), BF16),
        ((rows // SPAN * PAIRS, 2 * SPAN, SPAN + nspan), BF16),
        ((rows, D), BF16),
        ((rows, D), BF16),
        ((D, 3 * D), BF16),
        ((D, D), BF16),
        ((8, 4 * D), F32),
        ((nspan, 2 * D), BF16),
    ]
    kernel = functools.partial(attend_kernel, nf=len(weights), seqs=seqs)
    arrays = (x, order, nsum, *weights)
    return resident(kernel, "attend", 12, 12, (sc,), arrays, outs)


def relative(step, nf):
    half = nf // 2
    return jnp.where(step < half, 2 * step + 1, 2 * (step - half))


def up_kernel(sc, h2_ref, vec_ref, *refs, nf):
    up_refs = refs[:nf]
    g_ref, gp_ref, w_ref = refs[nf:]
    block = D // nf
    width = w_ref.shape[1] // nf
    k0 = 0.7978845608028654
    for q in range(nf):
        at = pl.ds(pl.multiple_of((sc[SC_F] ^ q) * block, block), block)
        w_ref[at, :] = up_refs[q][...]
    for j in range(nf):
        cols = slice(j * width, (j + 1) * width)

        def body(i):
            at = block_rows(i)
            u = dot(h2_ref[at, :], w_ref[:, cols]) + vec_ref[UB : UB + 1, cols]
            u2 = u * u
            t = jnp.tanh(u * (k0 + (k0 * 0.044715) * u2))
            half = 0.5 + 0.5 * t
            g_ref[at, cols] = (u * half).astype(BF16)
            slope = u * (k0 + (3 * k0 * 0.044715) * u2)
            gp_ref[at, cols] = (half + (0.5 - 0.5 * t * t) * slope).astype(BF16)

        each_block(h2_ref.shape[0], body)


def ffn_up(sc, h2, vec, up):
    rows, ff = h2.shape[0], up[0].shape[1]
    outs = [((rows, ff), BF16), ((rows, ff), BF16), ((D, ff), BF16)]
    kernel = functools.partial(up_kernel, nf=len(up))
    return resident(kernel, "ffn_up", 8, 12, (sc,), (h2, vec, *up), outs)


def down_grad_kernel(sc, g_ref, c_ref, send_ref, keep_ref, *, nf):
    width = g_ref.shape[1] // nf
    for q in range(nf):
        at = pl.ds(pl.multiple_of((sc[SC_F] ^ q) * width, width), width)
        grad = dot_at(g_ref[:, at], c_ref[...]).astype(BF16)
        ref = send_ref if q % 2 else keep_ref
        for j in range(D // LANE):
            ref[q // 2, j * width : (j + 1) * width, :] = grad[:, j * LANE : (j + 1) * LANE]


def down_gradient(sc, g, c, nf):
    piece = g.shape[1] // nf * D // LANE
    outs = [((nf // 2, piece, LANE), BF16)] * 2
    kernel = functools.partial(down_grad_kernel, nf=nf)
    return resident(kernel, "down_grad", 4, 12, (sc,), (g, c), outs)


def down_kernel(sc, h2_ref, c_ref, gp_ref, w_ref, *refs, nf):
    down_refs = refs[:nf]
    dh2_ref, dub_ref, send_ref, keep_ref, du_ref, grad_ref = refs[nf:]
    width = w_ref.shape[1] // nf
    block = D // nf
    rows = h2_ref.shape[0]
    for s in range(nf):
        f = sc[SC_F] ^ s
        cols = pl.ds(pl.multiple_of(f * width, width), width)
        dub_ref[:, cols] = jnp.zeros((1, width), F32)

        def body(i):
            at = block_rows(i)
            dg = dot_bt(c_ref[at, :], down_refs[s][...])
            du = (dg * gp_ref[at, cols].astype(F32)).astype(BF16)
            du_ref[at, :] = du
            dub_ref[:, cols] += jnp.sum(du.astype(F32), axis=0, keepdims=True)
            dh2 = dot_bt(du, w_ref[:, cols])
            if s == 0:
                dh2_ref[at, :] = dh2
            else:
                dh2_ref[at, :] += dh2

        each_block(rows, body)
        grad_ref[...] = dot_at(h2_ref[...], du_ref[...])
        for q in range(nf):
            ref = send_ref if q % 2 else keep_ref
            piece = grad_ref[pl.ds(pl.multiple_of((sc[SC_F] ^ q) * block, block), block), :]
            piece = piece.astype(BF16)
            for j in range(width // LANE):
                to = pl.multiple_of((f * (width // LANE) + j) * block, block)
                ref[q // 2, pl.ds(to, block), :] = piece[:, j * LANE : (j + 1) * LANE]


def ffn_down(sc, h2, c, gp, w, down):
    nf = len(down)
    rows = h2.shape[0]
    ff = w.shape[1]
    piece = ff // LANE * (D // nf)
    outs = [((rows, D), F32), ((1, ff), F32)] + [((nf // 2, piece, LANE), BF16)] * 2
    scratch = [pltpu.VMEM((rows, ff // nf), BF16), pltpu.VMEM((D, ff // nf), F32)]
    kernel = functools.partial(down_kernel, nf=nf)
    arrays = (h2, c, gp, w, *down)
    return resident(kernel, "ffn_down", 8, 14, (sc,), arrays, outs, scratch)


def mid_kernel(c_ref, dh2_ref, r1_ref, att_ref, wout, vec, dr1_ref, da_ref, gout_ref, gvec_ref):
    gout_ref[...] = jnp.zeros_like(gout_ref)
    gvec_ref[...] = jnp.zeros_like(gvec_ref)

    def add(row, values):
        gvec_ref[row : row + 1, :] += jnp.sum(values, axis=0, keepdims=True)

    def body(i):
        at = block_rows(i)
        c = c_ref[at, :].astype(F32)
        dh2 = dh2_ref[at, :]
        n2, rstd2 = normalize(r1_ref[at, :])
        add(G2, dh2 * n2)
        add(S2, dh2)
        add(DB, c)
        dr1 = c + norm_back(dh2 * vec[G2 : G2 + 1, :D], n2, rstd2)
        dr1_ref[at, :] = dr1
        dy = dr1.astype(BF16)
        add(OB, dy.astype(F32))
        gout_ref[...] += dot_at(att_ref[at, :], dy)
        da_ref[at, :] = dot_bt(dy, wout[...]).astype(BF16)

    each_block(c_ref.shape[0], body)


def mid(c, dh2, r1, att, wout, vec):
    rows = c.shape[0]
    outs = [((rows, D), F32), ((rows, D), BF16), ((D, D), F32), ((8, D), F32)]
    return resident(mid_kernel, "mid", 5, 12, (), (c, dh2, r1, att, wout, vec), outs)


def piece_rows(used, parts):
    return -(-used // (16 * parts)) * 16 * parts


def columns_of(half):
    wide = PAIRS // 2 * LANE
    return [slice(t * D + half * wide, t * D + (half + 1) * wide) for t in range(3)]


def back_kernel(sc, x_ref, da_ref, h1_ref, packed_ref, p_ref, tabs, wqkv, vec, nsum_ref, *refs, nf, copies, half):
    if half:
        (dub_ref, gvec_ref, before_ref, sums_ref), refs = refs[:4], refs[4:]
    else:
        (gout_ref,), refs = refs[:1], refs[1:]
    dh1_ref, sum_ref, far_send, far_keep, send_ref, keep_ref, acc, acc_span, accv, dp_ref = refs
    wide = PAIRS // 2 * LANE
    columns = columns_of(half)
    for ref in (acc, acc_span, accv):
        ref[...] = jnp.zeros_like(ref)

    def add(row, values):
        accv[row : row + 1, : values.shape[1]] += jnp.sum(values, axis=0, keepdims=True)

    def body(i):
        rows = block_rows(i)
        low = lax.broadcasted_iota(jnp.int32, (SPAN, LANE), 1) < HEAD
        for s in range(ROWS // SPAN):
            at = block_rows(i * (ROWS // SPAN) + s, SPAN)
            to = slice(s * SPAN, (s + 1) * SPAN)
            for k in range(PAIRS // 2):
                p = half * (PAIRS // 2) + k
                cq, ck, cv = (slice(t * D + p * LANE, t * D + (p + 1) * LANE) for t in range(3))
                oq, ok, ov = (slice(t * wide + k * LANE, t * wide + (k + 1) * LANE) for t in range(3))
                q = packed_ref[at, cq] * SCALE
                do = da_ref[at, cq]
                zero = jnp.zeros_like(q)
                q2 = jnp.concatenate([jnp.where(low, q, zero), jnp.where(low, zero, q)], axis=0)
                do2 = jnp.concatenate([jnp.where(low, do, zero), jnp.where(low, zero, do)], axis=0)
                kc = jnp.concatenate([packed_ref[at, ck], tabs[:, cq]], axis=0)
                vc = jnp.concatenate([packed_ref[at, cv], tabs[:, ck]], axis=0)
                w = p_ref[(i * (ROWS // SPAN) + s) * PAIRS + p]
                wf = w.astype(F32)
                dp = dot_bt(do2, vc)
                delta = jnp.sum(wf * dp, axis=1, keepdims=True)
                ds = (wf * (dp - delta)).astype(BF16)
                dq2 = dot(ds, kc)
                dq = jnp.where(low, dq2[:SPAN], dq2[SPAN:]) * SCALE
                dk = dot_at(ds, q2)
                dv = dot_at(w, do2)
                acc_span[:, oq] += dk[SPAN:]
                acc_span[:, ok] += dv[SPAN:]
                dp_ref[to, oq] = dq.astype(BF16)
                dp_ref[to, ok] = dk[:SPAN].astype(BF16)
                dp_ref[to, ov] = dv[:SPAN].astype(BF16)
        dpk = dp_ref[...]
        add(QB, dpk.astype(F32))
        acc[...] += dot_at(h1_ref[rows, :], dpk)
        dh1 = dot_bt(dpk[:, :wide], wqkv[:, columns[0]])
        for t in (1, 2):
            dh1 = dh1 + dot_bt(dpk[:, t * wide : (t + 1) * wide], wqkv[:, columns[t]])
        if half:
            dh1 = dh1 + before_ref[rows, :]
            n1, _ = normalize(x_ref[rows, :].astype(F32))
            add(G1, dh1 * n1)
            add(S1, dh1)
        dh1_ref[rows, :] = dh1

    each_block(x_ref.shape[0], body)

    span = acc_span[...]
    bit = sc[SC_C] & 1
    each = span.shape[0] // copies
    for k in range(copies):
        code = code_of(k, copies)
        part = span[k * each : (k + 1) * each]
        hold = jnp.concatenate(
            [part[:, t * LANE : (t + 1) * LANE] for t in range(2 * wide // LANE)], axis=0
        ).astype(BF16)
        to = slice(code % (copies // 2) * hold.shape[0], (code % (copies // 2) + 1) * hold.shape[0])
        mine = bit == code // (copies // 2)

        @pl.when(mine)
        def _():
            far_keep[to, :] = hold

        @pl.when(jnp.logical_not(mine))
        def _():
            far_send[to, :] = hold

    span = span * INV_ROOT
    low_span = span.astype(BF16)
    nsum = nsum_ref[...]
    hs = (nsum * vec[G1 : G1 + 1, :D] + SPAN * vec[S1 : S1 + 1, :D]).astype(BF16)
    acc[:, wide:] += dot_at(hs, low_span)
    accv[QB : QB + 1, wide : 3 * wide] += SPAN * jnp.sum(span, axis=0, keepdims=True)
    de = dot_bt(low_span[:, :wide], wqkv[:, columns[1]])
    de = de + dot_bt(low_span[:, wide:], wqkv[:, columns[2]])
    block = D // nf
    if half:
        de = de + sums_ref[: de.shape[0], :]
        add(G1, de * nsum)
        accv[S1 : S1 + 1, :D] += SPAN * jnp.sum(de, axis=0, keepdims=True)
        bias = sums_ref[de.shape[0] : de.shape[0] + 8, :]
    else:
        sum_ref[: de.shape[0], :] = de
        tail = [accv[QB : QB + 1, t * wide : (t + 1) * wide] for t in range(3)]
        bias = jnp.concatenate(tail + [jnp.zeros((5, wide), F32)], axis=0)
        sum_ref[de.shape[0] : de.shape[0] + 8, :] = jnp.concatenate([bias, bias], axis=1)

    for q in range(nf):
        ref = send_ref if q % 2 else keep_ref
        fq = sc[SC_F] ^ q
        at = pl.ds(pl.multiple_of(fq * block, block), block)
        base = 0
        pieces = [acc[at, :].astype(BF16)]
        if not half:
            pieces.append(gout_ref[at, :].astype(BF16))
        for piece in pieces:
            for j in range(piece.shape[1] // LANE):
                ref[q // 2, base : base + block, :] = piece[:, j * LANE : (j + 1) * LANE]
                base += block
        if half:
            whole = jnp.concatenate(
                [
                    part
                    for t in range(3)
                    for part in (bias[t : t + 1, :wide], accv[QB : QB + 1, t * wide : (t + 1) * wide])
                ],
                axis=1,
            )
            accv[QB + 1 : QB + 2, : 3 * D] = whole
            three = [
                accv[QB + 1 : QB + 2, pl.ds(pl.multiple_of((fq * 3 + t) * block, block), block)]
                for t in range(3)
            ]
            four = [
                dub_ref[0:1, pl.ds(pl.multiple_of((fq * 4 + t) * block, block), block)]
                for t in range(4)
            ]
            small = jnp.concatenate(
                [accv[G1 : G1 + 1, at], accv[S1 : S1 + 1, at]]
                + three
                + [gvec_ref[OB : OB + 1, at], gvec_ref[G2 : G2 + 1, at], gvec_ref[S2 : S2 + 1, at]]
                + four
                + [gvec_ref[DB : DB + 1, at], jnp.zeros((3, LANE), F32)],
                axis=0,
            ).astype(BF16)
            ref[q // 2, base : base + 16, :] = small
            base += 16
        left = ref.shape[1] - base
        if left:
            ref[q // 2, base:, :] = jnp.zeros((left, LANE), BF16)


def back(sc, x, da, h1, packed, p, tabs, wqkv, vec, nsum, more, half, nf, copies):
    rows = x.shape[0]
    nspan = nsum.shape[0]
    wide = PAIRS // 2 * LANE
    block = D // nf
    used = 3 * wide // LANE * block + (16 if half else D // LANE * block)
    piece = piece_rows(used, copies)
    far = nspan // 2 * 2 * wide // LANE
    outs = [((rows, D), F32), ((nspan + 8, D), F32)]
    outs += [((far, LANE), BF16)] * 2 + [((nf // 2, piece, LANE), BF16)] * 2
    scratch = [
        pltpu.VMEM((D, 3 * wide), F32),
        pltpu.VMEM((nspan, 2 * wide), F32),
        pltpu.VMEM((16, 3 * D), F32),
        pltpu.VMEM((ROWS, 3 * wide), BF16),
    ]
    kernel = functools.partial(back_kernel, nf=nf, copies=copies, half=half)
    arrays = (x, da, h1, packed, p, tabs, wqkv, vec, nsum, *more)
    return resident(kernel, f"back_{half}", 9, 18, (sc,), arrays, outs, scratch)


def first_kernel(x_ref, dr1_ref, dh1_ref, own_ref, wqkv, vec, o_ref, e_ref):
    i = pl.program_id(0)
    spans = ROWS // SPAN

    @pl.when(i == 0)
    def _():
        each = e_ref.shape[0]
        wide = PAIRS // 2 * LANE
        total = jnp.zeros((each, D), F32)
        for half in range(2):
            for k, columns in enumerate(columns_of(half)[1:]):
                for t in range(wide // LANE):
                    row = ((half * 2 + k) * (wide // LANE) + t) * each
                    own = own_ref[row : row + each, :].astype(F32) * INV_ROOT
                    cols = slice(columns.start + t * LANE, columns.start + (t + 1) * LANE)
                    total = total + dot_bt(own.astype(BF16), wqkv[:, cols])
        e_ref[...] = total

    at = block_rows(i)
    n1, rstd1 = normalize(x_ref[at, :].astype(F32))
    extra = jnp.concatenate(
        [jnp.broadcast_to(e_ref[pl.ds(i * spans + s, 1), :], (SPAN, D)) for s in range(spans)],
        axis=0,
    )
    dh1 = dh1_ref[at, :] + extra
    o_ref[...] = dr1_ref[at, :] + norm_back(dh1 * vec[G1 : G1 + 1, :D], n1, rstd1)


def first_back(x, dr1, dh1, own, wqkv, vec):
    rows = x.shape[0]
    return pl.pallas_call(
        first_kernel,
        grid=(rows // ROWS,),
        in_specs=in_vmem(6),
        out_specs=pl.BlockSpec((ROWS, D), lambda i: (i, 0)),
        out_shape=jax.ShapeDtypeStruct((rows, D), F32),
        scratch_shapes=[pltpu.VMEM((rows // SPAN, D), F32)],
        compiler_params=params(8),
        name="first_back",
        cost_estimate=cost(3),
    )(x, dr1, dh1, own, wqkv, vec)


def mixed_kernel(sc, r1_ref, g_ref, vec, *refs):
    w_refs, o_ref = refs[:-1], refs[-1]
    at = block_rows(pl.program_id(0))
    total = r1_ref[at, :] + vec[DB : DB + 1, :D]
    width = w_refs[0].shape[0]
    for q, w_ref in enumerate(w_refs):
        cols = pl.ds(pl.multiple_of((sc[SC_F] ^ q) * width, width), width)
        total = total + dot(g_ref[at, cols], w_ref[...])
    o_ref[...] = total.astype(BF16)


def block_output(sc, r1, g, vec, down):
    rows = r1.shape[0]
    return pl.pallas_call(
        mixed_kernel,
        grid=(rows // ROWS,),
        in_specs=[pl.BlockSpec(memory_space=pltpu.SMEM)] + in_vmem(3 + len(down)),
        out_specs=pl.BlockSpec((ROWS, D), lambda i: (i, 0)),
        out_shape=jax.ShapeDtypeStruct((rows, D), BF16),
        compiler_params=params(8),
        name="block_output",
        cost_estimate=cost(4),
    )(sc, r1, g, vec, *down)


def swap(array, axis, bit):
    n = lax.axis_size(axis)
    return lax.ppermute(array, axis, [(k, k ^ bit) for k in range(n)])


def after(array, *others):
    return lax.optimization_barrier((array, others))[0]


def first_gather(array, axis):
    return swap(array, axis, lax.axis_size(axis) // 2)


def gathered(array, far, axis):
    n = lax.axis_size(axis)
    bit = n // 2
    held = {0: array, bit: far}
    bit //= 2
    while bit:
        for r in sorted(held):
            held[r ^ bit] = swap(held[r], axis, bit)
        bit //= 2
    return [held[r] for r in range(n)]


def fold_kernel(sc, *refs, bit):
    own = lax.div(sc[SC_C], bit) & 1 if bit else 0
    arrays, (send_ref, own_ref) = refs[:-2], refs[-2:]
    at = 0
    for keep_ref, got_ref in zip(arrays[0::2], arrays[1::2]):
        a, _, h, _ = keep_ref.shape
        for ref, half in ((send_ref, 1 - own), (own_ref, own)):
            for k in range(a):
                total = keep_ref[k, half].astype(F32) + got_ref[k, half].astype(F32)
                ref[k, at : at + h, :] = total.astype(BF16)
        at += h


def fold(sc, bit, *pairs):
    a = pairs[0][0].shape[0]
    h = sum(keep.shape[2] for keep, _ in pairs)
    arrays = [array for pair in pairs for array in pair]
    kernel = functools.partial(fold_kernel, bit=bit)
    return resident(kernel, "fold", 1, 8, (sc,), arrays, [((a, h, LANE), BF16)] * 2)


def refold_kernel(sc, keep_ref, got_ref, send_ref, own_ref, *, bit, sizes):
    own = lax.div(sc[SC_C], bit) & 1
    at = 0
    for h in sizes:
        for ref, half in ((send_ref, 1 - own), (own_ref, own)):
            rows = pl.ds(pl.multiple_of(2 * at + half * h, 16), h)
            total = keep_ref[rows, :].astype(F32) + got_ref[rows, :].astype(F32)
            ref[at : at + h, :] = total.astype(BF16)
        at += h


def refold(sc, bit, keep, got, sizes):
    outs = [((sum(sizes), LANE), BF16)] * 2
    kernel = functools.partial(refold_kernel, bit=bit, sizes=sizes)
    return resident(kernel, "fold", 1, 8, (sc,), (keep, got), outs)


def last_kernel(keep_ref, got_ref, o_ref, *rest):
    used = o_ref.shape[0]
    total = keep_ref[:used, :].astype(F32) + got_ref[:used, :].astype(F32)
    o_ref[...] = total.astype(BF16)
    for ref in rest:
        total = keep_ref[used:, :].astype(F32) + got_ref[used:, :].astype(F32)
        ref[...] = total.astype(BF16)


def last_sum(keep, got, used):
    outs = [((used, LANE), BF16)]
    if used < keep.shape[0]:
        outs.append(((keep.shape[0] - used, LANE), BF16))
    return resident(last_kernel, "last", 1, 8, (), (keep, got), outs)


class Part:
    def __init__(self, sc, keep, send):
        self.sc, self.keep, self.send = sc, keep, send
        self.count, self.rows = keep.shape[0], keep.shape[1]
        self.total = self.rows
        self.move("fsdp", 1)

    def move(self, axis, bit):
        self.got = swap(self.send, axis, bit)

    def view(self, axis):
        if axis == "fsdp":
            self.count //= 2
            return 1, 2, self.count * self.rows, LANE
        self.rows //= 2
        return self.count, 2, self.rows, LANE

    def pair(self, axis):
        view = self.view(axis)
        return self.keep.reshape(view), self.got.reshape(view)

    def step(self, axis, bit):
        pair = self.pair(axis)
        self.send, self.keep = fold(self.sc, bit if axis == "ctx" else 0, pair)
        self.move(axis, bit)

    def wait(self, *arrays):
        self.keep = after(self.keep, *arrays)


def ctx_bits():
    n = lax.axis_size("ctx")
    return [1 << k for k in range(n.bit_length() - 1)]


def ctx_sum(sc, parts, extra=()):
    bits = ctx_bits()
    pairs = [part.pair("ctx") for part in parts]
    for keep, got in extra:
        view = (1, 2, keep.shape[0] // 2, LANE)
        pairs.append((keep.reshape(view), got.reshape(view)))
    sizes = [keep.shape[2] for keep, _ in pairs]
    used = sum(sizes[: len(parts)]) * 2 // bits[-1]
    send, keep = (a[0] for a in fold(sc, bits[1], *pairs))
    got = swap(send, "ctx", bits[1])
    for bit in bits[2:]:
        sizes = [size // 2 for size in sizes]
        send, keep = refold(sc, bit, keep, got, sizes)
        got = swap(send, "ctx", bit)
    return last_sum(keep, got, used)


def over_ctx(own):
    for bit in reversed(ctx_bits()):
        own = jnp.concatenate([own, swap(own, "ctx", bit)], axis=0)
    return own.reshape(lax.axis_size("ctx"), -1, LANE)


def code_of(index, n):
    code = 0
    for k in range(n.bit_length() - 1):
        bit = index >> k if isinstance(index, int) else lax.div(index, 1 << k)
        code = 2 * code + (bit & 1)
    return code


def finish_kernel(sc, got_ref, *refs, heights, plan):
    outs, rows = refs[:-1], refs[-1]
    n = got_ref.shape[0]
    code = code_of(sc[SC_C], n)
    for k in range(n):
        at, base = 0, 0
        for height in heights:
            h = height // n
            to = pl.multiple_of(base + (code ^ k) * h, 16)
            rows[pl.ds(to, h), :] = got_ref[k, at : at + h, :].astype(F32)
            at, base = at + h, base + height
    for ref, places in zip(outs, plan):
        height = ref.shape[0]
        for j, place in enumerate(places):
            ref[:, j * LANE : (j + 1) * LANE] = rows[place : place + height, :]


def finish(sc, got, heights, shapes, plan):
    return pl.pallas_call(
        functools.partial(finish_kernel, heights=heights, plan=plan),
        in_specs=[pl.BlockSpec(memory_space=pltpu.SMEM)] + in_vmem(1),
        out_shape=[jax.ShapeDtypeStruct(shape, F32) for shape in shapes],
        scratch_shapes=[pltpu.VMEM((sum(heights), LANE), F32)],
        compiler_params=params(16),
        name="finish",
        cost_estimate=cost(2),
    )(sc, got)


def local(
    tokens, ln1_gain, ln1_shift, qkv_weight, qkv_bias, out_weight, out_bias, ln2_gain, ln2_shift,
    up_weight, up_bias, down_weight, down_bias, seq_lengths, span_order, cotangent,
):
    nf = lax.axis_size("fsdp")
    nc = lax.axis_size("ctx")
    x, c = tokens[0], cotangent[0]
    spans = x.shape[0] // SPAN
    seqs = seq_lengths.shape[1]
    weights = packed_params(
        qkv_weight, out_weight,
        (ln1_gain, ln1_shift, qkv_bias, out_bias, ln2_gain, ln2_shift, up_bias, down_bias),
    )
    scalars = jnp.concatenate(
        [
            lax.axis_index("fsdp").reshape(1),
            lax.axis_index("ctx").reshape(1),
            (lax.axis_index("ctx") * spans).reshape(1),
            seq_lengths[0],
            span_order[0],
        ]
    ).astype(jnp.int32)
    far_weights = first_gather(weights, "fsdp")
    sums = span_sums(x, nc)
    nsum = lax.all_to_all(sums, "ctx", 0, 0, tiled=True).reshape(nc * spans, D)
    far_weights = after(far_weights, nsum)
    weights = gathered(weights, far_weights, "fsdp")
    up_weight = after(up_weight, far_weights)
    far_up = first_gather(up_weight, "fsdp")
    down_weight = after(down_weight, far_weights)
    far_down = first_gather(down_weight, "fsdp")

    packed, p, att, h1, wqkv, wout, vec, tabs = attend(
        scalars, x, span_order, nsum, weights, seqs
    )
    up = gathered(up_weight, after(far_up, att), "fsdp")
    r1, h2 = proj(x, att, wout, vec)
    g, gp, wup = ffn_up(scalars, h2, vec, up)
    down = gathered(down_weight, after(far_down, g), "fsdp")
    dsend, dkeep = down_gradient(scalars, g, c, nf)
    gp = after(gp, dkeep)
    dh2, dub, usend, ukeep = ffn_down(scalars, h2, c, gp, wup, down)
    bits = ctx_bits()
    near = [("fsdp", 1 << k) for k in range(1, nf.bit_length() - 1)]

    from_down = Part(scalars, dkeep, dsend)
    from_down.step(*near[0])
    dh2 = after(dh2, from_down.keep)
    dr1, da, gout, gvec = mid(c, dh2, r1, att, wout, vec)
    from_up = Part(scalars, ukeep, usend)
    from_up.step("ctx", bits[0])
    da = after(da, from_up.keep)
    fixed = (x, da, h1, packed, p, tabs, wqkv, vec, nsum)
    dh1, sums, fsend0, fkeep0, send, keep = back(scalars, *fixed, (gout,), 0, nf, nc)
    first = Part(scalars, keep, send)
    from_down.step("ctx", bits[0])
    from_up.step(*near[0])
    dh1 = after(dh1, from_down.keep, from_up.keep)
    dh1, _, fsend1, fkeep1, send, keep = back(
        scalars, *fixed, (dub, gvec, dh1, sums), 1, nf, nc
    )
    second = Part(scalars, keep, send)
    first.step(*near[0])
    second.step("ctx", bits[0])
    first.step("ctx", bits[0])
    second.step(*near[0])
    far = [(k, swap(t, "ctx", bits[0])) for k, t in ((fkeep0, fsend0), (fkeep1, fsend1))]

    block = D // nf
    height, width = down_weight.shape[0], up_weight.shape[1]
    feed = (from_down.total, from_up.total)
    (own,) = ctx_sum(scalars, [from_down, from_up])
    grad_down, grad_up = finish(
        scalars,
        over_ctx(own),
        feed,
        [(height, D), (block, width)],
        [
            [height * j for j in range(D // LANE)],
            [feed[0] + block * j for j in range(width // LANE)],
        ],
    )

    own, own_span = ctx_sum(scalars, [first, second], far)
    tokens_grad = first_back(x, dr1, dh1, own_span, wqkv, vec)
    mixed = block_output(scalars, r1, after(g, first.keep), vec, down)
    half = PAIRS // 2
    plan = [
        [
            p // half * first.total + block * (t * half + p % half)
            for t in range(3)
            for p in range(PAIRS)
        ],
        [block * (3 * half + j) for j in range(D // LANE)],
    ]
    shapes = [(block, 3 * D), (block, D)]
    at = first.total + 3 * half * block
    for wide in (block, block, 3 * block, block, block, block, 4 * block, block):
        shapes.append((1, wide))
        plan.append([at + j for j in range(wide // LANE)])
        at += wide // LANE
    grad_qkv, grad_out, *vectors = finish(
        scalars, over_ctx(own), (first.total, second.total), shapes, plan
    )
    g1, s1, qb, ob, g2, s2, ub, db = (v.reshape(-1) for v in vectors)
    return (
        mixed[None], tokens_grad[None], g1, s1, grad_qkv, qb, grad_out, ob, g2, s2,
        grad_up, ub, grad_down, db,
    )


def solution(mesh):
    rows, one, two = P("fsdp", "ctx", None), P("fsdp"), P("fsdp", None)
    return jax.shard_map(
        local,
        mesh=mesh,
        in_specs=(
            rows, one, one, two, one, two, one, one, one, two, one, two, one, two, two, rows,
        ),
        out_specs=(rows, rows, one, one, two, one, two, one, one, one, two, one, two, one),
        check_vma=False,
    )
```

```python
import functools

import jax
import jax.numpy as jnp
from jax import lax
from jax.experimental import pallas as pl
from jax.experimental.pallas import tpu as pltpu
from jax.sharding import PartitionSpec as P

D = 512
HEADS = 8
HEAD = 64
SPAN = 128
LANE = 128
PAIRS = D // LANE
ROWS = 256
EPSILON = 1e-05
MASKED = -1e30
SCALE = HEAD**-0.5
FILL = 4
INV_ROOT = SPAN**-0.5
F32 = jnp.float32
BF16 = jnp.bfloat16

G1, S1, OB, G2, S2, DB, QB, UB = range(8)
SC_F, SC_C, SC_SLOT, SC_LEN = range(4)


def dot(a, b):
    return lax.dot_general(a, b, (((1,), (0,)), ((), ())), preferred_element_type=F32)


def dot_bt(a, b):
    return lax.dot_general(a, b, (((1,), (1,)), ((), ())), preferred_element_type=F32)


def dot_at(a, b):
    return lax.dot_general(a, b, (((0,), (0,)), ((), ())), preferred_element_type=F32)


def normalize(values):
    centre = values - jnp.mean(values, axis=-1, keepdims=True)
    spread = jnp.mean(centre * centre, axis=-1, keepdims=True)
    rstd = lax.rsqrt(spread + EPSILON)
    return centre * rstd, rstd


def norm_back(e, n, rstd):
    return rstd * (
        e - jnp.mean(e, axis=-1, keepdims=True) - n * jnp.mean(e * n, axis=-1, keepdims=True)
    )


def params(mib):
    return pltpu.CompilerParams(vmem_limit_bytes=mib * 1024 * 1024)


def in_vmem(count):
    return [pl.BlockSpec(memory_space=pltpu.VMEM) for _ in range(count)]


def cost(micros):
    return pl.CostEstimate(
        flops=int(micros * 1e9), transcendentals=0, bytes_accessed=int(micros * 1e6)
    )


def resident(kernel, name, micros, mib, scalars, arrays, outs, scratch=()):
    return pl.pallas_call(
        kernel,
        in_specs=[pl.BlockSpec(memory_space=pltpu.SMEM)] * len(scalars) + in_vmem(len(arrays)),
        out_specs=in_vmem(len(outs)),
        out_shape=[jax.ShapeDtypeStruct(shape, dtype) for shape, dtype in outs],
        scratch_shapes=list(scratch),
        compiler_params=params(mib),
        name=name,
        cost_estimate=cost(micros),
    )(*scalars, *arrays)


def block_rows(i, size=ROWS):
    return pl.ds(pl.multiple_of(i * size, size), size)


def each_block(rows, body):
    def step(i, carry):
        body(i)
        return carry

    lax.fori_loop(0, rows // ROWS, step, 0)


def sums_kernel(x_ref, o_ref):
    spans = x_ref.shape[0] // SPAN
    sums = []
    for s in range(spans):
        n, _ = normalize(x_ref[s * SPAN : (s + 1) * SPAN, :].astype(F32))
        sums.append(jnp.sum(n, axis=0, keepdims=True))
    table = jnp.concatenate(sums, axis=0)
    for k in range(o_ref.shape[0]):
        o_ref[k] = table


def span_sums(x, copies):
    spans = x.shape[0] // SPAN
    return resident(sums_kernel, "span_sums", 3, 16, (), (x,), [((copies, spans, D), F32)])[0]


def pack_kernel(qkv_ref, out_ref, *refs):
    o_ref = refs[-1]
    rows, width = qkv_ref.shape
    o_ref[:rows, :width] = qkv_ref[...]
    o_ref[:rows, width:] = out_ref[...]
    parts = [ref[...].astype(F32) for ref in refs[:-1]]
    used = sum(part.shape[0] for part in parts)
    parts.append(jnp.zeros((16 - used, LANE), F32))
    o_ref[rows:, :LANE] = jnp.concatenate(parts, axis=0).astype(BF16)
    o_ref[rows:, LANE:] = jnp.zeros((16, o_ref.shape[1] - LANE), BF16)


def packed_params(qkv, out, vectors):
    shape = (qkv.shape[0] + 16, qkv.shape[1] + out.shape[1])
    vectors = [v.reshape(-1, LANE) for v in vectors]
    arrays = [qkv, out] + vectors
    return pl.pallas_call(
        pack_kernel,
        out_shape=jax.ShapeDtypeStruct(shape, BF16),
        compiler_params=params(58),
        name="pack",
        cost_estimate=cost(1),
    )(*arrays)


def attend_kernel(sc, x_ref, order_ref, nsum_ref, *refs, nf, seqs):
    param_refs = refs[:nf]
    (packed_ref, p_ref, att_ref, h1_ref, wqkv, wout, vec, tabs) = refs[nf:]
    nspan = nsum_ref.shape[0]
    block = D // nf

    vec[...] = jnp.zeros_like(vec)
    for q in range(nf):
        fq = sc[SC_F] ^ q
        at = pl.ds(pl.multiple_of(fq * block, block), block)
        wqkv[at, :] = param_refs[q][:block, : 3 * D]
        wout[at, :] = param_refs[q][:block, 3 * D :]
        sm = param_refs[q][block:, :LANE].astype(F32)
        for row, src in ((G1, 0), (S1, 1), (OB, 5), (G2, 6), (S2, 7), (DB, 12)):
            vec[row : row + 1, at] = sm[src : src + 1]
        for t in range(3):
            at3 = pl.ds(pl.multiple_of(fq * 3 * block + t * block, block), block)
            vec[QB : QB + 1, at3] = sm[2 + t : 3 + t]
        for t in range(4):
            at4 = pl.ds(pl.multiple_of(fq * 4 * block + t * block, block), block)
            vec[UB : UB + 1, at4] = sm[8 + t : 9 + t]
    hs = nsum_ref[...] * vec[G1 : G1 + 1, :D] + SPAN * vec[S1 : S1 + 1, :D]
    hi = hs.astype(BF16)
    lo = (hs - hi.astype(F32)).astype(BF16)
    t = dot(hi, wqkv[:, D:]) + dot(lo, wqkv[:, D:]) + SPAN * vec[QB : QB + 1, D : 3 * D]
    tabs[...] = (t * INV_ROOT).astype(BF16)
    prompt = lax.div(sc[SC_LEN], SPAN)
    spans = ROWS // SPAN

    def body(i):
        rows = block_rows(i)
        n1, _ = normalize(x_ref[rows, :].astype(F32))
        h1 = (n1 * vec[G1 : G1 + 1, :D] + vec[S1 : S1 + 1, :D]).astype(BF16)
        h1_ref[rows, :] = h1
        packed_ref[rows, :] = (dot(h1, wqkv[...]) + vec[QB : QB + 1, : 3 * D]).astype(BF16)

        lane = lax.broadcasted_iota(jnp.int32, (SPAN, LANE), 1)
        low = lane < HEAD
        causal = jnp.where(
            lane <= lax.broadcasted_iota(jnp.int32, (SPAN, LANE), 0), 0.0, MASKED
        ).astype(F32)
        order = order_ref[...]
        for s in range(spans):
            a = sc[SC_LEN + seqs + sc[SC_SLOT] + i * spans + s]
            start, begin = 0, 0
            for k in range(seqs):
                begin = jnp.where(start <= a, start, begin)
                start = start + lax.div(sc[SC_LEN + k], SPAN)
            seen = (order < a) & ((order >= begin) | (order < prompt))
            far = jnp.where(seen, 0.0, MASKED).astype(F32)
            bias = jnp.concatenate([causal, jnp.broadcast_to(far, (SPAN, nspan))], axis=1)
            bias = jnp.concatenate([bias, bias], axis=0)
            at = block_rows(i * spans + s, SPAN)
            for p in range(PAIRS):
                cq, ck, cv = (slice(t * D + p * LANE, t * D + (p + 1) * LANE) for t in range(3))
                q = packed_ref[at, cq] * SCALE
                zero = jnp.zeros_like(q)
                q2 = jnp.concatenate([jnp.where(low, q, zero), jnp.where(low, zero, q)], axis=0)
                kc = jnp.concatenate([packed_ref[at, ck], tabs[:, cq]], axis=0)
                vc = jnp.concatenate([packed_ref[at, cv], tabs[:, ck]], axis=0)
                scores = dot_bt(q2, kc) + bias
                peak = jnp.max(scores, axis=1, keepdims=True)
                e = jnp.exp(scores - peak)
                w = (e * (1.0 / jnp.sum(e, axis=1, keepdims=True))).astype(BF16)
                p_ref[(i * spans + s) * PAIRS + p] = w
                o2 = dot(w, vc)
                att_ref[at, cq] = jnp.where(low, o2[:SPAN], o2[SPAN:]).astype(BF16)

    each_block(x_ref.shape[0], body)


def proj_kernel(x_ref, att_ref, wout, vec, r1_ref, h2_ref):
    def body(i):
        at = block_rows(i)
        r1 = x_ref[at, :].astype(F32) + (dot(att_ref[at, :], wout[...]) + vec[OB : OB + 1, :D])
        r1_ref[at, :] = r1
        n2, _ = normalize(r1)
        h2_ref[at, :] = (n2 * vec[G2 : G2 + 1, :D] + vec[S2 : S2 + 1, :D]).astype(BF16)

    each_block(x_ref.shape[0], body)


def proj(x, att, wout, vec):
    outs = [(x.shape, F32), (x.shape, BF16)]
    return resident(proj_kernel, "proj", 3, 8, (), (x, att, wout, vec), outs)


def attend(sc, x, order, nsum, weights, seqs):
    rows = x.shape[0]
    nspan = nsum.shape[0]
    outs = [
        ((rows, 3 * D), BF16),
        ((rows // SPAN * PAIRS, 2 * SPAN, SPAN + nspan), BF16),
        ((rows, D), BF16),
        ((rows, D), BF16),
        ((D, 3 * D), BF16),
        ((D, D), BF16),
        ((8, 4 * D), F32),
        ((nspan, 2 * D), BF16),
    ]
    kernel = functools.partial(attend_kernel, nf=len(weights), seqs=seqs)
    arrays = (x, order, nsum, *weights)
    return resident(kernel, "attend", 12, 12, (sc,), arrays, outs)


def relative(step, nf):
    half = nf // 2
    return jnp.where(step < half, 2 * step + 1, 2 * (step - half))


def up_kernel(sc, h2_ref, vec_ref, *refs, nf):
    up_refs = refs[:nf]
    g_ref, gp_ref, w_ref = refs[nf:]
    block = D // nf
    width = w_ref.shape[1] // nf
    k0 = 0.7978845608028654
    for q in range(nf):
        at = pl.ds(pl.multiple_of((sc[SC_F] ^ q) * block, block), block)
        w_ref[at, :] = up_refs[q][...]
    for j in range(nf):
        cols = slice(j * width, (j + 1) * width)

        def body(i):
            at = block_rows(i)
            u = dot(h2_ref[at, :], w_ref[:, cols]) + vec_ref[UB : UB + 1, cols]
            u2 = u * u
            t = jnp.tanh(u * (k0 + (k0 * 0.044715) * u2))
            half = 0.5 + 0.5 * t
            g_ref[at, cols] = (u * half).astype(BF16)
            slope = u * (k0 + (3 * k0 * 0.044715) * u2)
            gp_ref[at, cols] = (half + (0.5 - 0.5 * t * t) * slope).astype(BF16)

        each_block(h2_ref.shape[0], body)


def ffn_up(sc, h2, vec, up):
    rows, ff = h2.shape[0], up[0].shape[1]
    outs = [((rows, ff), BF16), ((rows, ff), BF16), ((D, ff), BF16)]
    kernel = functools.partial(up_kernel, nf=len(up))
    return resident(kernel, "ffn_up", 8, 12, (sc,), (h2, vec, *up), outs)


def down_grad_kernel(sc, g_ref, c_ref, send_ref, keep_ref, *, nf):
    width = g_ref.shape[1] // nf
    for q in range(nf):
        at = pl.ds(pl.multiple_of((sc[SC_F] ^ q) * width, width), width)
        grad = dot_at(g_ref[:, at], c_ref[...]).astype(BF16)
        ref = send_ref if q % 2 else keep_ref
        for j in range(D // LANE):
            ref[q // 2, j * width : (j + 1) * width, :] = grad[:, j * LANE : (j + 1) * LANE]


def down_gradient(sc, g, c, nf):
    piece = g.shape[1] // nf * D // LANE
    outs = [((nf // 2, piece, LANE), BF16)] * 2
    kernel = functools.partial(down_grad_kernel, nf=nf)
    return resident(kernel, "down_grad", 4, 12, (sc,), (g, c), outs)


def down_kernel(sc, h2_ref, c_ref, gp_ref, w_ref, *refs, nf):
    down_refs = refs[:nf]
    dh2_ref, dub_ref, send_ref, keep_ref, du_ref, grad_ref = refs[nf:]
    width = w_ref.shape[1] // nf
    block = D // nf
    rows = h2_ref.shape[0]
    for s in range(nf):
        f = sc[SC_F] ^ s
        cols = pl.ds(pl.multiple_of(f * width, width), width)
        dub_ref[:, cols] = jnp.zeros((1, width), F32)

        def body(i):
            at = block_rows(i)
            dg = dot_bt(c_ref[at, :], down_refs[s][...])
            du = (dg * gp_ref[at, cols].astype(F32)).astype(BF16)
            du_ref[at, :] = du
            dub_ref[:, cols] += jnp.sum(du.astype(F32), axis=0, keepdims=True)
            dh2 = dot_bt(du, w_ref[:, cols])
            if s == 0:
                dh2_ref[at, :] = dh2
            else:
                dh2_ref[at, :] += dh2

        each_block(rows, body)
        grad_ref[...] = dot_at(h2_ref[...], du_ref[...])
        for q in range(nf):
            ref = send_ref if q % 2 else keep_ref
            piece = grad_ref[pl.ds(pl.multiple_of((sc[SC_F] ^ q) * block, block), block), :]
            piece = piece.astype(BF16)
            for j in range(width // LANE):
                to = pl.multiple_of((f * (width // LANE) + j) * block, block)
                ref[q // 2, pl.ds(to, block), :] = piece[:, j * LANE : (j + 1) * LANE]


def ffn_down(sc, h2, c, gp, w, down):
    nf = len(down)
    rows = h2.shape[0]
    ff = w.shape[1]
    piece = ff // LANE * (D // nf)
    outs = [((rows, D), F32), ((1, ff), F32)] + [((nf // 2, piece, LANE), BF16)] * 2
    scratch = [pltpu.VMEM((rows, ff // nf), BF16), pltpu.VMEM((D, ff // nf), F32)]
    kernel = functools.partial(down_kernel, nf=nf)
    arrays = (h2, c, gp, w, *down)
    return resident(kernel, "ffn_down", 8, 14, (sc,), arrays, outs, scratch)


def mid_kernel(c_ref, dh2_ref, r1_ref, att_ref, wout, vec, dr1_ref, da_ref, gout_ref, gvec_ref):
    gout_ref[...] = jnp.zeros_like(gout_ref)
    gvec_ref[...] = jnp.zeros_like(gvec_ref)

    def add(row, values):
        gvec_ref[row : row + 1, :] += jnp.sum(values, axis=0, keepdims=True)

    def body(i):
        at = block_rows(i)
        c = c_ref[at, :].astype(F32)
        dh2 = dh2_ref[at, :]
        n2, rstd2 = normalize(r1_ref[at, :])
        add(G2, dh2 * n2)
        add(S2, dh2)
        add(DB, c)
        dr1 = c + norm_back(dh2 * vec[G2 : G2 + 1, :D], n2, rstd2)
        dr1_ref[at, :] = dr1
        dy = dr1.astype(BF16)
        add(OB, dy.astype(F32))
        gout_ref[...] += dot_at(att_ref[at, :], dy)
        da_ref[at, :] = dot_bt(dy, wout[...]).astype(BF16)

    each_block(c_ref.shape[0], body)


def mid(c, dh2, r1, att, wout, vec):
    rows = c.shape[0]
    outs = [((rows, D), F32), ((rows, D), BF16), ((D, D), F32), ((8, D), F32)]
    return resident(mid_kernel, "mid", 5, 12, (), (c, dh2, r1, att, wout, vec), outs)


def piece_rows(used, parts):
    return -(-used // (16 * parts)) * 16 * parts


def columns_of(half):
    wide = PAIRS // 2 * LANE
    return [slice(t * D + half * wide, t * D + (half + 1) * wide) for t in range(3)]


def back_kernel(sc, x_ref, da_ref, h1_ref, packed_ref, p_ref, tabs, wqkv, vec, nsum_ref, *refs, nf, copies, half, first, last):
    if half:
        (dub_ref, gvec_ref, before_ref, sums_ref), refs = refs[:4], refs[4:]
    else:
        (gout_ref,), refs = refs[:1], refs[1:]
    olds, refs = ((), refs) if first else (refs[:3], refs[3:])
    (dh1_ref, acc, acc_span, accv), refs = refs[:4], refs[4:]
    if last:
        (sum_ref, far_send, far_keep, send_ref, keep_ref), refs = refs[:5], refs[5:]
    (dp_ref,) = refs
    wide = PAIRS // 2 * LANE
    columns = columns_of(half)
    for k, ref in enumerate((acc, acc_span, accv)):
        ref[...] = jnp.zeros_like(ref) if first else olds[k][...]

    def add(row, values):
        accv[row : row + 1, : values.shape[1]] += jnp.sum(values, axis=0, keepdims=True)

    def body(i):
        rows = block_rows(i)
        low = lax.broadcasted_iota(jnp.int32, (SPAN, LANE), 1) < HEAD
        for s in range(ROWS // SPAN):
            at = block_rows(i * (ROWS // SPAN) + s, SPAN)
            to = slice(s * SPAN, (s + 1) * SPAN)
            for k in range(PAIRS // 2):
                p = half * (PAIRS // 2) + k
                cq, ck, cv = (slice(t * D + p * LANE, t * D + (p + 1) * LANE) for t in range(3))
                oq, ok, ov = (slice(t * wide + k * LANE, t * wide + (k + 1) * LANE) for t in range(3))
                q = packed_ref[at, cq] * SCALE
                do = da_ref[at, cq]
                zero = jnp.zeros_like(q)
                q2 = jnp.concatenate([jnp.where(low, q, zero), jnp.where(low, zero, q)], axis=0)
                do2 = jnp.concatenate([jnp.where(low, do, zero), jnp.where(low, zero, do)], axis=0)
                kc = jnp.concatenate([packed_ref[at, ck], tabs[:, cq]], axis=0)
                vc = jnp.concatenate([packed_ref[at, cv], tabs[:, ck]], axis=0)
                w = p_ref[(i * (ROWS // SPAN) + s) * PAIRS + p]
                wf = w.astype(F32)
                dp = dot_bt(do2, vc)
                delta = jnp.sum(wf * dp, axis=1, keepdims=True)
                ds = (wf * (dp - delta)).astype(BF16)
                dq2 = dot(ds, kc)
                dq = jnp.where(low, dq2[:SPAN], dq2[SPAN:]) * SCALE
                dk = dot_at(ds, q2)
                dv = dot_at(w, do2)
                acc_span[:, oq] += dk[SPAN:]
                acc_span[:, ok] += dv[SPAN:]
                dp_ref[to, oq] = dq.astype(BF16)
                dp_ref[to, ok] = dk[:SPAN].astype(BF16)
                dp_ref[to, ov] = dv[:SPAN].astype(BF16)
        dpk = dp_ref[...]
        add(QB, dpk.astype(F32))
        acc[...] += dot_at(h1_ref[rows, :], dpk)
        dh1 = dot_bt(dpk[:, :wide], wqkv[:, columns[0]])
        for t in (1, 2):
            dh1 = dh1 + dot_bt(dpk[:, t * wide : (t + 1) * wide], wqkv[:, columns[t]])
        if half:
            dh1 = dh1 + before_ref[rows, :]
            n1, _ = normalize(x_ref[rows, :].astype(F32))
            add(G1, dh1 * n1)
            add(S1, dh1)
        dh1_ref[block_rows(i - start), :] = dh1

    blocks = dh1_ref.shape[0] // ROWS
    start = 0 if first else x_ref.shape[0] // ROWS - blocks
    each_block(blocks * ROWS, lambda i: body(i + start))
    if not last:
        return

    span = acc_span[...]
    bit = sc[SC_C] & 1
    each = span.shape[0] // copies
    for k in range(copies):
        code = code_of(k, copies)
        part = span[k * each : (k + 1) * each]
        hold = jnp.concatenate(
            [part[:, t * LANE : (t + 1) * LANE] for t in range(2 * wide // LANE)], axis=0
        ).astype(BF16)
        to = slice(code % (copies // 2) * hold.shape[0], (code % (copies // 2) + 1) * hold.shape[0])
        mine = bit == code // (copies // 2)

        @pl.when(mine)
        def _():
            far_keep[to, :] = hold

        @pl.when(jnp.logical_not(mine))
        def _():
            far_send[to, :] = hold

    span = span * INV_ROOT
    low_span = span.astype(BF16)
    nsum = nsum_ref[...]
    hs = (nsum * vec[G1 : G1 + 1, :D] + SPAN * vec[S1 : S1 + 1, :D]).astype(BF16)
    acc[:, wide:] += dot_at(hs, low_span)
    accv[QB : QB + 1, wide : 3 * wide] += SPAN * jnp.sum(span, axis=0, keepdims=True)
    de = dot_bt(low_span[:, :wide], wqkv[:, columns[1]])
    de = de + dot_bt(low_span[:, wide:], wqkv[:, columns[2]])
    block = D // nf
    if half:
        de = de + sums_ref[: de.shape[0], :]
        add(G1, de * nsum)
        accv[S1 : S1 + 1, :D] += SPAN * jnp.sum(de, axis=0, keepdims=True)
        bias = sums_ref[de.shape[0] : de.shape[0] + 8, :]
    else:
        sum_ref[: de.shape[0], :] = de
        tail = [accv[QB : QB + 1, t * wide : (t + 1) * wide] for t in range(3)]
        bias = jnp.concatenate(tail + [jnp.zeros((5, wide), F32)], axis=0)
        sum_ref[de.shape[0] : de.shape[0] + 8, :] = jnp.concatenate([bias, bias], axis=1)

    for q in range(nf):
        ref = send_ref if q % 2 else keep_ref
        fq = sc[SC_F] ^ q
        at = pl.ds(pl.multiple_of(fq * block, block), block)
        base = 0
        pieces = [acc[at, :].astype(BF16)]
        if not half:
            pieces.append(gout_ref[at, :].astype(BF16))
        for piece in pieces:
            for j in range(piece.shape[1] // LANE):
                ref[q // 2, base : base + block, :] = piece[:, j * LANE : (j + 1) * LANE]
                base += block
        if half:
            whole = jnp.concatenate(
                [
                    part
                    for t in range(3)
                    for part in (bias[t : t + 1, :wide], accv[QB : QB + 1, t * wide : (t + 1) * wide])
                ],
                axis=1,
            )
            accv[QB + 1 : QB + 2, : 3 * D] = whole
            three = [
                accv[QB + 1 : QB + 2, pl.ds(pl.multiple_of((fq * 3 + t) * block, block), block)]
                for t in range(3)
            ]
            four = [
                dub_ref[0:1, pl.ds(pl.multiple_of((fq * 4 + t) * block, block), block)]
                for t in range(4)
            ]
            small = jnp.concatenate(
                [accv[G1 : G1 + 1, at], accv[S1 : S1 + 1, at]]
                + three
                + [gvec_ref[OB : OB + 1, at], gvec_ref[G2 : G2 + 1, at], gvec_ref[S2 : S2 + 1, at]]
                + four
                + [gvec_ref[DB : DB + 1, at], jnp.zeros((3, LANE), F32)],
                axis=0,
            ).astype(BF16)
            ref[q // 2, base : base + 16, :] = small
            base += 16
        left = ref.shape[1] - base
        if left:
            ref[q // 2, base:, :] = jnp.zeros((left, LANE), BF16)


def back(sc, fixed, more, half, nf, copies, old=None, last=True):
    x, nsum = fixed[0], fixed[-1]
    rows = x.shape[0] if last and old is None else x.shape[0] // 2
    nspan = nsum.shape[0]
    wide = PAIRS // 2 * LANE
    block = D // nf
    used = 3 * wide // LANE * block + (16 if half else D // LANE * block)
    piece = piece_rows(used, copies)
    far = nspan // 2 * 2 * wide // LANE
    sums = [((D, 3 * wide), F32), ((nspan, 2 * wide), F32), ((16, 3 * D), F32)]
    outs = [((rows, D), F32)]
    scratch = [pltpu.VMEM((ROWS, 3 * wide), BF16)]
    if last:
        scratch = [pltpu.VMEM(*a) for a in sums] + scratch
        outs += [((nspan + 8, D), F32)]
        outs += [((far, LANE), BF16)] * 2 + [((nf // 2, piece, LANE), BF16)] * 2
    else:
        outs += sums
    kernel = functools.partial(
        back_kernel, nf=nf, copies=copies, half=half, first=old is None, last=last
    )

    def ordered(*refs):
        if not last:
            return kernel(*refs)
        at = len(refs) - len(scratch)
        return kernel(
            *refs[: at - len(outs) + 1], *refs[at:-1], *refs[at - len(outs) + 1 : at], refs[-1]
        )

    arrays = (*fixed, *more, *(old or ()))
    return resident(ordered, f"back_{half}", 9, 18, (sc,), arrays, outs, scratch)


def first_kernel(x_ref, dr1_ref, upper_ref, lower_ref, own_ref, wqkv, vec, o_ref, e_ref):
    i = pl.program_id(0)
    spans = ROWS // SPAN

    @pl.when(i == 0)
    def _():
        each = e_ref.shape[0]
        wide = PAIRS // 2 * LANE
        total = jnp.zeros((each, D), F32)
        for half in range(2):
            for k, columns in enumerate(columns_of(half)[1:]):
                for t in range(wide // LANE):
                    row = ((half * 2 + k) * (wide // LANE) + t) * each
                    own = own_ref[row : row + each, :].astype(F32) * INV_ROOT
                    cols = slice(columns.start + t * LANE, columns.start + (t + 1) * LANE)
                    total = total + dot_bt(own.astype(BF16), wqkv[:, cols])
        e_ref[...] = total

    at = block_rows(i)
    n1, rstd1 = normalize(x_ref[at, :].astype(F32))
    extra = jnp.concatenate(
        [jnp.broadcast_to(e_ref[pl.ds(i * spans + s, 1), :], (SPAN, D)) for s in range(spans)],
        axis=0,
    )
    half = pl.num_programs(0) // 2

    def write(ref, k):
        dh1 = ref[block_rows(k), :] + extra
        o_ref[...] = dr1_ref[at, :] + norm_back(dh1 * vec[G1 : G1 + 1, :D], n1, rstd1)

    @pl.when(i < half)
    def _():
        write(upper_ref, i)

    @pl.when(i >= half)
    def _():
        write(lower_ref, i - half)


def first_back(x, dr1, upper, lower, own, wqkv, vec):
    rows = x.shape[0]
    return pl.pallas_call(
        first_kernel,
        grid=(rows // ROWS,),
        in_specs=in_vmem(7),
        out_specs=pl.BlockSpec((ROWS, D), lambda i: (i, 0)),
        out_shape=jax.ShapeDtypeStruct((rows, D), F32),
        scratch_shapes=[pltpu.VMEM((rows // SPAN, D), F32)],
        compiler_params=params(8),
        name="first_back",
        cost_estimate=cost(3),
    )(x, dr1, upper, lower, own, wqkv, vec)


def mixed_kernel(sc, r1_ref, g_ref, vec, *refs):
    w_refs, o_ref = refs[:-1], refs[-1]
    at = block_rows(pl.program_id(0))
    total = r1_ref[at, :] + vec[DB : DB + 1, :D]
    width = w_refs[0].shape[0]
    for q, w_ref in enumerate(w_refs):
        cols = pl.ds(pl.multiple_of((sc[SC_F] ^ q) * width, width), width)
        total = total + dot(g_ref[at, cols], w_ref[...])
    o_ref[...] = total.astype(BF16)


def block_output(sc, r1, g, vec, down):
    rows = r1.shape[0]
    return pl.pallas_call(
        mixed_kernel,
        grid=(rows // ROWS,),
        in_specs=[pl.BlockSpec(memory_space=pltpu.SMEM)] + in_vmem(3 + len(down)),
        out_specs=pl.BlockSpec((ROWS, D), lambda i: (i, 0)),
        out_shape=jax.ShapeDtypeStruct((rows, D), BF16),
        compiler_params=params(8),
        name="block_output",
        cost_estimate=cost(4),
    )(sc, r1, g, vec, *down)


def swap(array, axis, bit):
    n = lax.axis_size(axis)
    return lax.ppermute(array, axis, [(k, k ^ bit) for k in range(n)])


def after(array, *others):
    return lax.optimization_barrier((array, others))[0]


def first_gather(array, axis):
    return swap(array, axis, lax.axis_size(axis) // 2)


def gathered(array, far, axis):
    n = lax.axis_size(axis)
    bit = n // 2
    held = {0: array, bit: far}
    bit //= 2
    while bit:
        for r in sorted(held):
            held[r ^ bit] = swap(held[r], axis, bit)
        bit //= 2
    return [held[r] for r in range(n)]


def fold_kernel(sc, *refs, bit):
    own = lax.div(sc[SC_C], bit) & 1 if bit else 0
    arrays, (send_ref, own_ref) = refs[:-2], refs[-2:]
    at = 0
    for keep_ref, got_ref in zip(arrays[0::2], arrays[1::2]):
        a, _, h, _ = keep_ref.shape
        for ref, half in ((send_ref, 1 - own), (own_ref, own)):
            for k in range(a):
                total = keep_ref[k, half].astype(F32) + got_ref[k, half].astype(F32)
                ref[k, at : at + h, :] = total.astype(BF16)
        at += h


def fold(sc, bit, *pairs, micros=1):
    a = pairs[0][0].shape[0]
    h = sum(keep.shape[2] for keep, _ in pairs)
    arrays = [array for pair in pairs for array in pair]
    kernel = functools.partial(fold_kernel, bit=bit)
    return resident(kernel, "fold", micros, 8, (sc,), arrays, [((a, h, LANE), BF16)] * 2)


def refold_kernel(sc, keep_ref, got_ref, send_ref, own_ref, *, bit, sizes):
    own = lax.div(sc[SC_C], bit) & 1
    at = 0
    for h in sizes:
        for ref, half in ((send_ref, 1 - own), (own_ref, own)):
            rows = pl.ds(pl.multiple_of(2 * at + half * h, 16), h)
            total = keep_ref[rows, :].astype(F32) + got_ref[rows, :].astype(F32)
            ref[at : at + h, :] = total.astype(BF16)
        at += h


def refold(sc, bit, keep, got, sizes, micros=1):
    outs = [((sum(sizes), LANE), BF16)] * 2
    kernel = functools.partial(refold_kernel, bit=bit, sizes=sizes)
    return resident(kernel, "fold", micros, 8, (sc,), (keep, got), outs)


def last_kernel(keep_ref, got_ref, o_ref, *rest):
    used = o_ref.shape[0]
    total = keep_ref[:used, :].astype(F32) + got_ref[:used, :].astype(F32)
    o_ref[...] = total.astype(BF16)
    for ref in rest:
        total = keep_ref[used:, :].astype(F32) + got_ref[used:, :].astype(F32)
        ref[...] = total.astype(BF16)


def last_sum(keep, got, used):
    outs = [((used, LANE), BF16)]
    if used < keep.shape[0]:
        outs.append(((keep.shape[0] - used, LANE), BF16))
    return resident(last_kernel, "last", 1, 8, (), (keep, got), outs)


class Sequence:
    def __init__(self):
        self.last = ()

    def next(self, array):
        return after(array, *self.last) if self.last else array

    def made(self, *arrays):
        self.last = arrays


class Part:
    def __init__(self, sc, seq, keep, send):
        self.sc, self.seq, self.keep, self.send = sc, seq, keep, send
        self.count, self.rows = keep.shape[0], keep.shape[1]
        self.total = self.rows
        self.move("fsdp", 1)

    def move(self, axis, bit):
        self.got = swap(self.send, axis, bit)

    def view(self, axis):
        if axis == "fsdp":
            self.count //= 2
            return 1, 2, self.count * self.rows, LANE
        self.rows //= 2
        return self.count, 2, self.rows, LANE

    def pair(self, axis):
        view = self.view(axis)
        return self.keep.reshape(view), self.got.reshape(view)

    def step(self, axis, bit, micros=1):
        keep, got = self.pair(axis)
        pair = (self.seq.next(keep), got)
        self.send, self.keep = fold(self.sc, bit if axis == "ctx" else 0, pair, micros=micros)
        self.seq.made(self.keep, self.send)
        self.move(axis, bit)


def ctx_bits():
    n = lax.axis_size("ctx")
    return [1 << k for k in range(n.bit_length() - 1)]


class Union:
    def __init__(self, sc, seq, parts, extra=()):
        self.sc, self.seq = sc, seq
        self.bits = ctx_bits()
        pairs = [part.pair("ctx") for part in parts]
        for keep, got in extra:
            view = (1, 2, keep.shape[0] // 2, LANE)
            pairs.append((keep.reshape(view), got.reshape(view)))
        self.sizes = [keep.shape[2] for keep, _ in pairs]
        self.used = sum(self.sizes[: len(parts)]) * 2 // self.bits[-1]
        pairs[0] = (self.seq.next(pairs[0][0]), pairs[0][1])
        self.received(self.bits[1], *(a[0] for a in fold(sc, self.bits[1], *pairs)))
        self.at = 2

    def received(self, bit, send, keep):
        self.keep = keep
        self.seq.made(keep, send)
        self.got = swap(send, "ctx", bit)

    def more(self):
        return self.at < len(self.bits)

    def step(self, micros=1):
        bit = self.bits[self.at]
        self.at += 1
        self.sizes = [size // 2 for size in self.sizes]
        keep = self.seq.next(self.keep)
        self.received(bit, *refold(self.sc, bit, keep, self.got, self.sizes, micros))

    def end(self):
        own, *rest = last_sum(self.seq.next(self.keep), self.got, self.used)
        self.received(self.bits[-1], own, own)
        self.at = len(self.bits) - 1
        return rest[0] if rest else None

    def gathering(self):
        return self.at > 0

    def join(self):
        both = jnp.concatenate([self.seq.next(self.keep), self.got], axis=0)
        self.at -= 1
        self.received(self.bits[self.at], both, both)

    def rows(self):
        both = jnp.concatenate([self.seq.next(self.keep), self.got], axis=0)
        return both.reshape(lax.axis_size("ctx"), -1, LANE)


def code_of(index, n):
    code = 0
    for k in range(n.bit_length() - 1):
        bit = index >> k if isinstance(index, int) else lax.div(index, 1 << k)
        code = 2 * code + (bit & 1)
    return code


def finish_kernel(sc, got_ref, *refs, heights, plan):
    outs, rows = refs[:-1], refs[-1]
    n = got_ref.shape[0]
    code = code_of(sc[SC_C], n)
    for k in range(n):
        at, base = 0, 0
        for height in heights:
            h = height // n
            to = pl.multiple_of(base + (code ^ k) * h, 16)
            rows[pl.ds(to, h), :] = got_ref[k, at : at + h, :].astype(F32)
            at, base = at + h, base + height
    for ref, places in zip(outs, plan):
        height = ref.shape[0]
        for j, place in enumerate(places):
            ref[:, j * LANE : (j + 1) * LANE] = rows[place : place + height, :]


def finish(sc, got, heights, shapes, plan):
    return pl.pallas_call(
        functools.partial(finish_kernel, heights=heights, plan=plan),
        in_specs=[pl.BlockSpec(memory_space=pltpu.SMEM)] + in_vmem(1),
        out_shape=[jax.ShapeDtypeStruct(shape, F32) for shape in shapes],
        scratch_shapes=[pltpu.VMEM((sum(heights), LANE), F32)],
        compiler_params=params(16),
        name="finish",
        cost_estimate=cost(2),
    )(sc, got)


def local(
    tokens, ln1_gain, ln1_shift, qkv_weight, qkv_bias, out_weight, out_bias, ln2_gain, ln2_shift,
    up_weight, up_bias, down_weight, down_bias, seq_lengths, span_order, cotangent,
):
    nf = lax.axis_size("fsdp")
    nc = lax.axis_size("ctx")
    x, c = tokens[0], cotangent[0]
    spans = x.shape[0] // SPAN
    seqs = seq_lengths.shape[1]
    weights = packed_params(
        qkv_weight, out_weight,
        (ln1_gain, ln1_shift, qkv_bias, out_bias, ln2_gain, ln2_shift, up_bias, down_bias),
    )
    scalars = jnp.concatenate(
        [
            lax.axis_index("fsdp").reshape(1),
            lax.axis_index("ctx").reshape(1),
            (lax.axis_index("ctx") * spans).reshape(1),
            seq_lengths[0],
            span_order[0],
        ]
    ).astype(jnp.int32)
    far_weights = first_gather(weights, "fsdp")
    sums = span_sums(x, nc)
    nsum = lax.all_to_all(sums, "ctx", 0, 0, tiled=True).reshape(nc * spans, D)
    far_weights = after(far_weights, nsum)
    weights = gathered(weights, far_weights, "fsdp")
    up_weight = after(up_weight, far_weights)
    far_up = first_gather(up_weight, "fsdp")
    down_weight = after(down_weight, far_weights)
    far_down = first_gather(down_weight, "fsdp")

    packed, p, att, h1, wqkv, wout, vec, tabs = attend(
        scalars, x, span_order, nsum, weights, seqs
    )
    up = gathered(up_weight, after(far_up, att), "fsdp")
    r1, h2 = proj(x, att, wout, vec)
    g, gp, wup = ffn_up(scalars, h2, vec, up)
    down = gathered(down_weight, after(far_down, g), "fsdp")
    dsend, dkeep = down_gradient(scalars, g, c, nf)
    gp = after(gp, dkeep)
    dh2, dub, usend, ukeep = ffn_down(scalars, h2, c, gp, wup, down)
    bits = ctx_bits()
    near = [("fsdp", 1 << k) for k in range(1, nf.bit_length() - 1)]

    seq = Sequence()
    from_down = Part(scalars, seq, dkeep, dsend)
    from_down.step(*near[0])
    dr1, da, gout, gvec = mid(c, seq.next(dh2), r1, att, wout, vec)
    seq.made(da)
    from_up = Part(scalars, seq, ukeep, usend)
    from_up.step("ctx", bits[0])
    da = seq.next(da)
    fixed = (x, da, h1, packed, p, tabs, wqkv, vec, nsum)
    dh1, sums, fsend0, fkeep0, send, keep = back(scalars, fixed, (gout,), 0, nf, nc)
    seq.made(dh1)
    first = Part(scalars, seq, keep, send)
    from_down.step("ctx", bits[0])
    from_up.step(*near[0])
    dh1 = seq.next(dh1)
    upper, *old = back(scalars, fixed, (dub, gvec, dh1, sums), 1, nf, nc, last=False)
    seq.made(old[0])
    first.step(*near[0])
    feed = Union(scalars, seq, [from_down, from_up])
    old[0] = seq.next(old[0])
    lower, _, fsend1, fkeep1, send, keep = back(
        scalars, fixed, (dub, gvec, dh1, sums), 1, nf, nc, old=old
    )
    seq.made(lower)
    second = Part(scalars, seq, keep, send)
    far = [(k, swap(t, "ctx", bits[0])) for k, t in ((fkeep0, fsend0), (fkeep1, fsend1))]
    while feed.more():
        feed.step(FILL)
    first.step("ctx", bits[0], FILL)
    second.step(*near[0])
    mixed = block_output(scalars, seq.next(r1), g, vec, down)
    seq.made(mixed, *(got for _, got in far))
    second.step("ctx", bits[0])
    feed.end()
    rest = Union(scalars, seq, [first, second], far)
    feed.join()
    while rest.more():
        rest.step()
    while feed.at > 1:
        feed.join()
    own_span = rest.end()
    feed.join()
    tokens_grad = first_back(seq.next(x), dr1, upper, lower, own_span, wqkv, vec)
    seq.made(tokens_grad)
    while rest.gathering():
        rest.join()
    block = D // nf
    height, width = down_weight.shape[0], up_weight.shape[1]
    heights = (from_down.total, from_up.total)
    grad_down, grad_up = finish(
        scalars,
        feed.rows(),
        heights,
        [(height, D), (block, width)],
        [
            [height * j for j in range(D // LANE)],
            [heights[0] + block * j for j in range(width // LANE)],
        ],
    )
    seq.made(grad_down)
    half = PAIRS // 2
    plan = [
        [
            p // half * first.total + block * (t * half + p % half)
            for t in range(3)
            for p in range(PAIRS)
        ],
        [block * (3 * half + j) for j in range(D // LANE)],
    ]
    shapes = [(block, 3 * D), (block, D)]
    at = first.total + 3 * half * block
    for wide in (block, block, 3 * block, block, block, block, 4 * block, block):
        shapes.append((1, wide))
        plan.append([at + j for j in range(wide // LANE)])
        at += wide // LANE
    grad_qkv, grad_out, *vectors = finish(
        scalars, rest.rows(), (first.total, second.total), shapes, plan
    )
    g1, s1, qb, ob, g2, s2, ub, db = (v.reshape(-1) for v in vectors)
    return (
        mixed[None], tokens_grad[None], g1, s1, grad_qkv, qb, grad_out, ob, g2, s2,
        grad_up, ub, grad_down, db,
    )


def solution(mesh):
    rows, one, two = P("fsdp", "ctx", None), P("fsdp"), P("fsdp", None)
    return jax.shard_map(
        local,
        mesh=mesh,
        in_specs=(
            rows, one, one, two, one, two, one, one, one, two, one, two, one, two, two, rows,
        ),
        out_specs=(rows, rows, one, one, two, one, two, one, one, one, two, one, two, one),
        check_vma=False,
    )
```

```python
import functools

import jax
import jax.numpy as jnp
from jax import lax
from jax.experimental import pallas as pl
from jax.experimental.pallas import tpu as pltpu
from jax.sharding import PartitionSpec as P

D = 512
HEADS = 8
HEAD = 64
SPAN = 128
LANE = 128
PAIRS = D // LANE
ROWS = 256
EPSILON = 1e-05
MASKED = -1e30
SCALE = HEAD**-0.5
FILL = 4
INV_ROOT = SPAN**-0.5
F32 = jnp.float32
BF16 = jnp.bfloat16

G1, S1, OB, G2, S2, DB, QB, UB = range(8)
SC_F, SC_C, SC_SLOT, SC_LEN = range(4)


def dot(a, b):
    return lax.dot_general(a, b, (((1,), (0,)), ((), ())), preferred_element_type=F32)


def dot_bt(a, b):
    return lax.dot_general(a, b, (((1,), (1,)), ((), ())), preferred_element_type=F32)


def dot_at(a, b):
    return lax.dot_general(a, b, (((0,), (0,)), ((), ())), preferred_element_type=F32)


def normalize(values):
    centre = values - jnp.mean(values, axis=-1, keepdims=True)
    spread = jnp.mean(centre * centre, axis=-1, keepdims=True)
    rstd = lax.rsqrt(spread + EPSILON)
    return centre * rstd, rstd


def norm_back(e, n, rstd):
    return rstd * (
        e - jnp.mean(e, axis=-1, keepdims=True) - n * jnp.mean(e * n, axis=-1, keepdims=True)
    )


def params(mib):
    return pltpu.CompilerParams(vmem_limit_bytes=mib * 1024 * 1024)


def in_vmem(count):
    return [pl.BlockSpec(memory_space=pltpu.VMEM) for _ in range(count)]


def cost(micros):
    return pl.CostEstimate(
        flops=int(micros * 1e9), transcendentals=0, bytes_accessed=int(micros * 1e6)
    )


def resident(kernel, name, micros, mib, scalars, arrays, outs, scratch=()):
    return pl.pallas_call(
        kernel,
        in_specs=[pl.BlockSpec(memory_space=pltpu.SMEM)] * len(scalars) + in_vmem(len(arrays)),
        out_specs=in_vmem(len(outs)),
        out_shape=[jax.ShapeDtypeStruct(shape, dtype) for shape, dtype in outs],
        scratch_shapes=list(scratch),
        compiler_params=params(mib),
        name=name,
        cost_estimate=cost(micros),
    )(*scalars, *arrays)


def block_rows(i, size=ROWS):
    if isinstance(i, int):
        return slice(i * size, (i + 1) * size)
    return pl.ds(pl.multiple_of(i * size, size), size)


def each_block(rows, body, size=ROWS, parts=1):
    each = rows // size // parts
    if parts == 1:
        for i in range(each):
            body(i)
        return

    def step(n, carry):
        for k in range(each):
            body(n * each + k)
        return carry

    lax.fori_loop(0, parts, step, 0)


def sums_kernel(x_ref, o_ref):
    spans = x_ref.shape[0] // SPAN
    sums = []
    for s in range(spans):
        n, _ = normalize(x_ref[s * SPAN : (s + 1) * SPAN, :].astype(F32))
        sums.append(jnp.sum(n, axis=0, keepdims=True))
    table = jnp.concatenate(sums, axis=0)
    for k in range(o_ref.shape[0]):
        o_ref[k] = table


def span_sums(x, copies):
    spans = x.shape[0] // SPAN
    return resident(sums_kernel, "span_sums", 3, 16, (), (x,), [((copies, spans, D), F32)])[0]


def pack_kernel(qkv_ref, out_ref, *refs):
    o_ref = refs[-1]
    rows, width = qkv_ref.shape
    o_ref[:rows, :width] = qkv_ref[...]
    o_ref[:rows, width:] = out_ref[...]
    parts = [ref[...].astype(F32) for ref in refs[:-1]]
    used = sum(part.shape[0] for part in parts)
    parts.append(jnp.zeros((16 - used, LANE), F32))
    o_ref[rows:, :LANE] = jnp.concatenate(parts, axis=0).astype(BF16)
    o_ref[rows:, LANE:] = jnp.zeros((16, o_ref.shape[1] - LANE), BF16)


def packed_params(qkv, out, vectors):
    shape = (qkv.shape[0] + 16, qkv.shape[1] + out.shape[1])
    vectors = [v.reshape(-1, LANE) for v in vectors]
    arrays = [qkv, out] + vectors
    return pl.pallas_call(
        pack_kernel,
        out_shape=jax.ShapeDtypeStruct(shape, BF16),
        compiler_params=params(58),
        name="pack",
        cost_estimate=cost(1),
    )(*arrays)


def attend_kernel(sc, x_ref, order_ref, nsum_ref, *refs, nf, seqs):
    param_refs = refs[:nf]
    (packed_ref, p_ref, att_ref, h1_ref, wqkv, wout, vec, tabs) = refs[nf:]
    nspan = nsum_ref.shape[0]
    block = D // nf

    vec[...] = jnp.zeros_like(vec)
    for q in range(nf):
        fq = sc[SC_F] ^ q
        at = pl.ds(pl.multiple_of(fq * block, block), block)
        wqkv[at, :] = param_refs[q][:block, : 3 * D]
        wout[at, :] = param_refs[q][:block, 3 * D :]
        sm = param_refs[q][block:, :LANE].astype(F32)
        for row, src in ((G1, 0), (S1, 1), (OB, 5), (G2, 6), (S2, 7), (DB, 12)):
            vec[row : row + 1, at] = sm[src : src + 1]
        for t in range(3):
            at3 = pl.ds(pl.multiple_of(fq * 3 * block + t * block, block), block)
            vec[QB : QB + 1, at3] = sm[2 + t : 3 + t]
        for t in range(4):
            at4 = pl.ds(pl.multiple_of(fq * 4 * block + t * block, block), block)
            vec[UB : UB + 1, at4] = sm[8 + t : 9 + t]
    hs = nsum_ref[...] * vec[G1 : G1 + 1, :D] + SPAN * vec[S1 : S1 + 1, :D]
    hi = hs.astype(BF16)
    lo = (hs - hi.astype(F32)).astype(BF16)
    both = dot(jnp.concatenate([hi, lo], axis=0), wqkv[:, D:])
    t = both[:nspan] + both[nspan:] + SPAN * vec[QB : QB + 1, D : 3 * D]
    tabs[...] = (t * INV_ROOT).astype(BF16)
    prompt = lax.div(sc[SC_LEN], SPAN)
    spans = ROWS // SPAN

    def body(i):
        rows = block_rows(i)
        n1, _ = normalize(x_ref[rows, :].astype(F32))
        h1 = (n1 * vec[G1 : G1 + 1, :D] + vec[S1 : S1 + 1, :D]).astype(BF16)
        h1_ref[rows, :] = h1
        packed_ref[rows, :] = (dot(h1, wqkv[...]) + vec[QB : QB + 1, : 3 * D]).astype(BF16)

        lane = lax.broadcasted_iota(jnp.int32, (SPAN, LANE), 1)
        low = lane < HEAD
        causal = jnp.where(
            lane <= lax.broadcasted_iota(jnp.int32, (SPAN, LANE), 0), 0.0, MASKED
        ).astype(F32)
        order = order_ref[...]
        for s in range(spans):
            a = sc[SC_LEN + seqs + sc[SC_SLOT] + i * spans + s]
            start, begin = 0, 0
            for k in range(seqs):
                begin = jnp.where(start <= a, start, begin)
                start = start + lax.div(sc[SC_LEN + k], SPAN)
            seen = (order < a) & ((order >= begin) | (order < prompt))
            far = jnp.where(seen, 0.0, MASKED).astype(F32)
            bias = jnp.concatenate([causal, jnp.broadcast_to(far, (SPAN, nspan))], axis=1)
            bias = jnp.concatenate([bias, bias], axis=0)
            at = block_rows(i * spans + s, SPAN)
            for p in range(PAIRS):
                cq, ck, cv = (slice(t * D + p * LANE, t * D + (p + 1) * LANE) for t in range(3))
                q = packed_ref[at, cq] * SCALE
                zero = jnp.zeros_like(q)
                q2 = jnp.concatenate([jnp.where(low, q, zero), jnp.where(low, zero, q)], axis=0)
                kc = jnp.concatenate([packed_ref[at, ck], tabs[:, cq]], axis=0)
                vc = jnp.concatenate([packed_ref[at, cv], tabs[:, ck]], axis=0)
                scores = dot_bt(q2, kc) + bias
                peak = jnp.max(scores, axis=1, keepdims=True)
                e = jnp.exp(scores - peak)
                w = (e * (1.0 / jnp.sum(e, axis=1, keepdims=True))).astype(BF16)
                p_ref[(i * spans + s) * PAIRS + p, :SPAN] = w[:, :SPAN].T
                p_ref[(i * spans + s) * PAIRS + p, SPAN:] = w[:, SPAN:].T
                o2 = dot(w, vc)
                att_ref[at, cq] = jnp.where(low, o2[:SPAN], o2[SPAN:]).astype(BF16)

    each_block(x_ref.shape[0], body, parts=2)


def proj_kernel(x_ref, att_ref, wout, vec, r1_ref, h2_ref):
    def body(i):
        at = block_rows(i)
        r1 = x_ref[at, :].astype(F32) + (dot(att_ref[at, :], wout[...]) + vec[OB : OB + 1, :D])
        r1_ref[at, :] = r1
        n2, _ = normalize(r1)
        h2_ref[at, :] = (n2 * vec[G2 : G2 + 1, :D] + vec[S2 : S2 + 1, :D]).astype(BF16)

    each_block(x_ref.shape[0], body)


def proj(x, att, wout, vec):
    outs = [(x.shape, F32), (x.shape, BF16)]
    return resident(proj_kernel, "proj", 3, 8, (), (x, att, wout, vec), outs)


def attend(sc, x, order, nsum, weights, seqs):
    rows = x.shape[0]
    nspan = nsum.shape[0]
    outs = [
        ((rows, 3 * D), BF16),
        ((rows // SPAN * PAIRS, SPAN + nspan, 2 * SPAN), BF16),
        ((rows, D), BF16),
        ((rows, D), BF16),
        ((D, 3 * D), BF16),
        ((D, D), BF16),
        ((8, 4 * D), F32),
        ((nspan, 2 * D), BF16),
    ]
    kernel = functools.partial(attend_kernel, nf=len(weights), seqs=seqs)
    arrays = (x, order, nsum, *weights)
    return resident(kernel, "attend", 12, 12, (sc,), arrays, outs)


def relative(step, nf):
    half = nf // 2
    return jnp.where(step < half, 2 * step + 1, 2 * (step - half))


def up_kernel(sc, h2_ref, vec_ref, *refs, nf):
    up_refs = refs[:nf]
    g_ref, gp_ref, w_ref = refs[nf:]
    block = D // nf
    width = w_ref.shape[1] // nf
    k0 = 0.7978845608028654
    for q in range(nf):
        at = pl.ds(pl.multiple_of((sc[SC_F] ^ q) * block, block), block)
        w_ref[at, :] = up_refs[q][...]
    rows = h2_ref.shape[0]

    def body(j):
        cols = pl.ds(pl.multiple_of(j * width, width), width)
        for i in range(rows // ROWS):
            at = block_rows(i)
            u = dot(h2_ref[at, :], w_ref[:, cols]) + vec_ref[UB : UB + 1, cols]
            u2 = u * u
            t = jnp.tanh(u * (k0 + (k0 * 0.044715) * u2))
            half = 0.5 + 0.5 * t
            g_ref[at, cols] = (u * half).astype(BF16)
            slope = u * (k0 + (3 * k0 * 0.044715) * u2)
            gp_ref[at, cols] = (half + (0.5 - 0.5 * t * t) * slope).astype(BF16)

    each_block(nf, body, 1, parts=2)


def ffn_up(sc, h2, vec, up):
    rows, ff = h2.shape[0], up[0].shape[1]
    outs = [((rows, ff), BF16), ((rows, ff), BF16), ((D, ff), BF16)]
    kernel = functools.partial(up_kernel, nf=len(up))
    return resident(kernel, "ffn_up", 8, 12, (sc,), (h2, vec, *up), outs)


def down_grad_kernel(sc, g_ref, c_ref, send_ref, keep_ref, *, nf):
    width = g_ref.shape[1] // nf
    for q in range(nf):
        at = pl.ds(pl.multiple_of((sc[SC_F] ^ q) * width, width), width)
        grad = dot_at(g_ref[:, at], c_ref[...]).astype(BF16)
        ref = send_ref if q % 2 else keep_ref
        for j in range(D // LANE):
            ref[q // 2, j * width : (j + 1) * width, :] = grad[:, j * LANE : (j + 1) * LANE]


def down_gradient(sc, g, c, nf):
    piece = g.shape[1] // nf * D // LANE
    outs = [((nf // 2, piece, LANE), BF16)] * 2
    kernel = functools.partial(down_grad_kernel, nf=nf)
    return resident(kernel, "down_grad", 4, 12, (sc,), (g, c), outs)


def down_kernel(sc, h2_ref, c_ref, gp_ref, w_ref, *refs, nf):
    down_refs = refs[:nf]
    dh2_ref, dub_ref, send_ref, keep_ref, du_ref, grad_ref = refs[nf:]
    width = w_ref.shape[1] // nf
    block = D // nf
    rows = h2_ref.shape[0]
    for s in range(nf):
        f = sc[SC_F] ^ s
        cols = pl.ds(pl.multiple_of(f * width, width), width)
        dub_ref[:, cols] = jnp.zeros((1, width), F32)

        def body(i):
            at = block_rows(i, 2 * ROWS)
            dg = dot_bt(c_ref[at, :], down_refs[s][...])
            du = (dg * gp_ref[at, cols].astype(F32)).astype(BF16)
            du_ref[at, :] = du
            dub_ref[:, cols] += jnp.sum(du.astype(F32), axis=0, keepdims=True)
            dh2 = dot_bt(du, w_ref[:, cols])
            if s == 0:
                dh2_ref[at, :] = dh2
            else:
                dh2_ref[at, :] += dh2

        each_block(rows, body, 2 * ROWS)
        grad_ref[...] = dot_at(h2_ref[...], du_ref[...])
        for q in range(nf):
            ref = send_ref if q % 2 else keep_ref
            piece = grad_ref[pl.ds(pl.multiple_of((sc[SC_F] ^ q) * block, block), block), :]
            piece = piece.astype(BF16)
            for j in range(width // LANE):
                to = pl.multiple_of((f * (width // LANE) + j) * block, block)
                ref[q // 2, pl.ds(to, block), :] = piece[:, j * LANE : (j + 1) * LANE]


def ffn_down(sc, h2, c, gp, w, down):
    nf = len(down)
    rows = h2.shape[0]
    ff = w.shape[1]
    piece = ff // LANE * (D // nf)
    outs = [((rows, D), F32), ((1, ff), F32)] + [((nf // 2, piece, LANE), BF16)] * 2
    scratch = [pltpu.VMEM((rows, ff // nf), BF16), pltpu.VMEM((D, ff // nf), F32)]
    kernel = functools.partial(down_kernel, nf=nf)
    arrays = (h2, c, gp, w, *down)
    return resident(kernel, "ffn_down", 8, 14, (sc,), arrays, outs, scratch)


def mid_kernel(c_ref, dh2_ref, r1_ref, att_ref, wout, vec, dr1_ref, da_ref, gout_ref, gvec_ref):
    gout_ref[...] = jnp.zeros_like(gout_ref)
    gvec_ref[...] = jnp.zeros_like(gvec_ref)

    def add(row, values):
        gvec_ref[row : row + 1, :] += jnp.sum(values, axis=0, keepdims=True)

    def body(i):
        at = block_rows(i)
        c = c_ref[at, :].astype(F32)
        dh2 = dh2_ref[at, :]
        n2, rstd2 = normalize(r1_ref[at, :])
        add(G2, dh2 * n2)
        add(S2, dh2)
        add(DB, c)
        dr1 = c + norm_back(dh2 * vec[G2 : G2 + 1, :D], n2, rstd2)
        dr1_ref[at, :] = dr1
        dy = dr1.astype(BF16)
        add(OB, dy.astype(F32))
        gout_ref[...] += dot_at(att_ref[at, :], dy)
        da_ref[at, :] = dot_bt(dy, wout[...]).astype(BF16)

    each_block(c_ref.shape[0], body)


def mid(c, dh2, r1, att, wout, vec):
    rows = c.shape[0]
    outs = [((rows, D), F32), ((rows, D), BF16), ((D, D), F32), ((8, D), F32)]
    return resident(mid_kernel, "mid", 5, 12, (), (c, dh2, r1, att, wout, vec), outs)


def piece_rows(used, parts):
    return -(-used // (16 * parts)) * 16 * parts


def columns_of(half):
    wide = PAIRS // 2 * LANE
    return [slice(t * D + half * wide, t * D + (half + 1) * wide) for t in range(3)]


def back_kernel(sc, x_ref, da_ref, h1_ref, packed_ref, p_ref, tabs, wqkv, vec, nsum_ref, *refs, nf, copies, half, first, last):
    if half:
        (dub_ref, gvec_ref, before_ref, sums_ref), refs = refs[:4], refs[4:]
    else:
        (gout_ref,), refs = refs[:1], refs[1:]
    olds, refs = ((), refs) if first else (refs[:3], refs[3:])
    (dh1_ref, acc, acc_span, accv), refs = refs[:4], refs[4:]
    if last:
        (sum_ref, far_send, far_keep, send_ref, keep_ref), refs = refs[:5], refs[5:]
    (dp_ref,) = refs
    wide = PAIRS // 2 * LANE
    columns = columns_of(half)
    for k, ref in enumerate((acc, acc_span, accv)):
        ref[...] = jnp.zeros_like(ref) if first else olds[k][...]

    def add(row, values):
        accv[row : row + 1, : values.shape[1]] += jnp.sum(values, axis=0, keepdims=True)

    def body(i):
        rows = block_rows(i)
        low = lax.broadcasted_iota(jnp.int32, (SPAN, LANE), 1) < HEAD
        for s in range(ROWS // SPAN):
            at = block_rows(i * (ROWS // SPAN) + s, SPAN)
            to = slice(s * SPAN, (s + 1) * SPAN)
            for k in range(PAIRS // 2):
                p = half * (PAIRS // 2) + k
                cq, ck, cv = (slice(t * D + p * LANE, t * D + (p + 1) * LANE) for t in range(3))
                oq, ok, ov = (slice(t * wide + k * LANE, t * wide + (k + 1) * LANE) for t in range(3))
                q = packed_ref[at, cq] * SCALE
                do = da_ref[at, cq]
                zero = jnp.zeros_like(q)
                q2 = jnp.concatenate([jnp.where(low, q, zero), jnp.where(low, zero, q)], axis=0)
                do2 = jnp.concatenate([jnp.where(low, do, zero), jnp.where(low, zero, do)], axis=0)
                kc = jnp.concatenate([packed_ref[at, ck], tabs[:, cq]], axis=0)
                vc = jnp.concatenate([packed_ref[at, cv], tabs[:, ck]], axis=0)
                w = p_ref[(i * (ROWS // SPAN) + s) * PAIRS + p]
                wf = w.astype(F32)
                dp = dot_bt(vc, do2)
                delta = jnp.sum(wf * dp, axis=0, keepdims=True)
                ds = (wf * (dp - delta)).astype(BF16)
                dq2 = dot_at(ds, kc)
                dq = jnp.where(low, dq2[:SPAN], dq2[SPAN:]) * SCALE
                dk = dot(ds, q2)
                dv = dot(w, do2)
                acc_span[:, oq] += dk[SPAN:]
                acc_span[:, ok] += dv[SPAN:]
                dp_ref[to, oq] = dq.astype(BF16)
                dp_ref[to, ok] = dk[:SPAN].astype(BF16)
                dp_ref[to, ov] = dv[:SPAN].astype(BF16)
        dpk = dp_ref[...]
        add(QB, dpk.astype(F32))
        acc[...] += dot_at(h1_ref[rows, :], dpk)
        dh1 = dot_bt(dpk[:, :wide], wqkv[:, columns[0]])
        for t in (1, 2):
            dh1 = dh1 + dot_bt(dpk[:, t * wide : (t + 1) * wide], wqkv[:, columns[t]])
        if half:
            dh1 = dh1 + before_ref[rows, :]
            n1, _ = normalize(x_ref[rows, :].astype(F32))
            add(G1, dh1 * n1)
            add(S1, dh1)
        dh1_ref[block_rows(i - start), :] = dh1

    blocks = dh1_ref.shape[0] // ROWS
    start = 0 if first else x_ref.shape[0] // ROWS - blocks
    each_block(blocks * ROWS, lambda i: body(i + start), parts=max(blocks // 2, 1))
    if not last:
        return

    span = acc_span[...]
    bit = sc[SC_C] & 1
    each = span.shape[0] // copies
    for k in range(copies):
        code = code_of(k, copies)
        part = span[k * each : (k + 1) * each]
        hold = jnp.concatenate(
            [part[:, t * LANE : (t + 1) * LANE] for t in range(2 * wide // LANE)], axis=0
        ).astype(BF16)
        to = slice(code % (copies // 2) * hold.shape[0], (code % (copies // 2) + 1) * hold.shape[0])
        mine = bit == code // (copies // 2)

        @pl.when(mine)
        def _():
            far_keep[to, :] = hold

        @pl.when(jnp.logical_not(mine))
        def _():
            far_send[to, :] = hold

    span = span * INV_ROOT
    low_span = span.astype(BF16)
    nsum = nsum_ref[...]
    hs = (nsum * vec[G1 : G1 + 1, :D] + SPAN * vec[S1 : S1 + 1, :D]).astype(BF16)
    acc[:, wide:] += dot_at(hs, low_span)
    accv[QB : QB + 1, wide : 3 * wide] += SPAN * jnp.sum(span, axis=0, keepdims=True)
    de = dot_bt(low_span[:, :wide], wqkv[:, columns[1]])
    de = de + dot_bt(low_span[:, wide:], wqkv[:, columns[2]])
    block = D // nf
    if half:
        de = de + sums_ref[: de.shape[0], :]
        add(G1, de * nsum)
        accv[S1 : S1 + 1, :D] += SPAN * jnp.sum(de, axis=0, keepdims=True)
        bias = sums_ref[de.shape[0] : de.shape[0] + 8, :]
    else:
        sum_ref[: de.shape[0], :] = de
        tail = [accv[QB : QB + 1, t * wide : (t + 1) * wide] for t in range(3)]
        bias = jnp.concatenate(tail + [jnp.zeros((5, wide), F32)], axis=0)
        sum_ref[de.shape[0] : de.shape[0] + 8, :] = jnp.concatenate([bias, bias], axis=1)

    for q in range(nf):
        ref = send_ref if q % 2 else keep_ref
        fq = sc[SC_F] ^ q
        at = pl.ds(pl.multiple_of(fq * block, block), block)
        base = 0
        pieces = [acc[at, :].astype(BF16)]
        if not half:
            pieces.append(gout_ref[at, :].astype(BF16))
        for piece in pieces:
            for j in range(piece.shape[1] // LANE):
                ref[q // 2, base : base + block, :] = piece[:, j * LANE : (j + 1) * LANE]
                base += block
        if half:
            whole = jnp.concatenate(
                [
                    part
                    for t in range(3)
                    for part in (bias[t : t + 1, :wide], accv[QB : QB + 1, t * wide : (t + 1) * wide])
                ],
                axis=1,
            )
            accv[QB + 1 : QB + 2, : 3 * D] = whole
            three = [
                accv[QB + 1 : QB + 2, pl.ds(pl.multiple_of((fq * 3 + t) * block, block), block)]
                for t in range(3)
            ]
            four = [
                dub_ref[0:1, pl.ds(pl.multiple_of((fq * 4 + t) * block, block), block)]
                for t in range(4)
            ]
            small = jnp.concatenate(
                [accv[G1 : G1 + 1, at], accv[S1 : S1 + 1, at]]
                + three
                + [gvec_ref[OB : OB + 1, at], gvec_ref[G2 : G2 + 1, at], gvec_ref[S2 : S2 + 1, at]]
                + four
                + [gvec_ref[DB : DB + 1, at], jnp.zeros((3, LANE), F32)],
                axis=0,
            ).astype(BF16)
            ref[q // 2, base : base + 16, :] = small
            base += 16
        left = ref.shape[1] - base
        if left:
            ref[q // 2, base:, :] = jnp.zeros((left, LANE), BF16)


def back(sc, fixed, more, half, nf, copies, old=None, last=True):
    x, nsum = fixed[0], fixed[-1]
    rows = x.shape[0] if last and old is None else x.shape[0] // 2
    nspan = nsum.shape[0]
    wide = PAIRS // 2 * LANE
    block = D // nf
    used = 3 * wide // LANE * block + (16 if half else D // LANE * block)
    piece = piece_rows(used, copies)
    far = nspan // 2 * 2 * wide // LANE
    sums = [((D, 3 * wide), F32), ((nspan, 2 * wide), F32), ((16, 3 * D), F32)]
    outs = [((rows, D), F32)]
    scratch = [pltpu.VMEM((ROWS, 3 * wide), BF16)]
    if last:
        scratch = [pltpu.VMEM(*a) for a in sums] + scratch
        outs += [((nspan + 8, D), F32)]
        outs += [((far, LANE), BF16)] * 2 + [((nf // 2, piece, LANE), BF16)] * 2
    else:
        outs += sums
    kernel = functools.partial(
        back_kernel, nf=nf, copies=copies, half=half, first=old is None, last=last
    )

    def ordered(*refs):
        if not last:
            return kernel(*refs)
        at = len(refs) - len(scratch)
        return kernel(
            *refs[: at - len(outs) + 1], *refs[at:-1], *refs[at - len(outs) + 1 : at], refs[-1]
        )

    arrays = (*fixed, *more, *(old or ()))
    return resident(ordered, f"back_{half}", 9, 18, (sc,), arrays, outs, scratch)


def first_kernel(x_ref, dr1_ref, upper_ref, lower_ref, own_ref, wqkv, vec, o_ref, e_ref):
    i = pl.program_id(0)
    spans = ROWS // SPAN

    @pl.when(i == 0)
    def _():
        each = e_ref.shape[0]
        wide = PAIRS // 2 * LANE
        total = jnp.zeros((each, D), F32)
        for half in range(2):
            for k, columns in enumerate(columns_of(half)[1:]):
                for t in range(wide // LANE):
                    row = ((half * 2 + k) * (wide // LANE) + t) * each
                    own = own_ref[row : row + each, :].astype(F32) * INV_ROOT
                    cols = slice(columns.start + t * LANE, columns.start + (t + 1) * LANE)
                    total = total + dot_bt(own.astype(BF16), wqkv[:, cols])
        e_ref[...] = total

    at = block_rows(i)
    n1, rstd1 = normalize(x_ref[at, :].astype(F32))
    extra = jnp.concatenate(
        [jnp.broadcast_to(e_ref[pl.ds(i * spans + s, 1), :], (SPAN, D)) for s in range(spans)],
        axis=0,
    )
    half = pl.num_programs(0) // 2

    def write(ref, k):
        dh1 = ref[block_rows(k), :] + extra
        o_ref[...] = dr1_ref[at, :] + norm_back(dh1 * vec[G1 : G1 + 1, :D], n1, rstd1)

    @pl.when(i < half)
    def _():
        write(upper_ref, i)

    @pl.when(i >= half)
    def _():
        write(lower_ref, i - half)


def first_back(x, dr1, upper, lower, own, wqkv, vec):
    rows = x.shape[0]
    return pl.pallas_call(
        first_kernel,
        grid=(rows // ROWS,),
        in_specs=in_vmem(7),
        out_specs=pl.BlockSpec((ROWS, D), lambda i: (i, 0)),
        out_shape=jax.ShapeDtypeStruct((rows, D), F32),
        scratch_shapes=[pltpu.VMEM((rows // SPAN, D), F32)],
        compiler_params=params(8),
        name="first_back",
        cost_estimate=cost(3),
    )(x, dr1, upper, lower, own, wqkv, vec)


def mixed_kernel(sc, r1_ref, g_ref, vec, *refs):
    w_refs, o_ref = refs[:-1], refs[-1]
    at = block_rows(pl.program_id(0))
    total = r1_ref[at, :] + vec[DB : DB + 1, :D]
    width = w_refs[0].shape[0]
    for q, w_ref in enumerate(w_refs):
        cols = pl.ds(pl.multiple_of((sc[SC_F] ^ q) * width, width), width)
        total = total + dot(g_ref[at, cols], w_ref[...])
    o_ref[...] = total.astype(BF16)


def block_output(sc, r1, g, vec, down):
    rows = r1.shape[0]
    return pl.pallas_call(
        mixed_kernel,
        grid=(rows // ROWS,),
        in_specs=[pl.BlockSpec(memory_space=pltpu.SMEM)] + in_vmem(3 + len(down)),
        out_specs=pl.BlockSpec((ROWS, D), lambda i: (i, 0)),
        out_shape=jax.ShapeDtypeStruct((rows, D), BF16),
        compiler_params=params(8),
        name="block_output",
        cost_estimate=cost(4),
    )(sc, r1, g, vec, *down)


def swap(array, axis, bit):
    n = lax.axis_size(axis)
    return lax.ppermute(array, axis, [(k, k ^ bit) for k in range(n)])


def after(array, *others):
    return lax.optimization_barrier((array, others))[0]


def first_gather(array, axis):
    return swap(array, axis, lax.axis_size(axis) // 2)


def gathered(array, far, axis):
    n = lax.axis_size(axis)
    bit = n // 2
    held = {0: array, bit: far}
    bit //= 2
    while bit:
        for r in sorted(held):
            held[r ^ bit] = swap(held[r], axis, bit)
        bit //= 2
    return [held[r] for r in range(n)]


def fold_kernel(sc, *refs, bit):
    own = lax.div(sc[SC_C], bit) & 1 if bit else 0
    arrays, (send_ref, own_ref) = refs[:-2], refs[-2:]
    at = 0
    for keep_ref, got_ref in zip(arrays[0::2], arrays[1::2]):
        a, _, h, _ = keep_ref.shape
        for ref, half in ((send_ref, 1 - own), (own_ref, own)):
            for k in range(a):
                total = keep_ref[k, half].astype(F32) + got_ref[k, half].astype(F32)
                ref[k, at : at + h, :] = total.astype(BF16)
        at += h


def fold(sc, bit, *pairs, micros=1):
    a = pairs[0][0].shape[0]
    h = sum(keep.shape[2] for keep, _ in pairs)
    arrays = [array for pair in pairs for array in pair]
    kernel = functools.partial(fold_kernel, bit=bit)
    return resident(kernel, "fold", micros, 8, (sc,), arrays, [((a, h, LANE), BF16)] * 2)


def refold_kernel(sc, keep_ref, got_ref, send_ref, own_ref, *, bit, sizes):
    own = lax.div(sc[SC_C], bit) & 1
    at = 0
    for h in sizes:
        for ref, half in ((send_ref, 1 - own), (own_ref, own)):
            rows = pl.ds(pl.multiple_of(2 * at + half * h, 16), h)
            total = keep_ref[rows, :].astype(F32) + got_ref[rows, :].astype(F32)
            ref[at : at + h, :] = total.astype(BF16)
        at += h


def refold(sc, bit, keep, got, sizes, micros=1):
    outs = [((sum(sizes), LANE), BF16)] * 2
    kernel = functools.partial(refold_kernel, bit=bit, sizes=sizes)
    return resident(kernel, "fold", micros, 8, (sc,), (keep, got), outs)


def last_kernel(keep_ref, got_ref, o_ref, *rest):
    used = o_ref.shape[0]
    total = keep_ref[:used, :].astype(F32) + got_ref[:used, :].astype(F32)
    o_ref[...] = total.astype(BF16)
    for ref in rest:
        total = keep_ref[used:, :].astype(F32) + got_ref[used:, :].astype(F32)
        ref[...] = total.astype(BF16)


def last_sum(keep, got, used):
    outs = [((used, LANE), BF16)]
    if used < keep.shape[0]:
        outs.append(((keep.shape[0] - used, LANE), BF16))
    return resident(last_kernel, "last", 1, 8, (), (keep, got), outs)


class Sequence:
    def __init__(self):
        self.last = ()

    def next(self, array):
        return after(array, *self.last) if self.last else array

    def made(self, *arrays):
        self.last = arrays


class Part:
    def __init__(self, sc, seq, keep, send):
        self.sc, self.seq, self.keep, self.send = sc, seq, keep, send
        self.count, self.rows = keep.shape[0], keep.shape[1]
        self.total = self.rows
        self.move("fsdp", 1)

    def move(self, axis, bit):
        self.got = swap(self.send, axis, bit)

    def view(self, axis):
        if axis == "fsdp":
            self.count //= 2
            return 1, 2, self.count * self.rows, LANE
        self.rows //= 2
        return self.count, 2, self.rows, LANE

    def pair(self, axis):
        view = self.view(axis)
        return self.keep.reshape(view), self.got.reshape(view)

    def step(self, axis, bit, micros=1):
        keep, got = self.pair(axis)
        pair = (self.seq.next(keep), got)
        self.send, self.keep = fold(self.sc, bit if axis == "ctx" else 0, pair, micros=micros)
        self.seq.made(self.keep, self.send)
        self.move(axis, bit)


def ctx_bits():
    n = lax.axis_size("ctx")
    return [1 << k for k in range(n.bit_length() - 1)]


class Union:
    def __init__(self, sc, seq, parts, extra=()):
        self.sc, self.seq = sc, seq
        self.bits = ctx_bits()
        pairs = [part.pair("ctx") for part in parts]
        for keep, got in extra:
            view = (1, 2, keep.shape[0] // 2, LANE)
            pairs.append((keep.reshape(view), got.reshape(view)))
        self.sizes = [keep.shape[2] for keep, _ in pairs]
        self.used = sum(self.sizes[: len(parts)]) * 2 // self.bits[-1]
        pairs[0] = (self.seq.next(pairs[0][0]), pairs[0][1])
        self.received(self.bits[1], *(a[0] for a in fold(sc, self.bits[1], *pairs)))
        self.at = 2

    def received(self, bit, send, keep):
        self.keep = keep
        self.seq.made(keep, send)
        self.got = swap(send, "ctx", bit)

    def more(self):
        return self.at < len(self.bits)

    def step(self, micros=1):
        bit = self.bits[self.at]
        self.at += 1
        self.sizes = [size // 2 for size in self.sizes]
        keep = self.seq.next(self.keep)
        self.received(bit, *refold(self.sc, bit, keep, self.got, self.sizes, micros))

    def end(self):
        own, *rest = last_sum(self.seq.next(self.keep), self.got, self.used)
        self.received(self.bits[-1], own, own)
        self.at = len(self.bits) - 1
        return rest[0] if rest else None

    def gathering(self):
        return self.at > 0

    def join(self):
        both = jnp.concatenate([self.seq.next(self.keep), self.got], axis=0)
        self.at -= 1
        self.received(self.bits[self.at], both, both)

    def rows(self):
        both = jnp.concatenate([self.seq.next(self.keep), self.got], axis=0)
        return both.reshape(lax.axis_size("ctx"), -1, LANE)


def code_of(index, n):
    code = 0
    for k in range(n.bit_length() - 1):
        bit = index >> k if isinstance(index, int) else lax.div(index, 1 << k)
        code = 2 * code + (bit & 1)
    return code


def finish_kernel(sc, got_ref, *refs, heights, plan):
    outs, rows = refs[:-1], refs[-1]
    n = got_ref.shape[0]
    code = code_of(sc[SC_C], n)
    for k in range(n):
        at, base = 0, 0
        for height in heights:
            h = height // n
            to = pl.multiple_of(base + (code ^ k) * h, 16)
            rows[pl.ds(to, h), :] = got_ref[k, at : at + h, :].astype(F32)
            at, base = at + h, base + height
    for ref, places in zip(outs, plan):
        height = ref.shape[0]
        for j, place in enumerate(places):
            ref[:, j * LANE : (j + 1) * LANE] = rows[place : place + height, :]


def finish(sc, got, heights, shapes, plan):
    return pl.pallas_call(
        functools.partial(finish_kernel, heights=heights, plan=plan),
        in_specs=[pl.BlockSpec(memory_space=pltpu.SMEM)] + in_vmem(1),
        out_shape=[jax.ShapeDtypeStruct(shape, F32) for shape in shapes],
        scratch_shapes=[pltpu.VMEM((sum(heights), LANE), F32)],
        compiler_params=params(16),
        name="finish",
        cost_estimate=cost(2),
    )(sc, got)


def local(
    tokens, ln1_gain, ln1_shift, qkv_weight, qkv_bias, out_weight, out_bias, ln2_gain, ln2_shift,
    up_weight, up_bias, down_weight, down_bias, seq_lengths, span_order, cotangent,
):
    nf = lax.axis_size("fsdp")
    nc = lax.axis_size("ctx")
    x, c = tokens[0], cotangent[0]
    spans = x.shape[0] // SPAN
    seqs = seq_lengths.shape[1]
    weights = packed_params(
        qkv_weight, out_weight,
        (ln1_gain, ln1_shift, qkv_bias, out_bias, ln2_gain, ln2_shift, up_bias, down_bias),
    )
    scalars = jnp.concatenate(
        [
            lax.axis_index("fsdp").reshape(1),
            lax.axis_index("ctx").reshape(1),
            (lax.axis_index("ctx") * spans).reshape(1),
            seq_lengths[0],
            span_order[0],
        ]
    ).astype(jnp.int32)
    far_weights = first_gather(weights, "fsdp")
    sums = span_sums(x, nc)
    nsum = lax.all_to_all(sums, "ctx", 0, 0, tiled=True).reshape(nc * spans, D)
    far_weights = after(far_weights, nsum)
    weights = gathered(weights, far_weights, "fsdp")
    up_weight = after(up_weight, far_weights)
    far_up = first_gather(up_weight, "fsdp")
    down_weight = after(down_weight, far_weights)
    far_down = first_gather(down_weight, "fsdp")

    packed, p, att, h1, wqkv, wout, vec, tabs = attend(
        scalars, x, span_order, nsum, weights, seqs
    )
    up = gathered(up_weight, after(far_up, att), "fsdp")
    r1, h2 = proj(x, att, wout, vec)
    g, gp, wup = ffn_up(scalars, h2, vec, up)
    dsend, dkeep = down_gradient(scalars, g, c, nf)
    down = gathered(down_weight, after(far_down, dkeep), "fsdp")
    dh2, dub, usend, ukeep = ffn_down(scalars, h2, c, gp, wup, down)
    bits = ctx_bits()
    near = [("fsdp", 1 << k) for k in range(1, nf.bit_length() - 1)]

    seq = Sequence()
    from_down = Part(scalars, seq, dkeep, dsend)
    from_down.step(*near[0])
    dr1, da, gout, gvec = mid(c, seq.next(dh2), r1, att, wout, vec)
    seq.made(da)
    from_up = Part(scalars, seq, ukeep, usend)
    from_up.step("ctx", bits[0])
    da = seq.next(da)
    fixed = (x, da, h1, packed, p, tabs, wqkv, vec, nsum)
    dh1, sums, fsend0, fkeep0, send, keep = back(scalars, fixed, (gout,), 0, nf, nc)
    seq.made(dh1)
    first = Part(scalars, seq, keep, send)
    from_down.step("ctx", bits[0])
    from_up.step(*near[0])
    dh1 = seq.next(dh1)
    upper, *old = back(scalars, fixed, (dub, gvec, dh1, sums), 1, nf, nc, last=False)
    seq.made(old[0])
    first.step(*near[0])
    feed = Union(scalars, seq, [from_down, from_up])
    old[0] = seq.next(old[0])
    lower, _, fsend1, fkeep1, send, keep = back(
        scalars, fixed, (dub, gvec, dh1, sums), 1, nf, nc, old=old
    )
    seq.made(lower)
    second = Part(scalars, seq, keep, send)
    far = [(k, swap(t, "ctx", bits[0])) for k, t in ((fkeep0, fsend0), (fkeep1, fsend1))]
    while feed.more():
        feed.step(FILL)
    first.step("ctx", bits[0], FILL)
    second.step(*near[0])
    mixed = block_output(scalars, seq.next(r1), g, vec, down)
    seq.made(mixed, *(got for _, got in far))
    second.step("ctx", bits[0])
    feed.end()
    rest = Union(scalars, seq, [first, second], far)
    feed.join()
    while rest.more():
        rest.step()
    while feed.at > 1:
        feed.join()
    own_span = rest.end()
    feed.join()
    tokens_grad = first_back(seq.next(x), dr1, upper, lower, own_span, wqkv, vec)
    seq.made(tokens_grad)
    while rest.gathering():
        rest.join()
    block = D // nf
    height, width = down_weight.shape[0], up_weight.shape[1]
    heights = (from_down.total, from_up.total)
    grad_down, grad_up = finish(
        scalars,
        feed.rows(),
        heights,
        [(height, D), (block, width)],
        [
            [height * j for j in range(D // LANE)],
            [heights[0] + block * j for j in range(width // LANE)],
        ],
    )
    seq.made(grad_down)
    half = PAIRS // 2
    plan = [
        [
            p // half * first.total + block * (t * half + p % half)
            for t in range(3)
            for p in range(PAIRS)
        ],
        [block * (3 * half + j) for j in range(D // LANE)],
    ]
    shapes = [(block, 3 * D), (block, D)]
    at = first.total + 3 * half * block
    for wide in (block, block, 3 * block, block, block, block, 4 * block, block):
        shapes.append((1, wide))
        plan.append([at + j for j in range(wide // LANE)])
        at += wide // LANE
    grad_qkv, grad_out, *vectors = finish(
        scalars, rest.rows(), (first.total, second.total), shapes, plan
    )
    g1, s1, qb, ob, g2, s2, ub, db = (v.reshape(-1) for v in vectors)
    return (
        mixed[None], tokens_grad[None], g1, s1, grad_qkv, qb, grad_out, ob, g2, s2,
        grad_up, ub, grad_down, db,
    )


def solution(mesh):
    rows, one, two = P("fsdp", "ctx", None), P("fsdp"), P("fsdp", None)
    return jax.shard_map(
        local,
        mesh=mesh,
        in_specs=(
            rows, one, one, two, one, two, one, one, one, two, one, two, one, two, two, rows,
        ),
        out_specs=(rows, rows, one, one, two, one, two, one, one, one, two, one, two, one),
        check_vma=False,
    )
```

```python
import functools

import jax
import jax.numpy as jnp
from jax import lax
from jax.experimental import pallas as pl
from jax.experimental.pallas import tpu as pltpu
from jax.sharding import PartitionSpec as P

D = 512
HEADS = 8
HEAD = 64
SPAN = 128
LANE = 128
PAIRS = D // LANE
ROWS = 256
EPSILON = 1e-05
MASKED = -1e30
SCALE = HEAD**-0.5
FILL = 6
INV_ROOT = SPAN**-0.5
F32 = jnp.float32
BF16 = jnp.bfloat16

G1, S1, OB, G2, S2, DB, QB, UB = range(8)
SC_F, SC_C, SC_SLOT, SC_LEN = range(4)


def dot(a, b):
    return lax.dot_general(a, b, (((1,), (0,)), ((), ())), preferred_element_type=F32)


def dot_bt(a, b):
    return lax.dot_general(a, b, (((1,), (1,)), ((), ())), preferred_element_type=F32)


def dot_at(a, b):
    return lax.dot_general(a, b, (((0,), (0,)), ((), ())), preferred_element_type=F32)


def normalize(values):
    centre = values - jnp.mean(values, axis=-1, keepdims=True)
    spread = jnp.mean(centre * centre, axis=-1, keepdims=True)
    rstd = lax.rsqrt(spread + EPSILON)
    return centre * rstd, rstd


def norm_back(e, n, rstd):
    return rstd * (
        e - jnp.mean(e, axis=-1, keepdims=True) - n * jnp.mean(e * n, axis=-1, keepdims=True)
    )


def params(mib):
    return pltpu.CompilerParams(vmem_limit_bytes=mib * 1024 * 1024)


def in_vmem(count):
    return [pl.BlockSpec(memory_space=pltpu.VMEM) for _ in range(count)]


def cost(micros):
    return pl.CostEstimate(
        flops=int(micros * 1e9), transcendentals=0, bytes_accessed=int(micros * 1e6)
    )


def resident(kernel, name, micros, mib, scalars, arrays, outs, scratch=()):
    return pl.pallas_call(
        kernel,
        in_specs=[pl.BlockSpec(memory_space=pltpu.SMEM)] * len(scalars) + in_vmem(len(arrays)),
        out_specs=in_vmem(len(outs)),
        out_shape=[jax.ShapeDtypeStruct(shape, dtype) for shape, dtype in outs],
        scratch_shapes=list(scratch),
        compiler_params=params(mib),
        name=name,
        cost_estimate=cost(micros),
    )(*scalars, *arrays)


def block_rows(i, size=ROWS):
    if isinstance(i, int):
        return slice(i * size, (i + 1) * size)
    return pl.ds(pl.multiple_of(i * size, size), size)


def each_block(rows, body, size=ROWS, parts=1):
    each = rows // size // parts
    if parts == 1:
        for i in range(each):
            body(i)
        return

    def step(n, carry):
        for k in range(each):
            body(n * each + k)
        return carry

    lax.fori_loop(0, parts, step, 0)


def sums_kernel(x_ref, o_ref):
    spans = x_ref.shape[0] // SPAN
    sums = []
    for s in range(spans):
        n, _ = normalize(x_ref[s * SPAN : (s + 1) * SPAN, :].astype(F32))
        sums.append(jnp.sum(n, axis=0, keepdims=True))
    table = jnp.concatenate(sums, axis=0)
    for k in range(o_ref.shape[0]):
        o_ref[k] = table


def span_sums(x, copies):
    spans = x.shape[0] // SPAN
    return resident(sums_kernel, "span_sums", 3, 16, (), (x,), [((copies, spans, D), F32)])[0]


def pack_kernel(qkv_ref, out_ref, *refs):
    o_ref = refs[-1]
    rows, width = qkv_ref.shape
    o_ref[:rows, :width] = qkv_ref[...]
    o_ref[:rows, width:] = out_ref[...]
    parts = [ref[...].astype(F32) for ref in refs[:-1]]
    used = sum(part.shape[0] for part in parts)
    parts.append(jnp.zeros((16 - used, LANE), F32))
    o_ref[rows:, :LANE] = jnp.concatenate(parts, axis=0).astype(BF16)
    o_ref[rows:, LANE:] = jnp.zeros((16, o_ref.shape[1] - LANE), BF16)


def packed_params(qkv, out, vectors):
    shape = (qkv.shape[0] + 16, qkv.shape[1] + out.shape[1])
    vectors = [v.reshape(-1, LANE) for v in vectors]
    arrays = [qkv, out] + vectors
    return pl.pallas_call(
        pack_kernel,
        out_shape=jax.ShapeDtypeStruct(shape, BF16),
        compiler_params=params(58),
        name="pack",
        cost_estimate=cost(1),
    )(*arrays)


def attend_kernel(sc, x_ref, order_ref, nsum_ref, *refs, nf, seqs):
    param_refs = refs[:nf]
    (packed_ref, p_ref, att_ref, h1_ref, wqkv, wout, vec, tabs) = refs[nf:]
    nspan = nsum_ref.shape[0]
    block = D // nf

    vec[...] = jnp.zeros_like(vec)
    for q in range(nf):
        fq = sc[SC_F] ^ q
        at = pl.ds(pl.multiple_of(fq * block, block), block)
        wqkv[at, :] = param_refs[q][:block, : 3 * D]
        wout[at, :] = param_refs[q][:block, 3 * D :]
        sm = param_refs[q][block:, :LANE].astype(F32)
        for row, src in ((G1, 0), (S1, 1), (OB, 5), (G2, 6), (S2, 7), (DB, 12)):
            vec[row : row + 1, at] = sm[src : src + 1]
        for t in range(3):
            at3 = pl.ds(pl.multiple_of(fq * 3 * block + t * block, block), block)
            vec[QB : QB + 1, at3] = sm[2 + t : 3 + t]
        for t in range(4):
            at4 = pl.ds(pl.multiple_of(fq * 4 * block + t * block, block), block)
            vec[UB : UB + 1, at4] = sm[8 + t : 9 + t]
    hs = nsum_ref[...] * vec[G1 : G1 + 1, :D] + SPAN * vec[S1 : S1 + 1, :D]
    hi = hs.astype(BF16)
    lo = (hs - hi.astype(F32)).astype(BF16)
    both = dot(jnp.concatenate([hi, lo], axis=0), wqkv[:, D:])
    t = both[:nspan] + both[nspan:] + SPAN * vec[QB : QB + 1, D : 3 * D]
    tabs[...] = (t * INV_ROOT).astype(BF16)
    prompt = lax.div(sc[SC_LEN], SPAN)
    spans = ROWS // SPAN

    def body(i):
        rows = block_rows(i)
        n1, _ = normalize(x_ref[rows, :].astype(F32))
        h1 = (n1 * vec[G1 : G1 + 1, :D] + vec[S1 : S1 + 1, :D]).astype(BF16)
        h1_ref[rows, :] = h1
        packed_ref[rows, :] = (dot(h1, wqkv[...]) + vec[QB : QB + 1, : 3 * D]).astype(BF16)

        lane = lax.broadcasted_iota(jnp.int32, (SPAN, LANE), 1)
        low = lane < HEAD
        causal = jnp.where(
            lane <= lax.broadcasted_iota(jnp.int32, (SPAN, LANE), 0), 0.0, MASKED
        ).astype(F32)
        order = order_ref[...]
        for s in range(spans):
            a = sc[SC_LEN + seqs + sc[SC_SLOT] + i * spans + s]
            start, begin = 0, 0
            for k in range(seqs):
                begin = jnp.where(start <= a, start, begin)
                start = start + lax.div(sc[SC_LEN + k], SPAN)
            seen = (order < a) & ((order >= begin) | (order < prompt))
            far = jnp.where(seen, 0.0, MASKED).astype(F32)
            bias = jnp.concatenate([causal, jnp.broadcast_to(far, (SPAN, nspan))], axis=1)
            bias = jnp.concatenate([bias, bias], axis=0)
            at = block_rows(i * spans + s, SPAN)
            for p in range(PAIRS):
                cq, ck, cv = (slice(t * D + p * LANE, t * D + (p + 1) * LANE) for t in range(3))
                q = packed_ref[at, cq] * SCALE
                zero = jnp.zeros_like(q)
                q2 = jnp.concatenate([jnp.where(low, q, zero), jnp.where(low, zero, q)], axis=0)
                kc = jnp.concatenate([packed_ref[at, ck], tabs[:, cq]], axis=0)
                vc = jnp.concatenate([packed_ref[at, cv], tabs[:, ck]], axis=0)
                scores = dot_bt(q2, kc) + bias
                peak = jnp.max(scores, axis=1, keepdims=True)
                e = jnp.exp(scores - peak)
                w = (e * (1.0 / jnp.sum(e, axis=1, keepdims=True))).astype(BF16)
                p_ref[(i * spans + s) * PAIRS + p, :SPAN] = w[:, :SPAN].T
                p_ref[(i * spans + s) * PAIRS + p, SPAN:] = w[:, SPAN:].T
                o2 = dot(w, vc)
                att_ref[at, cq] = jnp.where(low, o2[:SPAN], o2[SPAN:]).astype(BF16)

    each_block(x_ref.shape[0], body, parts=2)


def proj_kernel(x_ref, att_ref, wout, vec, r1_ref, h2_ref):
    def body(i):
        at = block_rows(i)
        r1 = x_ref[at, :].astype(F32) + (dot(att_ref[at, :], wout[...]) + vec[OB : OB + 1, :D])
        r1_ref[at, :] = r1
        n2, _ = normalize(r1)
        h2_ref[at, :] = (n2 * vec[G2 : G2 + 1, :D] + vec[S2 : S2 + 1, :D]).astype(BF16)

    each_block(x_ref.shape[0], body)


def proj(x, att, wout, vec):
    outs = [(x.shape, F32), (x.shape, BF16)]
    return resident(proj_kernel, "proj", 3, 8, (), (x, att, wout, vec), outs)


def attend(sc, x, order, nsum, weights, seqs):
    rows = x.shape[0]
    nspan = nsum.shape[0]
    outs = [
        ((rows, 3 * D), BF16),
        ((rows // SPAN * PAIRS, SPAN + nspan, 2 * SPAN), BF16),
        ((rows, D), BF16),
        ((rows, D), BF16),
        ((D, 3 * D), BF16),
        ((D, D), BF16),
        ((8, 4 * D), F32),
        ((nspan, 2 * D), BF16),
    ]
    kernel = functools.partial(attend_kernel, nf=len(weights), seqs=seqs)
    arrays = (x, order, nsum, *weights)
    return resident(kernel, "attend", 12, 12, (sc,), arrays, outs)


def relative(step, nf):
    half = nf // 2
    return jnp.where(step < half, 2 * step + 1, 2 * (step - half))


def up_kernel(sc, h2_ref, vec_ref, *refs, nf):
    up_refs = refs[:nf]
    g_ref, gp_ref, w_ref = refs[nf:]
    block = D // nf
    width = w_ref.shape[1] // nf
    k0 = 0.7978845608028654
    for q in range(nf):
        at = pl.ds(pl.multiple_of((sc[SC_F] ^ q) * block, block), block)
        w_ref[at, :] = up_refs[q][...]
    rows = h2_ref.shape[0]

    def body(j):
        cols = pl.ds(pl.multiple_of(j * width, width), width)
        for i in range(rows // ROWS):
            at = block_rows(i)
            u = dot(h2_ref[at, :], w_ref[:, cols]) + vec_ref[UB : UB + 1, cols]
            u2 = u * u
            t = jnp.tanh(u * (k0 + (k0 * 0.044715) * u2))
            half = 0.5 + 0.5 * t
            g_ref[at, cols] = (u * half).astype(BF16)
            slope = u * (k0 + (3 * k0 * 0.044715) * u2)
            gp_ref[at, cols] = (half + (0.5 - 0.5 * t * t) * slope).astype(BF16)

    each_block(nf, body, 1, parts=2)


def ffn_up(sc, h2, vec, up):
    rows, ff = h2.shape[0], up[0].shape[1]
    outs = [((rows, ff), BF16), ((rows, ff), BF16), ((D, ff), BF16)]
    kernel = functools.partial(up_kernel, nf=len(up))
    return resident(kernel, "ffn_up", 8, 12, (sc,), (h2, vec, *up), outs)


def down_grad_kernel(sc, g_ref, c_ref, send_ref, keep_ref, *, nf):
    width = g_ref.shape[1] // nf
    for q in range(nf):
        at = pl.ds(pl.multiple_of((sc[SC_F] ^ q) * width, width), width)
        grad = dot_at(g_ref[:, at], c_ref[...]).astype(BF16)
        ref = send_ref if q % 2 else keep_ref
        for j in range(D // LANE):
            ref[q // 2, j * width : (j + 1) * width, :] = grad[:, j * LANE : (j + 1) * LANE]


def down_gradient(sc, g, c, nf):
    piece = g.shape[1] // nf * D // LANE
    outs = [((nf // 2, piece, LANE), BF16)] * 2
    kernel = functools.partial(down_grad_kernel, nf=nf)
    return resident(kernel, "down_grad", 4, 12, (sc,), (g, c), outs)


def down_kernel(sc, h2_ref, c_ref, gp_ref, w_ref, *refs, nf):
    down_refs = refs[:nf]
    dh2_ref, dub_ref, send_ref, keep_ref, du_ref, grad_ref = refs[nf:]
    width = w_ref.shape[1] // nf
    block = D // nf
    rows = h2_ref.shape[0]
    for s in range(nf):
        f = sc[SC_F] ^ s
        cols = pl.ds(pl.multiple_of(f * width, width), width)
        dub_ref[:, cols] = jnp.zeros((1, width), F32)

        def body(i):
            at = block_rows(i, 2 * ROWS)
            dg = dot_bt(c_ref[at, :], down_refs[s][...])
            du = (dg * gp_ref[at, cols].astype(F32)).astype(BF16)
            du_ref[at, :] = du
            dub_ref[:, cols] += jnp.sum(du.astype(F32), axis=0, keepdims=True)
            dh2 = dot_bt(du, w_ref[:, cols])
            if s == 0:
                dh2_ref[at, :] = dh2
            else:
                dh2_ref[at, :] += dh2

        each_block(rows, body, 2 * ROWS)
        grad_ref[...] = dot_at(h2_ref[...], du_ref[...])
        for q in range(nf):
            ref = send_ref if q % 2 else keep_ref
            piece = grad_ref[pl.ds(pl.multiple_of((sc[SC_F] ^ q) * block, block), block), :]
            piece = piece.astype(BF16)
            for j in range(width // LANE):
                to = pl.multiple_of((f * (width // LANE) + j) * block, block)
                ref[q // 2, pl.ds(to, block), :] = piece[:, j * LANE : (j + 1) * LANE]


def ffn_down(sc, h2, c, gp, w, down):
    nf = len(down)
    rows = h2.shape[0]
    ff = w.shape[1]
    piece = ff // LANE * (D // nf)
    outs = [((rows, D), F32), ((1, ff), F32)] + [((nf // 2, piece, LANE), BF16)] * 2
    scratch = [pltpu.VMEM((rows, ff // nf), BF16), pltpu.VMEM((D, ff // nf), F32)]
    kernel = functools.partial(down_kernel, nf=nf)
    arrays = (h2, c, gp, w, *down)
    return resident(kernel, "ffn_down", 8, 14, (sc,), arrays, outs, scratch)


def mid_kernel(c_ref, dh2_ref, r1_ref, att_ref, wout, vec, dr1_ref, da_ref, gout_ref, gvec_ref):
    gout_ref[...] = jnp.zeros_like(gout_ref)
    gvec_ref[...] = jnp.zeros_like(gvec_ref)

    def add(row, values):
        gvec_ref[row : row + 1, :] += jnp.sum(values, axis=0, keepdims=True)

    def body(i):
        at = block_rows(i)
        c = c_ref[at, :].astype(F32)
        dh2 = dh2_ref[at, :]
        n2, rstd2 = normalize(r1_ref[at, :])
        add(G2, dh2 * n2)
        add(S2, dh2)
        add(DB, c)
        dr1 = c + norm_back(dh2 * vec[G2 : G2 + 1, :D], n2, rstd2)
        dr1_ref[at, :] = dr1
        dy = dr1.astype(BF16)
        add(OB, dy.astype(F32))
        gout_ref[...] += dot_at(att_ref[at, :], dy)
        da_ref[at, :] = dot_bt(dy, wout[...]).astype(BF16)

    each_block(c_ref.shape[0], body)


def mid(c, dh2, r1, att, wout, vec):
    rows = c.shape[0]
    outs = [((rows, D), F32), ((rows, D), BF16), ((D, D), F32), ((8, D), F32)]
    return resident(mid_kernel, "mid", 5, 12, (), (c, dh2, r1, att, wout, vec), outs)


def piece_rows(used, parts):
    return -(-used // (16 * parts)) * 16 * parts


def columns_of(half):
    wide = PAIRS // 2 * LANE
    return [slice(t * D + half * wide, t * D + (half + 1) * wide) for t in range(3)]


def back_kernel(sc, x_ref, da_ref, h1_ref, packed_ref, p_ref, tabs, wqkv, vec, nsum_ref, *refs, nf, copies, half, first, last):
    if half:
        (dub_ref, gvec_ref, before_ref, sums_ref), refs = refs[:4], refs[4:]
    else:
        (gout_ref,), refs = refs[:1], refs[1:]
    olds, refs = ((), refs) if first else (refs[:3], refs[3:])
    (dh1_ref, acc, acc_span, accv), refs = refs[:4], refs[4:]
    if last:
        (sum_ref, far_send, far_keep, send_ref, keep_ref), refs = refs[:5], refs[5:]
    (dp_ref,) = refs
    wide = PAIRS // 2 * LANE
    columns = columns_of(half)
    for k, ref in enumerate((acc, acc_span, accv)):
        ref[...] = jnp.zeros_like(ref) if first else olds[k][...]

    def add(row, values):
        accv[row : row + 1, : values.shape[1]] += jnp.sum(values, axis=0, keepdims=True)

    def body(i):
        rows = block_rows(i)
        low = lax.broadcasted_iota(jnp.int32, (SPAN, LANE), 1) < HEAD
        for s in range(ROWS // SPAN):
            at = block_rows(i * (ROWS // SPAN) + s, SPAN)
            to = slice(s * SPAN, (s + 1) * SPAN)
            for k in range(PAIRS // 2):
                p = half * (PAIRS // 2) + k
                cq, ck, cv = (slice(t * D + p * LANE, t * D + (p + 1) * LANE) for t in range(3))
                oq, ok, ov = (slice(t * wide + k * LANE, t * wide + (k + 1) * LANE) for t in range(3))
                q = packed_ref[at, cq] * SCALE
                do = da_ref[at, cq]
                zero = jnp.zeros_like(q)
                q2 = jnp.concatenate([jnp.where(low, q, zero), jnp.where(low, zero, q)], axis=0)
                do2 = jnp.concatenate([jnp.where(low, do, zero), jnp.where(low, zero, do)], axis=0)
                kc = jnp.concatenate([packed_ref[at, ck], tabs[:, cq]], axis=0)
                vc = jnp.concatenate([packed_ref[at, cv], tabs[:, ck]], axis=0)
                w = p_ref[(i * (ROWS // SPAN) + s) * PAIRS + p]
                wf = w.astype(F32)
                dp = dot_bt(vc, do2)
                delta = jnp.sum(wf * dp, axis=0, keepdims=True)
                ds = (wf * (dp - delta)).astype(BF16)
                dq2 = dot_at(ds, kc)
                dq = jnp.where(low, dq2[:SPAN], dq2[SPAN:]) * SCALE
                dk = dot(ds, q2)
                dv = dot(w, do2)
                acc_span[:, oq] += dk[SPAN:]
                acc_span[:, ok] += dv[SPAN:]
                dp_ref[to, oq] = dq.astype(BF16)
                dp_ref[to, ok] = dk[:SPAN].astype(BF16)
                dp_ref[to, ov] = dv[:SPAN].astype(BF16)
        dpk = dp_ref[...]
        add(QB, dpk.astype(F32))
        acc[...] += dot_at(h1_ref[rows, :], dpk)
        dh1 = dot_bt(dpk[:, :wide], wqkv[:, columns[0]])
        for t in (1, 2):
            dh1 = dh1 + dot_bt(dpk[:, t * wide : (t + 1) * wide], wqkv[:, columns[t]])
        if half:
            dh1 = dh1 + before_ref[rows, :]
            n1, _ = normalize(x_ref[rows, :].astype(F32))
            add(G1, dh1 * n1)
            add(S1, dh1)
        dh1_ref[block_rows(i - start), :] = dh1

    blocks = dh1_ref.shape[0] // ROWS
    start = 0 if first else x_ref.shape[0] // ROWS - blocks
    each_block(blocks * ROWS, lambda i: body(i + start), parts=max(blocks // 2, 1))
    if not last:
        return

    span = acc_span[...]
    bit = sc[SC_C] & 1
    each = span.shape[0] // copies
    for k in range(copies):
        code = code_of(k, copies)
        part = span[k * each : (k + 1) * each]
        hold = jnp.concatenate(
            [part[:, t * LANE : (t + 1) * LANE] for t in range(2 * wide // LANE)], axis=0
        ).astype(BF16)
        to = slice(code % (copies // 2) * hold.shape[0], (code % (copies // 2) + 1) * hold.shape[0])
        mine = bit == code // (copies // 2)

        @pl.when(mine)
        def _():
            far_keep[to, :] = hold

        @pl.when(jnp.logical_not(mine))
        def _():
            far_send[to, :] = hold

    span = span * INV_ROOT
    low_span = span.astype(BF16)
    nsum = nsum_ref[...]
    hs = (nsum * vec[G1 : G1 + 1, :D] + SPAN * vec[S1 : S1 + 1, :D]).astype(BF16)
    acc[:, wide:] += dot_at(hs, low_span)
    accv[QB : QB + 1, wide : 3 * wide] += SPAN * jnp.sum(span, axis=0, keepdims=True)
    de = dot_bt(low_span[:, :wide], wqkv[:, columns[1]])
    de = de + dot_bt(low_span[:, wide:], wqkv[:, columns[2]])
    block = D // nf
    if half:
        de = de + sums_ref[: de.shape[0], :]
        add(G1, de * nsum)
        accv[S1 : S1 + 1, :D] += SPAN * jnp.sum(de, axis=0, keepdims=True)
        bias = sums_ref[de.shape[0] : de.shape[0] + 8, :]
    else:
        sum_ref[: de.shape[0], :] = de
        tail = [accv[QB : QB + 1, t * wide : (t + 1) * wide] for t in range(3)]
        bias = jnp.concatenate(tail + [jnp.zeros((5, wide), F32)], axis=0)
        sum_ref[de.shape[0] : de.shape[0] + 8, :] = jnp.concatenate([bias, bias], axis=1)

    for q in range(nf):
        ref = send_ref if q % 2 else keep_ref
        fq = sc[SC_F] ^ q
        at = pl.ds(pl.multiple_of(fq * block, block), block)
        base = 0
        pieces = [acc[at, :].astype(BF16)]
        if not half:
            pieces.append(gout_ref[at, :].astype(BF16))
        for piece in pieces:
            for j in range(piece.shape[1] // LANE):
                ref[q // 2, base : base + block, :] = piece[:, j * LANE : (j + 1) * LANE]
                base += block
        if half:
            whole = jnp.concatenate(
                [
                    part
                    for t in range(3)
                    for part in (bias[t : t + 1, :wide], accv[QB : QB + 1, t * wide : (t + 1) * wide])
                ],
                axis=1,
            )
            accv[QB + 1 : QB + 2, : 3 * D] = whole
            three = [
                accv[QB + 1 : QB + 2, pl.ds(pl.multiple_of((fq * 3 + t) * block, block), block)]
                for t in range(3)
            ]
            four = [
                dub_ref[0:1, pl.ds(pl.multiple_of((fq * 4 + t) * block, block), block)]
                for t in range(4)
            ]
            small = jnp.concatenate(
                [accv[G1 : G1 + 1, at], accv[S1 : S1 + 1, at]]
                + three
                + [gvec_ref[OB : OB + 1, at], gvec_ref[G2 : G2 + 1, at], gvec_ref[S2 : S2 + 1, at]]
                + four
                + [gvec_ref[DB : DB + 1, at], jnp.zeros((3, LANE), F32)],
                axis=0,
            ).astype(BF16)
            ref[q // 2, base : base + 16, :] = small
            base += 16
        left = ref.shape[1] - base
        if left:
            ref[q // 2, base:, :] = jnp.zeros((left, LANE), BF16)


def back(sc, fixed, more, half, nf, copies, old=None, last=True):
    x, nsum = fixed[0], fixed[-1]
    rows = x.shape[0] if last and old is None else x.shape[0] // 2
    nspan = nsum.shape[0]
    wide = PAIRS // 2 * LANE
    block = D // nf
    used = 3 * wide // LANE * block + (16 if half else D // LANE * block)
    piece = piece_rows(used, copies)
    far = nspan // 2 * 2 * wide // LANE
    sums = [((D, 3 * wide), F32), ((nspan, 2 * wide), F32), ((16, 3 * D), F32)]
    outs = [((rows, D), F32)]
    scratch = [pltpu.VMEM((ROWS, 3 * wide), BF16)]
    if last:
        scratch = [pltpu.VMEM(*a) for a in sums] + scratch
        outs += [((nspan + 8, D), F32)]
        outs += [((far, LANE), BF16)] * 2 + [((nf // 2, piece, LANE), BF16)] * 2
    else:
        outs += sums
    kernel = functools.partial(
        back_kernel, nf=nf, copies=copies, half=half, first=old is None, last=last
    )

    def ordered(*refs):
        if not last:
            return kernel(*refs)
        at = len(refs) - len(scratch)
        return kernel(
            *refs[: at - len(outs) + 1], *refs[at:-1], *refs[at - len(outs) + 1 : at], refs[-1]
        )

    arrays = (*fixed, *more, *(old or ()))
    return resident(ordered, f"back_{half}", 9, 18, (sc,), arrays, outs, scratch)


def first_kernel(x_ref, dr1_ref, upper_ref, lower_ref, own_ref, wqkv, vec, o_ref, e_ref):
    i = pl.program_id(0)
    spans = ROWS // SPAN

    @pl.when(i == 0)
    def _():
        each = e_ref.shape[0]
        wide = PAIRS // 2 * LANE
        total = jnp.zeros((each, D), F32)
        for half in range(2):
            for k, columns in enumerate(columns_of(half)[1:]):
                for t in range(wide // LANE):
                    row = ((half * 2 + k) * (wide // LANE) + t) * each
                    own = own_ref[row : row + each, :].astype(F32) * INV_ROOT
                    cols = slice(columns.start + t * LANE, columns.start + (t + 1) * LANE)
                    total = total + dot_bt(own.astype(BF16), wqkv[:, cols])
        e_ref[...] = total

    at = block_rows(i)
    n1, rstd1 = normalize(x_ref[at, :].astype(F32))
    extra = jnp.concatenate(
        [jnp.broadcast_to(e_ref[pl.ds(i * spans + s, 1), :], (SPAN, D)) for s in range(spans)],
        axis=0,
    )
    half = pl.num_programs(0) // 2

    def write(ref, k):
        dh1 = ref[block_rows(k), :] + extra
        o_ref[...] = dr1_ref[at, :] + norm_back(dh1 * vec[G1 : G1 + 1, :D], n1, rstd1)

    @pl.when(i < half)
    def _():
        write(upper_ref, i)

    @pl.when(i >= half)
    def _():
        write(lower_ref, i - half)


def first_back(x, dr1, upper, lower, own, wqkv, vec):
    rows = x.shape[0]
    return pl.pallas_call(
        first_kernel,
        grid=(rows // ROWS,),
        in_specs=in_vmem(7),
        out_specs=pl.BlockSpec((ROWS, D), lambda i: (i, 0)),
        out_shape=jax.ShapeDtypeStruct((rows, D), F32),
        scratch_shapes=[pltpu.VMEM((rows // SPAN, D), F32)],
        compiler_params=params(8),
        name="first_back",
        cost_estimate=cost(3),
    )(x, dr1, upper, lower, own, wqkv, vec)


def mixed_kernel(sc, r1_ref, g_ref, vec, *refs):
    w_refs, o_ref = refs[:-1], refs[-1]
    at = block_rows(pl.program_id(0))
    total = r1_ref[at, :] + vec[DB : DB + 1, :D]
    width = w_refs[0].shape[0]
    for q, w_ref in enumerate(w_refs):
        cols = pl.ds(pl.multiple_of((sc[SC_F] ^ q) * width, width), width)
        total = total + dot(g_ref[at, cols], w_ref[...])
    o_ref[...] = total.astype(BF16)


def block_output(sc, r1, g, vec, down):
    rows = r1.shape[0]
    return pl.pallas_call(
        mixed_kernel,
        grid=(rows // ROWS,),
        in_specs=[pl.BlockSpec(memory_space=pltpu.SMEM)] + in_vmem(3 + len(down)),
        out_specs=pl.BlockSpec((ROWS, D), lambda i: (i, 0)),
        out_shape=jax.ShapeDtypeStruct((rows, D), BF16),
        compiler_params=params(8),
        name="block_output",
        cost_estimate=cost(4),
    )(sc, r1, g, vec, *down)


def swap(array, axis, bit):
    n = lax.axis_size(axis)
    return lax.ppermute(array, axis, [(k, k ^ bit) for k in range(n)])


def after(array, *others):
    return lax.optimization_barrier((array, others))[0]


def first_gather(array, axis):
    return swap(array, axis, lax.axis_size(axis) // 2)


def gathered(array, far, axis):
    n = lax.axis_size(axis)
    bit = n // 2
    held = {0: array, bit: far}
    bit //= 2
    while bit:
        for r in sorted(held):
            held[r ^ bit] = swap(held[r], axis, bit)
        bit //= 2
    return [held[r] for r in range(n)]


def total_of(values):
    total = values[0].astype(F32)
    for value in values[1:]:
        total = total + value.astype(F32)
    return total.astype(BF16)


def fold_kernel(sc, *refs, bit, counts):
    own = lax.div(sc[SC_C], bit) & 1 if bit else 0
    arrays, (send_ref, own_ref) = refs[:-2], refs[-2:]
    at = 0
    for count in counts:
        group, arrays = arrays[:count], arrays[count:]
        a, _, h, _ = group[0].shape
        for ref, half in ((send_ref, 1 - own), (own_ref, own)):
            for k in range(a):
                ref[k, at : at + h, :] = total_of([g[k, half] for g in group])
        at += h


def fold(sc, bit, *groups, micros=1):
    a = groups[0][0].shape[0]
    h = sum(group[0].shape[2] for group in groups)
    arrays = [array for group in groups for array in group]
    counts = tuple(len(group) for group in groups)
    kernel = functools.partial(fold_kernel, bit=bit, counts=counts)
    return resident(kernel, "fold", micros, 8, (sc,), arrays, [((a, h, LANE), BF16)] * 2)


def quad_kernel(sc, keep_ref, got_ref, *refs, bit):
    along, (own_ref, ctx_ref, near_ref, both_ref) = refs[:-4], refs[-4:]
    own = lax.div(sc[SC_C], bit) & 1
    for ref, x in ((own_ref, own), (ctx_ref, 1 - own)):
        at = keep_ref.shape[2]
        ref[:at, :] = total_of((keep_ref[0, x], got_ref[0, x]))
        for array in along[0::2] if ref is own_ref else along[1::2]:
            ref[at : at + array.shape[0], :] = array[...]
            at += array.shape[0]
    near_ref[...] = total_of((keep_ref[1, own], got_ref[1, own]))
    both_ref[...] = total_of((keep_ref[1, 1 - own], got_ref[1, 1 - own]))


def quad(sc, bit, keep, got, along):
    kernel = functools.partial(quad_kernel, bit=bit)
    arrays = (keep, got, *(a for pair in along for a in pair))
    h = keep.shape[2]
    rows = h + sum(kept.shape[0] for kept, _ in along)
    outs = [((n, LANE), BF16) for n in (rows, rows, h, h)]
    return resident(kernel, "quad", 1, 8, (sc,), arrays, outs)


def swap_both(array, ctx_bit, near_bit):
    n, nf = lax.axis_size("ctx"), lax.axis_size("fsdp")
    pairs = [
        (a * nf + b, (a ^ ctx_bit) * nf + (b ^ near_bit)) for a in range(n) for b in range(nf)
    ]
    return lax.ppermute(array, ("ctx", "fsdp"), pairs)


def refold_kernel(sc, *refs, bit, sizes, whole):
    arrays, (send_ref, own_ref) = refs[:-2], refs[-2:]
    own = lax.div(sc[SC_C], bit) & 1
    at = 0
    for n, h in enumerate(sizes):
        group = arrays if n == 0 else arrays[:whole]
        for ref, half in ((send_ref, 1 - own), (own_ref, own)):
            rows = pl.ds(pl.multiple_of(2 * at + half * h, 16), h)
            ref[at : at + h, :] = total_of([g[rows, :] for g in group])
        at += h


def refold(sc, bit, arrays, sizes, micros=1, whole=2):
    outs = [((sum(sizes), LANE), BF16)] * 2
    kernel = functools.partial(refold_kernel, bit=bit, sizes=sizes, whole=whole)
    return resident(kernel, "fold", micros, 8, (sc,), arrays, outs)


def last_kernel(keep_ref, got_ref, o_ref, *rest):
    used = o_ref.shape[0]
    total = keep_ref[:used, :].astype(F32) + got_ref[:used, :].astype(F32)
    o_ref[...] = total.astype(BF16)
    for ref in rest:
        total = keep_ref[used:, :].astype(F32) + got_ref[used:, :].astype(F32)
        ref[...] = total.astype(BF16)


def last_sum(keep, got, used):
    outs = [((used, LANE), BF16)]
    if used < keep.shape[0]:
        outs.append(((keep.shape[0] - used, LANE), BF16))
    return resident(last_kernel, "last", 1, 8, (), (keep, got), outs)


class Sequence:
    def __init__(self):
        self.last = ()

    def next(self, array):
        return after(array, *self.last) if self.last else array

    def made(self, *arrays):
        self.last = arrays


class Part:
    def __init__(self, sc, seq, keep, send):
        self.sc, self.seq, self.keep, self.send = sc, seq, keep, send
        self.count, self.rows = keep.shape[0], keep.shape[1]
        self.total = self.rows
        self.move("fsdp", 1)

    def move(self, axis, bit):
        self.gots = (swap(self.send, axis, bit),)

    def view(self, axis):
        if axis == "fsdp":
            self.count //= 2
            return 1, 2, self.count * self.rows, LANE
        self.rows //= 2
        return self.count, 2, self.rows, LANE

    def pair(self, axis):
        view = self.view(axis)
        return tuple(a.reshape(view) for a in (self.keep, *self.gots))

    def split(self, axis, bit, micros=1):
        keep, got = self.pair(axis)
        pair = (self.seq.next(keep), got)
        self.send, self.keep = fold(self.sc, bit if axis == "ctx" else 0, pair, micros=micros)
        self.seq.made(self.keep, self.send)

    def step(self, axis, bit, micros=1):
        self.split(axis, bit, micros)
        self.move(axis, bit)


def ctx_bits():
    n = lax.axis_size("ctx")
    return [1 << k for k in range(n.bit_length() - 1)]


def united(sc, seq, parts):
    groups = [part.pair("ctx") for part in parts]
    groups[0] = (seq.next(groups[0][0]), *groups[0][1:])
    sizes = [group[0].shape[2] for group in groups]
    return Union(sc, seq, [a[0] for a in fold(sc, ctx_bits()[1], *groups)], sizes, len(sizes))


class Union:
    def __init__(self, sc, seq, halves, sizes, few):
        self.sc, self.seq, self.sizes = sc, seq, sizes
        self.bits = ctx_bits()
        self.used = sum(sizes[:few]) * 2 // self.bits[-1]
        self.received(self.bits[1], *halves)
        self.at = 2

    def received(self, bit, send, keep):
        self.keep = keep
        self.seq.made(keep, send)
        self.got = swap(send, "ctx", bit)

    def more(self):
        return self.at < len(self.bits)

    def step(self, micros=1):
        bit = self.bits[self.at]
        self.at += 1
        self.sizes = [size // 2 for size in self.sizes]
        keep = self.seq.next(self.keep)
        self.received(bit, *refold(self.sc, bit, (keep, self.got), self.sizes, micros))

    def end(self):
        own, *rest = last_sum(self.seq.next(self.keep), self.got, self.used)
        self.received(self.bits[-1], own, own)
        self.at = len(self.bits) - 1
        return rest[0] if rest else None

    def gathering(self):
        return self.at > 0

    def join(self):
        both = jnp.concatenate([self.seq.next(self.keep), self.got], axis=0)
        self.at -= 1
        self.received(self.bits[self.at], both, both)

    def rows(self):
        both = jnp.concatenate([self.seq.next(self.keep), self.got], axis=0)
        return both.reshape(lax.axis_size("ctx"), -1, LANE)


def code_of(index, n):
    code = 0
    for k in range(n.bit_length() - 1):
        bit = index >> k if isinstance(index, int) else lax.div(index, 1 << k)
        code = 2 * code + (bit & 1)
    return code


def finish_kernel(sc, got_ref, *refs, heights, plan):
    outs, rows = refs[:-1], refs[-1]
    n = got_ref.shape[0]
    code = code_of(sc[SC_C], n)
    for k in range(n):
        at, base = 0, 0
        for height in heights:
            h = height // n
            to = pl.multiple_of(base + (code ^ k) * h, 16)
            rows[pl.ds(to, h), :] = got_ref[k, at : at + h, :].astype(F32)
            at, base = at + h, base + height
    for ref, places in zip(outs, plan):
        height = ref.shape[0]
        for j, place in enumerate(places):
            ref[:, j * LANE : (j + 1) * LANE] = rows[place : place + height, :]


def finish(sc, got, heights, shapes, plan):
    return pl.pallas_call(
        functools.partial(finish_kernel, heights=heights, plan=plan),
        in_specs=[pl.BlockSpec(memory_space=pltpu.SMEM)] + in_vmem(1),
        out_shape=[jax.ShapeDtypeStruct(shape, F32) for shape in shapes],
        scratch_shapes=[pltpu.VMEM((sum(heights), LANE), F32)],
        compiler_params=params(16),
        name="finish",
        cost_estimate=cost(2),
    )(sc, got)


def local(
    tokens, ln1_gain, ln1_shift, qkv_weight, qkv_bias, out_weight, out_bias, ln2_gain, ln2_shift,
    up_weight, up_bias, down_weight, down_bias, seq_lengths, span_order, cotangent,
):
    nf = lax.axis_size("fsdp")
    nc = lax.axis_size("ctx")
    x, c = tokens[0], cotangent[0]
    spans = x.shape[0] // SPAN
    seqs = seq_lengths.shape[1]
    weights = packed_params(
        qkv_weight, out_weight,
        (ln1_gain, ln1_shift, qkv_bias, out_bias, ln2_gain, ln2_shift, up_bias, down_bias),
    )
    scalars = jnp.concatenate(
        [
            lax.axis_index("fsdp").reshape(1),
            lax.axis_index("ctx").reshape(1),
            (lax.axis_index("ctx") * spans).reshape(1),
            seq_lengths[0],
            span_order[0],
        ]
    ).astype(jnp.int32)
    far_weights = first_gather(weights, "fsdp")
    sums = span_sums(x, nc)
    nsum = lax.all_to_all(sums, "ctx", 0, 0, tiled=True).reshape(nc * spans, D)
    far_weights = after(far_weights, nsum)
    weights = gathered(weights, far_weights, "fsdp")
    up_weight = after(up_weight, far_weights)
    far_up = first_gather(up_weight, "fsdp")
    down_weight = after(down_weight, far_weights)
    far_down = first_gather(down_weight, "fsdp")

    packed, p, att, h1, wqkv, wout, vec, tabs = attend(
        scalars, x, span_order, nsum, weights, seqs
    )
    up = gathered(up_weight, after(far_up, att), "fsdp")
    r1, h2 = proj(x, att, wout, vec)
    g, gp, wup = ffn_up(scalars, h2, vec, up)
    dsend, dkeep = down_gradient(scalars, g, c, nf)
    down = gathered(down_weight, after(far_down, dkeep), "fsdp")
    dh2, dub, usend, ukeep = ffn_down(scalars, h2, c, gp, wup, down)
    bits = ctx_bits()
    near = [("fsdp", 1 << k) for k in range(1, nf.bit_length() - 1)]

    seq = Sequence()
    from_down = Part(scalars, seq, dkeep, dsend)
    from_down.step(*near[0])
    dr1, da, gout, gvec = mid(c, seq.next(dh2), r1, att, wout, vec)
    seq.made(da)
    from_up = Part(scalars, seq, ukeep, usend)
    from_up.step("ctx", bits[0])
    da = seq.next(da)
    fixed = (x, da, h1, packed, p, tabs, wqkv, vec, nsum)
    dh1, sums, fsend0, fkeep0, send, keep = back(scalars, fixed, (gout,), 0, nf, nc)
    seq.made(dh1)
    first = Part(scalars, seq, keep, send)
    from_down.step("ctx", bits[0])
    from_up.step(*near[0])
    dh1 = seq.next(dh1)
    upper, *old = back(scalars, fixed, (dub, gvec, dh1, sums), 1, nf, nc, last=False)
    seq.made(old[0])
    first.step(*near[0])
    feed = united(scalars, seq, [from_down, from_up])
    old[0] = seq.next(old[0])
    lower, _, fsend1, fkeep1, send, keep = back(
        scalars, fixed, (dub, gvec, dh1, sums), 1, nf, nc, old=old
    )
    seq.made(lower)
    second = Part(scalars, seq, keep, send)
    while feed.more():
        feed.step(FILL)
    first.split("ctx", bits[0], FILL)
    along = ((first.keep[0], first.send[0]), (fkeep0, fsend0), (fkeep1, fsend1))
    view = (2, 2, second.rows // 2, LANE)
    keep, got = (a.reshape(view) for a in (second.keep, *second.gots))
    own, to_ctx, to_near, to_both = quad(scalars, bits[0], seq.next(keep), got, along)
    seq.made(own)
    arrays = (
        own,
        swap(to_ctx, "ctx", bits[0]),
        swap(to_near, *near[0]),
        swap_both(to_both, bits[0], near[0][1]),
    )
    mixed = block_output(scalars, seq.next(r1), g, vec, down)
    seq.made(mixed)
    feed.end()
    sizes = [second.total // 4] + [kept.shape[0] // 2 for kept, _ in along]
    arrays = (seq.next(arrays[0]), *arrays[1:])
    rest = Union(scalars, seq, refold(scalars, bits[1], arrays, sizes), sizes, 2)
    while feed.at > 1:
        feed.join()
    while rest.more():
        rest.step()
    feed.join()
    own_span = rest.end()
    rest.join()
    tokens_grad = first_back(seq.next(x), dr1, upper, lower, own_span, wqkv, vec)
    seq.made(tokens_grad)
    while rest.gathering():
        rest.join()
    block = D // nf
    height, width = down_weight.shape[0], up_weight.shape[1]
    heights = (from_down.total, from_up.total)
    grad_down, grad_up = finish(
        scalars,
        feed.rows(),
        heights,
        [(height, D), (block, width)],
        [
            [height * j for j in range(D // LANE)],
            [heights[0] + block * j for j in range(width // LANE)],
        ],
    )
    seq.made(grad_down)
    half = PAIRS // 2
    plan = [
        [
            (second.total if p < half else 0) + block * (t * half + p % half)
            for t in range(3)
            for p in range(PAIRS)
        ],
        [second.total + block * (3 * half + j) for j in range(D // LANE)],
    ]
    shapes = [(block, 3 * D), (block, D)]
    at = 3 * half * block
    for wide in (block, block, 3 * block, block, block, block, 4 * block, block):
        shapes.append((1, wide))
        plan.append([at + j for j in range(wide // LANE)])
        at += wide // LANE
    grad_qkv, grad_out, *vectors = finish(
        scalars, rest.rows(), (second.total, first.total), shapes, plan
    )
    g1, s1, qb, ob, g2, s2, ub, db = (v.reshape(-1) for v in vectors)
    return (
        mixed[None], tokens_grad[None], g1, s1, grad_qkv, qb, grad_out, ob, g2, s2,
        grad_up, ub, grad_down, db,
    )


def solution(mesh):
    rows, one, two = P("fsdp", "ctx", None), P("fsdp"), P("fsdp", None)
    return jax.shard_map(
        local,
        mesh=mesh,
        in_specs=(
            rows, one, one, two, one, two, one, one, one, two, one, two, one, two, two, rows,
        ),
        out_specs=(rows, rows, one, one, two, one, two, one, one, one, two, one, two, one),
        check_vma=False,
    )
```

```python
import functools

import jax
import jax.numpy as jnp
from jax import lax
from jax.experimental import pallas as pl
from jax.experimental.pallas import tpu as pltpu
from jax.sharding import PartitionSpec as P

D = 512
HEADS = 8
HEAD = 64
SPAN = 128
LANE = 128
PAIRS = D // LANE
ROWS = 256
EPSILON = 1e-05
MASKED = -1e30
SCALE = HEAD**-0.5
FILL = 3
INV_ROOT = SPAN**-0.5
F32 = jnp.float32
BF16 = jnp.bfloat16

G1, S1, OB, G2, S2, DB, QB, UB = range(8)
SC_F, SC_C, SC_SLOT, SC_LEN = range(4)


def dot(a, b):
    return lax.dot_general(a, b, (((1,), (0,)), ((), ())), preferred_element_type=F32)


def dot_bt(a, b):
    return lax.dot_general(a, b, (((1,), (1,)), ((), ())), preferred_element_type=F32)


def dot_at(a, b):
    return lax.dot_general(a, b, (((0,), (0,)), ((), ())), preferred_element_type=F32)


def normalize(values):
    centre = values - jnp.mean(values, axis=-1, keepdims=True)
    spread = jnp.mean(centre * centre, axis=-1, keepdims=True)
    rstd = lax.rsqrt(spread + EPSILON)
    return centre * rstd, rstd


def norm_back(e, n, rstd):
    return rstd * (
        e - jnp.mean(e, axis=-1, keepdims=True) - n * jnp.mean(e * n, axis=-1, keepdims=True)
    )


def params(mib):
    return pltpu.CompilerParams(vmem_limit_bytes=mib * 1024 * 1024)


def in_vmem(count):
    return [pl.BlockSpec(memory_space=pltpu.VMEM) for _ in range(count)]


def cost(micros):
    return pl.CostEstimate(
        flops=int(micros * 1e9), transcendentals=0, bytes_accessed=int(micros * 1e6)
    )


def resident(kernel, name, micros, mib, scalars, arrays, outs, scratch=()):
    return pl.pallas_call(
        kernel,
        in_specs=[pl.BlockSpec(memory_space=pltpu.SMEM)] * len(scalars) + in_vmem(len(arrays)),
        out_specs=in_vmem(len(outs)),
        out_shape=[jax.ShapeDtypeStruct(shape, dtype) for shape, dtype in outs],
        scratch_shapes=list(scratch),
        compiler_params=params(mib),
        name=name,
        cost_estimate=cost(micros),
    )(*scalars, *arrays)


def block_rows(i, size=ROWS):
    if isinstance(i, int):
        return slice(i * size, (i + 1) * size)
    return pl.ds(pl.multiple_of(i * size, size), size)


def each_block(rows, body, size=ROWS, parts=1):
    each = rows // size // parts
    if parts == 1:
        for i in range(each):
            body(i)
        return

    def step(n, carry):
        for k in range(each):
            body(n * each + k)
        return carry

    lax.fori_loop(0, parts, step, 0)


def sums_kernel(x_ref, o_ref):
    spans = x_ref.shape[0] // SPAN
    sums = []
    for s in range(spans):
        n, _ = normalize(x_ref[s * SPAN : (s + 1) * SPAN, :].astype(F32))
        sums.append(jnp.sum(n, axis=0, keepdims=True))
    table = jnp.concatenate(sums, axis=0)
    for k in range(o_ref.shape[0]):
        o_ref[k] = table


def span_sums(x, copies):
    spans = x.shape[0] // SPAN
    return resident(sums_kernel, "span_sums", 3, 16, (), (x,), [((copies, spans, D), F32)])[0]


def pack_kernel(qkv_ref, out_ref, *refs):
    o_ref = refs[-1]
    rows, width = qkv_ref.shape
    o_ref[:rows, :width] = qkv_ref[...]
    o_ref[:rows, width:] = out_ref[...]
    parts = [ref[...].astype(F32) for ref in refs[:-1]]
    used = sum(part.shape[0] for part in parts)
    parts.append(jnp.zeros((16 - used, LANE), F32))
    o_ref[rows:, :LANE] = jnp.concatenate(parts, axis=0).astype(BF16)
    o_ref[rows:, LANE:] = jnp.zeros((16, o_ref.shape[1] - LANE), BF16)


def packed_params(qkv, out, vectors):
    shape = (qkv.shape[0] + 16, qkv.shape[1] + out.shape[1])
    vectors = [v.reshape(-1, LANE) for v in vectors]
    arrays = [qkv, out] + vectors
    return pl.pallas_call(
        pack_kernel,
        out_shape=jax.ShapeDtypeStruct(shape, BF16),
        compiler_params=params(58),
        name="pack",
        cost_estimate=cost(1),
    )(*arrays)


def attend_kernel(sc, x_ref, order_ref, nsum_ref, *refs, nf, seqs):
    param_refs = refs[:nf]
    (packed_ref, p_ref, att_ref, h1_ref, wqkv, wout, vec, tabs) = refs[nf:]
    nspan = nsum_ref.shape[0]
    block = D // nf

    vec[...] = jnp.zeros_like(vec)
    for q in range(nf):
        fq = sc[SC_F] ^ q
        at = pl.ds(pl.multiple_of(fq * block, block), block)
        wqkv[at, :] = param_refs[q][:block, : 3 * D]
        wout[at, :] = param_refs[q][:block, 3 * D :]
        sm = param_refs[q][block:, :LANE].astype(F32)
        for row, src in ((G1, 0), (S1, 1), (OB, 5), (G2, 6), (S2, 7), (DB, 12)):
            vec[row : row + 1, at] = sm[src : src + 1]
        for t in range(3):
            at3 = pl.ds(pl.multiple_of(fq * 3 * block + t * block, block), block)
            vec[QB : QB + 1, at3] = sm[2 + t : 3 + t]
        for t in range(4):
            at4 = pl.ds(pl.multiple_of(fq * 4 * block + t * block, block), block)
            vec[UB : UB + 1, at4] = sm[8 + t : 9 + t]
    hs = nsum_ref[...] * vec[G1 : G1 + 1, :D] + SPAN * vec[S1 : S1 + 1, :D]
    hi = hs.astype(BF16)
    lo = (hs - hi.astype(F32)).astype(BF16)
    both = dot(jnp.concatenate([hi, lo], axis=0), wqkv[:, D:])
    t = both[:nspan] + both[nspan:] + SPAN * vec[QB : QB + 1, D : 3 * D]
    tabs[...] = (t * INV_ROOT).astype(BF16)
    prompt = lax.div(sc[SC_LEN], SPAN)
    spans = ROWS // SPAN

    def body(i):
        rows = block_rows(i)
        n1, _ = normalize(x_ref[rows, :].astype(F32))
        h1 = (n1 * vec[G1 : G1 + 1, :D] + vec[S1 : S1 + 1, :D]).astype(BF16)
        h1_ref[rows, :] = h1
        packed_ref[rows, :] = (dot(h1, wqkv[...]) + vec[QB : QB + 1, : 3 * D]).astype(BF16)

        lane = lax.broadcasted_iota(jnp.int32, (SPAN, LANE), 1)
        low = lane < HEAD
        causal = jnp.where(
            lane <= lax.broadcasted_iota(jnp.int32, (SPAN, LANE), 0), 0.0, MASKED
        ).astype(F32)
        order = order_ref[...]
        for s in range(spans):
            a = sc[SC_LEN + seqs + sc[SC_SLOT] + i * spans + s]
            start, begin = 0, 0
            for k in range(seqs):
                begin = jnp.where(start <= a, start, begin)
                start = start + lax.div(sc[SC_LEN + k], SPAN)
            seen = (order < a) & ((order >= begin) | (order < prompt))
            far = jnp.where(seen, 0.0, MASKED).astype(F32)
            bias = jnp.concatenate([causal, jnp.broadcast_to(far, (SPAN, nspan))], axis=1)
            bias = jnp.concatenate([bias, bias], axis=0)
            at = block_rows(i * spans + s, SPAN)
            for p in range(PAIRS):
                cq, ck, cv = (slice(t * D + p * LANE, t * D + (p + 1) * LANE) for t in range(3))
                q = packed_ref[at, cq] * SCALE
                zero = jnp.zeros_like(q)
                q2 = jnp.concatenate([jnp.where(low, q, zero), jnp.where(low, zero, q)], axis=0)
                kc = jnp.concatenate([packed_ref[at, ck], tabs[:, cq]], axis=0)
                vc = jnp.concatenate([packed_ref[at, cv], tabs[:, ck]], axis=0)
                scores = dot_bt(q2, kc) + bias
                peak = jnp.max(scores, axis=1, keepdims=True)
                e = jnp.exp(scores - peak)
                w = (e * (1.0 / jnp.sum(e, axis=1, keepdims=True))).astype(BF16)
                p_ref[(i * spans + s) * PAIRS + p, :SPAN] = w[:, :SPAN].T
                p_ref[(i * spans + s) * PAIRS + p, SPAN:] = w[:, SPAN:].T
                o2 = dot(w, vc)
                att_ref[at, cq] = jnp.where(low, o2[:SPAN], o2[SPAN:]).astype(BF16)

    each_block(x_ref.shape[0], body, parts=2)


def proj_kernel(x_ref, att_ref, wout, vec, r1_ref, h2_ref):
    def body(i):
        at = block_rows(i)
        r1 = x_ref[at, :].astype(F32) + (dot(att_ref[at, :], wout[...]) + vec[OB : OB + 1, :D])
        r1_ref[at, :] = r1
        n2, _ = normalize(r1)
        h2_ref[at, :] = (n2 * vec[G2 : G2 + 1, :D] + vec[S2 : S2 + 1, :D]).astype(BF16)

    each_block(x_ref.shape[0], body)


def proj(x, att, wout, vec):
    outs = [(x.shape, F32), (x.shape, BF16)]
    return resident(proj_kernel, "proj", 3, 8, (), (x, att, wout, vec), outs)


def attend(sc, x, order, nsum, weights, seqs):
    rows = x.shape[0]
    nspan = nsum.shape[0]
    outs = [
        ((rows, 3 * D), BF16),
        ((rows // SPAN * PAIRS, SPAN + nspan, 2 * SPAN), BF16),
        ((rows, D), BF16),
        ((rows, D), BF16),
        ((D, 3 * D), BF16),
        ((D, D), BF16),
        ((8, 4 * D), F32),
        ((nspan, 2 * D), BF16),
    ]
    kernel = functools.partial(attend_kernel, nf=len(weights), seqs=seqs)
    arrays = (x, order, nsum, *weights)
    return resident(kernel, "attend", 12, 12, (sc,), arrays, outs)


def relative(step, nf):
    half = nf // 2
    return jnp.where(step < half, 2 * step + 1, 2 * (step - half))


def up_kernel(sc, h2_ref, vec_ref, *refs, nf):
    up_refs = refs[:nf]
    g_ref, gp_ref, w_ref = refs[nf:]
    block = D // nf
    width = w_ref.shape[1] // nf
    k0 = 0.7978845608028654
    for q in range(nf):
        at = pl.ds(pl.multiple_of((sc[SC_F] ^ q) * block, block), block)
        w_ref[at, :] = up_refs[q][...]
    rows = h2_ref.shape[0]

    def body(j):
        cols = pl.ds(pl.multiple_of(j * width, width), width)
        for i in range(rows // ROWS):
            at = block_rows(i)
            u = dot(h2_ref[at, :], w_ref[:, cols]) + vec_ref[UB : UB + 1, cols]
            u2 = u * u
            t = jnp.tanh(u * (k0 + (k0 * 0.044715) * u2))
            half = 0.5 + 0.5 * t
            g_ref[at, cols] = (u * half).astype(BF16)
            slope = u * (k0 + (3 * k0 * 0.044715) * u2)
            gp_ref[at, cols] = (half + (0.5 - 0.5 * t * t) * slope).astype(BF16)

    each_block(nf, body, 1, parts=2)


def ffn_up(sc, h2, vec, up):
    rows, ff = h2.shape[0], up[0].shape[1]
    outs = [((rows, ff), BF16), ((rows, ff), BF16), ((D, ff), BF16)]
    kernel = functools.partial(up_kernel, nf=len(up))
    return resident(kernel, "ffn_up", 8, 12, (sc,), (h2, vec, *up), outs)


def down_grad_kernel(sc, g_ref, c_ref, send_ref, keep_ref, *, nf):
    width = g_ref.shape[1] // nf
    for q in range(nf):
        at = pl.ds(pl.multiple_of((sc[SC_F] ^ q) * width, width), width)
        grad = dot_at(g_ref[:, at], c_ref[...]).astype(BF16)
        ref = send_ref if q % 2 else keep_ref
        for j in range(D // LANE):
            ref[q // 2, j * width : (j + 1) * width, :] = grad[:, j * LANE : (j + 1) * LANE]


def down_gradient(sc, g, c, nf):
    piece = g.shape[1] // nf * D // LANE
    outs = [((nf // 2, piece, LANE), BF16)] * 2
    kernel = functools.partial(down_grad_kernel, nf=nf)
    return resident(kernel, "down_grad", 4, 12, (sc,), (g, c), outs)


def down_kernel(sc, h2_ref, c_ref, gp_ref, w_ref, *refs, nf):
    down_refs = refs[:nf]
    dh2_ref, dub_ref, send_ref, keep_ref, du_ref, grad_ref = refs[nf:]
    width = w_ref.shape[1] // nf
    block = D // nf
    rows = h2_ref.shape[0]
    for s in range(nf):
        f = sc[SC_F] ^ s
        cols = pl.ds(pl.multiple_of(f * width, width), width)
        dub_ref[:, cols] = jnp.zeros((1, width), F32)

        def body(i):
            at = block_rows(i, 2 * ROWS)
            dg = dot_bt(c_ref[at, :], down_refs[s][...])
            du = (dg * gp_ref[at, cols].astype(F32)).astype(BF16)
            du_ref[at, :] = du
            dub_ref[:, cols] += jnp.sum(du.astype(F32), axis=0, keepdims=True)
            dh2 = dot_bt(du, w_ref[:, cols])
            if s == 0:
                dh2_ref[at, :] = dh2
            else:
                dh2_ref[at, :] += dh2

        each_block(rows, body, 2 * ROWS)
        grad_ref[...] = dot_at(h2_ref[...], du_ref[...])
        for q in range(nf):
            ref = send_ref if q % 2 else keep_ref
            piece = grad_ref[pl.ds(pl.multiple_of((sc[SC_F] ^ q) * block, block), block), :]
            piece = piece.astype(BF16)
            for j in range(width // LANE):
                to = pl.multiple_of((f * (width // LANE) + j) * block, block)
                ref[q // 2, pl.ds(to, block), :] = piece[:, j * LANE : (j + 1) * LANE]


def ffn_down(sc, h2, c, gp, w, down):
    nf = len(down)
    rows = h2.shape[0]
    ff = w.shape[1]
    piece = ff // LANE * (D // nf)
    outs = [((rows, D), F32), ((1, ff), F32)] + [((nf // 2, piece, LANE), BF16)] * 2
    scratch = [pltpu.VMEM((rows, ff // nf), BF16), pltpu.VMEM((D, ff // nf), F32)]
    kernel = functools.partial(down_kernel, nf=nf)
    arrays = (h2, c, gp, w, *down)
    return resident(kernel, "ffn_down", 8, 14, (sc,), arrays, outs, scratch)


def mid_kernel(c_ref, dh2_ref, r1_ref, att_ref, wout, vec, dr1_ref, da_ref, gout_ref, gvec_ref):
    gout_ref[...] = jnp.zeros_like(gout_ref)
    gvec_ref[...] = jnp.zeros_like(gvec_ref)

    def add(row, values):
        gvec_ref[row : row + 1, :] += jnp.sum(values, axis=0, keepdims=True)

    def body(i):
        at = block_rows(i)
        c = c_ref[at, :].astype(F32)
        dh2 = dh2_ref[at, :]
        n2, rstd2 = normalize(r1_ref[at, :])
        add(G2, dh2 * n2)
        add(S2, dh2)
        add(DB, c)
        dr1 = c + norm_back(dh2 * vec[G2 : G2 + 1, :D], n2, rstd2)
        dr1_ref[at, :] = dr1
        dy = dr1.astype(BF16)
        add(OB, dy.astype(F32))
        gout_ref[...] += dot_at(att_ref[at, :], dy)
        da_ref[at, :] = dot_bt(dy, wout[...]).astype(BF16)

    each_block(c_ref.shape[0], body)


def mid(c, dh2, r1, att, wout, vec):
    rows = c.shape[0]
    outs = [((rows, D), F32), ((rows, D), BF16), ((D, D), F32), ((8, D), F32)]
    return resident(mid_kernel, "mid", 5, 12, (), (c, dh2, r1, att, wout, vec), outs)


def piece_rows(used, parts):
    return -(-used // (16 * parts)) * 16 * parts


def columns_of(half):
    wide = PAIRS // 2 * LANE
    return [slice(t * D + half * wide, t * D + (half + 1) * wide) for t in range(3)]


def back_kernel(sc, x_ref, da_ref, h1_ref, packed_ref, p_ref, tabs, wqkv, vec, nsum_ref, *refs, nf, copies, half, first, last):
    if half:
        (dub_ref, gvec_ref, before_ref, sums_ref), refs = refs[:4], refs[4:]
    else:
        (gout_ref,), refs = refs[:1], refs[1:]
    olds, refs = ((), refs) if first else (refs[:3], refs[3:])
    (dh1_ref, acc, acc_span, accv), refs = refs[:4], refs[4:]
    if last:
        (sum_ref, far_send, far_keep, send_ref, keep_ref), refs = refs[:5], refs[5:]
    (dp_ref,) = refs
    wide = PAIRS // 2 * LANE
    columns = columns_of(half)
    for k, ref in enumerate((acc, acc_span, accv)):
        ref[...] = jnp.zeros_like(ref) if first else olds[k][...]

    def add(row, values):
        accv[row : row + 1, : values.shape[1]] += jnp.sum(values, axis=0, keepdims=True)

    def body(i):
        rows = block_rows(i)
        low = lax.broadcasted_iota(jnp.int32, (SPAN, LANE), 1) < HEAD
        for s in range(ROWS // SPAN):
            at = block_rows(i * (ROWS // SPAN) + s, SPAN)
            to = slice(s * SPAN, (s + 1) * SPAN)
            for k in range(PAIRS // 2):
                p = half * (PAIRS // 2) + k
                cq, ck, cv = (slice(t * D + p * LANE, t * D + (p + 1) * LANE) for t in range(3))
                oq, ok, ov = (slice(t * wide + k * LANE, t * wide + (k + 1) * LANE) for t in range(3))
                q = packed_ref[at, cq] * SCALE
                do = da_ref[at, cq]
                zero = jnp.zeros_like(q)
                q2 = jnp.concatenate([jnp.where(low, q, zero), jnp.where(low, zero, q)], axis=0)
                do2 = jnp.concatenate([jnp.where(low, do, zero), jnp.where(low, zero, do)], axis=0)
                kc = jnp.concatenate([packed_ref[at, ck], tabs[:, cq]], axis=0)
                vc = jnp.concatenate([packed_ref[at, cv], tabs[:, ck]], axis=0)
                w = p_ref[(i * (ROWS // SPAN) + s) * PAIRS + p]
                wf = w.astype(F32)
                dp = dot_bt(vc, do2)
                delta = jnp.sum(wf * dp, axis=0, keepdims=True)
                ds = (wf * (dp - delta)).astype(BF16)
                dq2 = dot_at(ds, kc)
                dq = jnp.where(low, dq2[:SPAN], dq2[SPAN:]) * SCALE
                dk = dot(ds, q2)
                dv = dot(w, do2)
                acc_span[:, oq] += dk[SPAN:]
                acc_span[:, ok] += dv[SPAN:]
                dp_ref[to, oq] = dq.astype(BF16)
                dp_ref[to, ok] = dk[:SPAN].astype(BF16)
                dp_ref[to, ov] = dv[:SPAN].astype(BF16)
        dpk = dp_ref[...]
        add(QB, dpk.astype(F32))
        acc[...] += dot_at(h1_ref[rows, :], dpk)
        dh1 = dot_bt(dpk[:, :wide], wqkv[:, columns[0]])
        for t in (1, 2):
            dh1 = dh1 + dot_bt(dpk[:, t * wide : (t + 1) * wide], wqkv[:, columns[t]])
        if half:
            dh1 = dh1 + before_ref[rows, :]
            n1, _ = normalize(x_ref[rows, :].astype(F32))
            add(G1, dh1 * n1)
            add(S1, dh1)
        dh1_ref[block_rows(i - start), :] = dh1

    blocks = dh1_ref.shape[0] // ROWS
    start = 0 if first else x_ref.shape[0] // ROWS - blocks
    each_block(blocks * ROWS, lambda i: body(i + start), parts=max(blocks // 2, 1))
    if not last:
        return

    span = acc_span[...]
    bit = sc[SC_C] & 1
    each = span.shape[0] // copies
    for k in range(copies):
        code = code_of(k, copies)
        part = span[k * each : (k + 1) * each]
        hold = jnp.concatenate(
            [part[:, t * LANE : (t + 1) * LANE] for t in range(2 * wide // LANE)], axis=0
        ).astype(BF16)
        to = slice(code % (copies // 2) * hold.shape[0], (code % (copies // 2) + 1) * hold.shape[0])
        mine = bit == code // (copies // 2)

        @pl.when(mine)
        def _():
            far_keep[to, :] = hold

        @pl.when(jnp.logical_not(mine))
        def _():
            far_send[to, :] = hold

    span = span * INV_ROOT
    low_span = span.astype(BF16)
    nsum = nsum_ref[...]
    hs = (nsum * vec[G1 : G1 + 1, :D] + SPAN * vec[S1 : S1 + 1, :D]).astype(BF16)
    acc[:, wide:] += dot_at(hs, low_span)
    accv[QB : QB + 1, wide : 3 * wide] += SPAN * jnp.sum(span, axis=0, keepdims=True)
    de = dot_bt(low_span[:, :wide], wqkv[:, columns[1]])
    de = de + dot_bt(low_span[:, wide:], wqkv[:, columns[2]])
    block = D // nf
    if half:
        de = de + sums_ref[: de.shape[0], :]
        add(G1, de * nsum)
        accv[S1 : S1 + 1, :D] += SPAN * jnp.sum(de, axis=0, keepdims=True)
        bias = sums_ref[de.shape[0] : de.shape[0] + 8, :]
    else:
        sum_ref[: de.shape[0], :] = de
        tail = [accv[QB : QB + 1, t * wide : (t + 1) * wide] for t in range(3)]
        bias = jnp.concatenate(tail + [jnp.zeros((5, wide), F32)], axis=0)
        sum_ref[de.shape[0] : de.shape[0] + 8, :] = jnp.concatenate([bias, bias], axis=1)

    for q in range(nf):
        ref = send_ref if q % 2 else keep_ref
        fq = sc[SC_F] ^ q
        at = pl.ds(pl.multiple_of(fq * block, block), block)
        base = 0
        pieces = [acc[at, :].astype(BF16)]
        if not half:
            pieces.append(gout_ref[at, :].astype(BF16))
        for piece in pieces:
            for j in range(piece.shape[1] // LANE):
                ref[q // 2, base : base + block, :] = piece[:, j * LANE : (j + 1) * LANE]
                base += block
        if half:
            whole = jnp.concatenate(
                [
                    part
                    for t in range(3)
                    for part in (bias[t : t + 1, :wide], accv[QB : QB + 1, t * wide : (t + 1) * wide])
                ],
                axis=1,
            )
            accv[QB + 1 : QB + 2, : 3 * D] = whole
            three = [
                accv[QB + 1 : QB + 2, pl.ds(pl.multiple_of((fq * 3 + t) * block, block), block)]
                for t in range(3)
            ]
            four = [
                dub_ref[0:1, pl.ds(pl.multiple_of((fq * 4 + t) * block, block), block)]
                for t in range(4)
            ]
            small = jnp.concatenate(
                [accv[G1 : G1 + 1, at], accv[S1 : S1 + 1, at]]
                + three
                + [gvec_ref[OB : OB + 1, at], gvec_ref[G2 : G2 + 1, at], gvec_ref[S2 : S2 + 1, at]]
                + four
                + [gvec_ref[DB : DB + 1, at], jnp.zeros((3, LANE), F32)],
                axis=0,
            ).astype(BF16)
            ref[q // 2, base : base + 16, :] = small
            base += 16
        left = ref.shape[1] - base
        if left:
            ref[q // 2, base:, :] = jnp.zeros((left, LANE), BF16)


def back(sc, fixed, more, half, nf, copies, old=None, last=True):
    x, nsum = fixed[0], fixed[-1]
    rows = x.shape[0] if last and old is None else x.shape[0] // 2
    nspan = nsum.shape[0]
    wide = PAIRS // 2 * LANE
    block = D // nf
    used = 3 * wide // LANE * block + (16 if half else D // LANE * block)
    piece = piece_rows(used, copies)
    far = nspan // 2 * 2 * wide // LANE
    sums = [((D, 3 * wide), F32), ((nspan, 2 * wide), F32), ((16, 3 * D), F32)]
    outs = [((rows, D), F32)]
    scratch = [pltpu.VMEM((ROWS, 3 * wide), BF16)]
    if last:
        scratch = [pltpu.VMEM(*a) for a in sums] + scratch
        outs += [((nspan + 8, D), F32)]
        outs += [((far, LANE), BF16)] * 2 + [((nf // 2, piece, LANE), BF16)] * 2
    else:
        outs += sums
    kernel = functools.partial(
        back_kernel, nf=nf, copies=copies, half=half, first=old is None, last=last
    )

    def ordered(*refs):
        if not last:
            return kernel(*refs)
        at = len(refs) - len(scratch)
        return kernel(
            *refs[: at - len(outs) + 1], *refs[at:-1], *refs[at - len(outs) + 1 : at], refs[-1]
        )

    arrays = (*fixed, *more, *(old or ()))
    return resident(ordered, f"back_{half}", 9, 18, (sc,), arrays, outs, scratch)


def first_kernel(x_ref, dr1_ref, upper_ref, lower_ref, own_ref, wqkv, vec, o_ref, e_ref):
    i = pl.program_id(0)
    spans = ROWS // SPAN

    @pl.when(i == 0)
    def _():
        each = e_ref.shape[0]
        wide = PAIRS // 2 * LANE
        total = jnp.zeros((each, D), F32)
        for half in range(2):
            for k, columns in enumerate(columns_of(half)[1:]):
                for t in range(wide // LANE):
                    row = ((half * 2 + k) * (wide // LANE) + t) * each
                    own = own_ref[row : row + each, :].astype(F32) * INV_ROOT
                    cols = slice(columns.start + t * LANE, columns.start + (t + 1) * LANE)
                    total = total + dot_bt(own.astype(BF16), wqkv[:, cols])
        e_ref[...] = total

    at = block_rows(i)
    n1, rstd1 = normalize(x_ref[at, :].astype(F32))
    extra = jnp.concatenate(
        [jnp.broadcast_to(e_ref[pl.ds(i * spans + s, 1), :], (SPAN, D)) for s in range(spans)],
        axis=0,
    )
    half = pl.num_programs(0) // 2

    def write(ref, k):
        dh1 = ref[block_rows(k), :] + extra
        o_ref[...] = dr1_ref[at, :] + norm_back(dh1 * vec[G1 : G1 + 1, :D], n1, rstd1)

    @pl.when(i < half)
    def _():
        write(upper_ref, i)

    @pl.when(i >= half)
    def _():
        write(lower_ref, i - half)


def first_back(x, dr1, upper, lower, own, wqkv, vec):
    rows = x.shape[0]
    return pl.pallas_call(
        first_kernel,
        grid=(rows // ROWS,),
        in_specs=in_vmem(7),
        out_specs=pl.BlockSpec((ROWS, D), lambda i: (i, 0)),
        out_shape=jax.ShapeDtypeStruct((rows, D), F32),
        scratch_shapes=[pltpu.VMEM((rows // SPAN, D), F32)],
        compiler_params=params(8),
        name="first_back",
        cost_estimate=cost(3),
    )(x, dr1, upper, lower, own, wqkv, vec)


def mixed_kernel(sc, r1_ref, g_ref, vec, *refs):
    w_refs, o_ref = refs[:-1], refs[-1]
    at = block_rows(pl.program_id(0))
    total = r1_ref[at, :] + vec[DB : DB + 1, :D]
    width = w_refs[0].shape[0]
    for q, w_ref in enumerate(w_refs):
        cols = pl.ds(pl.multiple_of((sc[SC_F] ^ q) * width, width), width)
        total = total + dot(g_ref[at, cols], w_ref[...])
    o_ref[...] = total.astype(BF16)


def block_output(sc, r1, g, vec, down):
    rows = r1.shape[0]
    return pl.pallas_call(
        mixed_kernel,
        grid=(rows // ROWS,),
        in_specs=[pl.BlockSpec(memory_space=pltpu.SMEM)] + in_vmem(3 + len(down)),
        out_specs=pl.BlockSpec((ROWS, D), lambda i: (i, 0)),
        out_shape=jax.ShapeDtypeStruct((rows, D), BF16),
        compiler_params=params(8),
        name="block_output",
        cost_estimate=cost(4),
    )(sc, r1, g, vec, *down)


def swap(array, axis, bit):
    n = lax.axis_size(axis)
    return lax.ppermute(array, axis, [(k, k ^ bit) for k in range(n)])


def after(array, *others):
    return lax.optimization_barrier((array, others))[0]


def first_gather(array, axis):
    return swap(array, axis, lax.axis_size(axis) // 2)


def gathered(array, far, axis):
    n = lax.axis_size(axis)
    bit = n // 2
    held = {0: array, bit: far}
    bit //= 2
    while bit:
        for r in sorted(held):
            held[r ^ bit] = swap(held[r], axis, bit)
        bit //= 2
    return [held[r] for r in range(n)]


def total_of(values):
    total = values[0].astype(F32)
    for value in values[1:]:
        total = total + value.astype(F32)
    return total.astype(BF16)


def fold_kernel(sc, *refs, bit, counts):
    own = lax.div(sc[SC_C], bit) & 1 if bit else 0
    arrays, (send_ref, own_ref) = refs[:-2], refs[-2:]
    at = 0
    for count in counts:
        group, arrays = arrays[:count], arrays[count:]
        a, _, h, _ = group[0].shape
        for ref, half in ((send_ref, 1 - own), (own_ref, own)):
            for k in range(a):
                ref[k, at : at + h, :] = total_of([g[k, half] for g in group])
        at += h


def fold(sc, bit, *groups, micros=1):
    a = groups[0][0].shape[0]
    h = sum(group[0].shape[2] for group in groups)
    arrays = [array for group in groups for array in group]
    counts = tuple(len(group) for group in groups)
    kernel = functools.partial(fold_kernel, bit=bit, counts=counts)
    return resident(kernel, "fold", micros, 8, (sc,), arrays, [((a, h, LANE), BF16)] * 2)


def quad_kernel(sc, keep_ref, got_ref, *refs, bit, beside):
    pairs, (own_ref, ctx_ref, near_ref, both_ref) = refs[:-4], refs[-4:]
    own = lax.div(sc[SC_C], bit) & 1
    at = keep_ref.shape[2]
    own_ref[:at, :] = total_of((keep_ref[0, own], got_ref[0, own]))
    ctx_ref[:at, :] = total_of((keep_ref[0, 1 - own], got_ref[0, 1 - own]))
    near_ref[:at, :] = total_of((keep_ref[1, own], got_ref[1, own]))
    both_ref[...] = total_of((keep_ref[1, 1 - own], got_ref[1, 1 - own]))
    ends = {True: at, False: at}
    for n, (kept, sent) in enumerate(zip(pairs[0::2], pairs[1::2])):
        rows = kept.shape[0]
        own_ref[at : at + rows, :] = kept[...]
        at += rows
        ref, end = (near_ref if n < beside else ctx_ref), ends[n < beside]
        ref[end : end + rows, :] = sent[...]
        ends[n < beside] += rows


def quad(sc, bit, keep, got, with_near, with_ctx):
    kernel = functools.partial(quad_kernel, bit=bit, beside=len(with_near))
    arrays = (keep, got, *(a for pair in (*with_near, *with_ctx) for a in pair))
    h = keep.shape[2]
    near = h + sum(kept.shape[0] for kept, _ in with_near)
    ctx = h + sum(kept.shape[0] for kept, _ in with_ctx)
    outs = [((n, LANE), BF16) for n in (near + ctx - h, ctx, near, h)]
    return resident(kernel, "quad", 1, 8, (sc,), arrays, outs)


def swap_both(array, ctx_bit, near_bit):
    n, nf = lax.axis_size("ctx"), lax.axis_size("fsdp")
    pairs = [
        (a * nf + b, (a ^ ctx_bit) * nf + (b ^ near_bit)) for a in range(n) for b in range(nf)
    ]
    return lax.ppermute(array, ("ctx", "fsdp"), pairs)


def refold_kernel(sc, *refs, bit, sizes, sources):
    arrays, (send_ref, own_ref) = refs[:-2], refs[-2:]
    own = lax.div(sc[SC_C], bit) & 1
    at = 0
    for h, source in zip(sizes, sources):
        for ref, half in ((send_ref, 1 - own), (own_ref, own)):
            values = [
                arrays[k][pl.ds(pl.multiple_of(base + half * h, 16), h), :] for k, base in source
            ]
            ref[at : at + h, :] = total_of(values)
        at += h


def refold(sc, bit, arrays, sizes, micros=1, sources=None):
    if sources is None:
        starts = [2 * sum(sizes[:n]) for n in range(len(sizes))]
        sources = [[(k, start) for k in range(len(arrays))] for start in starts]
    outs = [((sum(sizes), LANE), BF16)] * 2
    kernel = functools.partial(refold_kernel, bit=bit, sizes=sizes, sources=sources)
    return resident(kernel, "fold", micros, 8, (sc,), arrays, outs)


def last_kernel(keep_ref, got_ref, o_ref, *rest):
    used = o_ref.shape[0]
    total = keep_ref[:used, :].astype(F32) + got_ref[:used, :].astype(F32)
    o_ref[...] = total.astype(BF16)
    for ref in rest:
        total = keep_ref[used:, :].astype(F32) + got_ref[used:, :].astype(F32)
        ref[...] = total.astype(BF16)


def last_sum(keep, got, used):
    outs = [((used, LANE), BF16)]
    if used < keep.shape[0]:
        outs.append(((keep.shape[0] - used, LANE), BF16))
    return resident(last_kernel, "last", 1, 8, (), (keep, got), outs)


class Sequence:
    def __init__(self):
        self.last = ()

    def next(self, array):
        return after(array, *self.last) if self.last else array

    def made(self, *arrays):
        self.last = arrays


class Part:
    def __init__(self, sc, seq, keep, send):
        self.sc, self.seq, self.keep, self.send = sc, seq, keep, send
        self.count, self.rows = keep.shape[0], keep.shape[1]
        self.total = self.rows
        self.move("fsdp", 1)

    def move(self, axis, bit):
        self.gots = (swap(self.send, axis, bit),)

    def view(self, axis):
        if axis == "fsdp":
            self.count //= 2
            return 1, 2, self.count * self.rows, LANE
        self.rows //= 2
        return self.count, 2, self.rows, LANE

    def pair(self, axis):
        view = self.view(axis)
        return tuple(a.reshape(view) for a in (self.keep, *self.gots))

    def split(self, axis, bit, micros=1):
        keep, got = self.pair(axis)
        pair = (self.seq.next(keep), got)
        self.send, self.keep = fold(self.sc, bit if axis == "ctx" else 0, pair, micros=micros)
        self.seq.made(self.keep, self.send)

    def step(self, axis, bit, micros=1):
        self.split(axis, bit, micros)
        self.move(axis, bit)


def ctx_bits():
    n = lax.axis_size("ctx")
    return [1 << k for k in range(n.bit_length() - 1)]


def united(sc, seq, parts):
    groups = [part.pair("ctx") for part in parts]
    groups[0] = (seq.next(groups[0][0]), *groups[0][1:])
    sizes = [group[0].shape[2] for group in groups]
    return Union(sc, seq, [a[0] for a in fold(sc, ctx_bits()[1], *groups)], sizes, len(sizes))


class Union:
    def __init__(self, sc, seq, halves, sizes, few):
        self.sc, self.seq, self.sizes = sc, seq, sizes
        self.bits = ctx_bits()
        self.used = sum(sizes[:few]) * 2 // self.bits[-1]
        self.received(self.bits[1], *halves)
        self.at = 2

    def received(self, bit, send, keep):
        self.keep = keep
        self.seq.made(keep, send)
        self.got = swap(send, "ctx", bit)

    def more(self):
        return self.at < len(self.bits)

    def step(self, micros=1):
        bit = self.bits[self.at]
        self.at += 1
        self.sizes = [size // 2 for size in self.sizes]
        keep = self.seq.next(self.keep)
        self.received(bit, *refold(self.sc, bit, (keep, self.got), self.sizes, micros))

    def end(self):
        own, *rest = last_sum(self.seq.next(self.keep), self.got, self.used)
        self.received(self.bits[-1], own, own)
        self.at = len(self.bits) - 1
        return rest[0] if rest else None

    def gathering(self):
        return self.at > 0

    def join(self):
        both = jnp.concatenate([self.seq.next(self.keep), self.got], axis=0)
        self.at -= 1
        self.received(self.bits[self.at], both, both)

    def rows(self):
        both = jnp.concatenate([self.seq.next(self.keep), self.got], axis=0)
        return both.reshape(lax.axis_size("ctx"), -1, LANE)


def code_of(index, n):
    code = 0
    for k in range(n.bit_length() - 1):
        bit = index >> k if isinstance(index, int) else lax.div(index, 1 << k)
        code = 2 * code + (bit & 1)
    return code


def finish_kernel(sc, got_ref, *refs, heights, plan):
    outs, rows = refs[:-1], refs[-1]
    n = got_ref.shape[0]
    code = code_of(sc[SC_C], n)
    for k in range(n):
        at, base = 0, 0
        for height in heights:
            h = height // n
            to = pl.multiple_of(base + (code ^ k) * h, 16)
            rows[pl.ds(to, h), :] = got_ref[k, at : at + h, :].astype(F32)
            at, base = at + h, base + height
    for ref, places in zip(outs, plan):
        if len(ref.shape) == 1:
            for j, place in enumerate(places):
                ref[j * LANE : (j + 1) * LANE] = rows[place, :]
            continue
        height = ref.shape[0]
        for j, place in enumerate(places):
            ref[:, j * LANE : (j + 1) * LANE] = rows[place : place + height, :]


def finish(sc, got, heights, shapes, plan):
    return pl.pallas_call(
        functools.partial(finish_kernel, heights=heights, plan=plan),
        in_specs=[pl.BlockSpec(memory_space=pltpu.SMEM)] + in_vmem(1),
        out_shape=[jax.ShapeDtypeStruct(shape, F32) for shape in shapes],
        scratch_shapes=[pltpu.VMEM((sum(heights), LANE), F32)],
        compiler_params=params(16),
        name="finish",
        cost_estimate=cost(2),
    )(sc, got)


def local(
    tokens, ln1_gain, ln1_shift, qkv_weight, qkv_bias, out_weight, out_bias, ln2_gain, ln2_shift,
    up_weight, up_bias, down_weight, down_bias, seq_lengths, span_order, cotangent,
):
    nf = lax.axis_size("fsdp")
    nc = lax.axis_size("ctx")
    x, c = tokens[0], cotangent[0]
    spans = x.shape[0] // SPAN
    seqs = seq_lengths.shape[1]
    weights = packed_params(
        qkv_weight, out_weight,
        (ln1_gain, ln1_shift, qkv_bias, out_bias, ln2_gain, ln2_shift, up_bias, down_bias),
    )
    scalars = jnp.concatenate(
        [
            lax.axis_index("fsdp").reshape(1),
            lax.axis_index("ctx").reshape(1),
            (lax.axis_index("ctx") * spans).reshape(1),
            seq_lengths[0],
            span_order[0],
        ]
    ).astype(jnp.int32)
    far_weights = first_gather(weights, "fsdp")
    sums = span_sums(x, nc)
    nsum = lax.all_to_all(sums, "ctx", 0, 0, tiled=True).reshape(nc * spans, D)
    far_weights = after(far_weights, nsum)
    weights = gathered(weights, far_weights, "fsdp")
    up_weight = after(up_weight, far_weights)
    far_up = first_gather(up_weight, "fsdp")
    down_weight = after(down_weight, far_weights)
    far_down = first_gather(down_weight, "fsdp")

    packed, p, att, h1, wqkv, wout, vec, tabs = attend(
        scalars, x, span_order, nsum, weights, seqs
    )
    up = gathered(up_weight, after(far_up, att), "fsdp")
    r1, h2 = proj(x, att, wout, vec)
    g, gp, wup = ffn_up(scalars, h2, vec, up)
    dsend, dkeep = down_gradient(scalars, g, c, nf)
    down = gathered(down_weight, after(far_down, dkeep), "fsdp")
    dh2, dub, usend, ukeep = ffn_down(scalars, h2, c, gp, wup, down)
    bits = ctx_bits()
    near = [("fsdp", 1 << k) for k in range(1, nf.bit_length() - 1)]

    seq = Sequence()
    from_down = Part(scalars, seq, dkeep, dsend)
    from_down.step(*near[0])
    dr1, da, gout, gvec = mid(c, seq.next(dh2), r1, att, wout, vec)
    seq.made(da)
    from_up = Part(scalars, seq, ukeep, usend)
    from_up.step("ctx", bits[0])
    da = seq.next(da)
    fixed = (x, da, h1, packed, p, tabs, wqkv, vec, nsum)
    dh1, sums, fsend0, fkeep0, send, keep = back(scalars, fixed, (gout,), 0, nf, nc)
    seq.made(dh1)
    first = Part(scalars, seq, keep, send)
    from_down.step("ctx", bits[0])
    from_up.step(*near[0])
    dh1 = seq.next(dh1)
    upper, *old = back(scalars, fixed, (dub, gvec, dh1, sums), 1, nf, nc, last=False)
    seq.made(old[0])
    first.step("ctx", bits[0])
    feed = united(scalars, seq, [from_down, from_up])
    old[0] = seq.next(old[0])
    lower, _, fsend1, fkeep1, send, keep = back(
        scalars, fixed, (dub, gvec, dh1, sums), 1, nf, nc, old=old
    )
    seq.made(lower)
    second = Part(scalars, seq, keep, send)
    while feed.more():
        feed.step(FILL)
    first.split(*near[0], FILL)
    with_near = ((first.keep[0], first.send[0]),)
    with_ctx = ((fkeep0, fsend0), (fkeep1, fsend1))
    view = (2, 2, second.rows // 2, LANE)
    keep, got = (a.reshape(view) for a in (second.keep, *second.gots))
    own, to_ctx, to_near, to_both = quad(
        scalars, bits[0], seq.next(keep), got, with_near, with_ctx
    )
    seq.made(own)
    arrays = (
        own,
        swap(to_ctx, "ctx", bits[0]),
        swap(to_near, *near[0]),
        swap_both(to_both, bits[0], near[0][1]),
    )
    feed.end()
    heights = [second.total // 2] + [kept.shape[0] for kept, _ in (*with_near, *with_ctx)]
    sources, at, ends = [[(k, 0) for k in range(4)]], heights[0], {1: heights[0], 2: heights[0]}
    for n, rows in enumerate(heights[1:]):
        where = 2 if n < len(with_near) else 1
        sources.append([(0, at), (where, ends[where])])
        at += rows
        ends[where] += rows
    sizes = [rows // 2 for rows in heights]
    arrays = (seq.next(arrays[0]), *arrays[1:])
    halves = refold(scalars, bits[1], arrays, sizes, sources=sources)
    rest = Union(scalars, seq, halves, sizes, 2)
    mixed = block_output(scalars, seq.next(r1), g, vec, down)
    seq.made(mixed)
    while feed.at > 1:
        feed.join()
    while rest.more():
        rest.step()
    feed.join()
    own_span = rest.end()
    rest.join()
    tokens_grad = first_back(seq.next(x), dr1, upper, lower, own_span, wqkv, vec)
    seq.made(tokens_grad)
    while rest.gathering():
        rest.join()
    block = D // nf
    height, width = down_weight.shape[0], up_weight.shape[1]
    heights = (from_down.total, from_up.total)
    grad_down, grad_up = finish(
        scalars,
        feed.rows(),
        heights,
        [(height, D), (block, width)],
        [
            [height * j for j in range(D // LANE)],
            [heights[0] + block * j for j in range(width // LANE)],
        ],
    )
    seq.made(grad_down)
    half = PAIRS // 2
    plan = [
        [
            (second.total if p < half else 0) + block * (t * half + p % half)
            for t in range(3)
            for p in range(PAIRS)
        ],
        [second.total + block * (3 * half + j) for j in range(D // LANE)],
    ]
    shapes = [(block, 3 * D), (block, D)]
    at = 3 * half * block
    for wide in (block, block, 3 * block, block, block, block, 4 * block, block):
        shapes.append((wide,))
        plan.append([at + j for j in range(wide // LANE)])
        at += wide // LANE
    grad_qkv, grad_out, *vectors = finish(
        scalars, rest.rows(), (second.total, first.total), shapes, plan
    )
    g1, s1, qb, ob, g2, s2, ub, db = vectors
    return (
        mixed[None], tokens_grad[None], g1, s1, grad_qkv, qb, grad_out, ob, g2, s2,
        grad_up, ub, grad_down, db,
    )


def solution(mesh):
    rows, one, two = P("fsdp", "ctx", None), P("fsdp"), P("fsdp", None)
    return jax.shard_map(
        local,
        mesh=mesh,
        in_specs=(
            rows, one, one, two, one, two, one, one, one, two, one, two, one, two, two, rows,
        ),
        out_specs=(rows, rows, one, one, two, one, two, one, one, one, two, one, two, one),
        check_vma=False,
    )
```

```python
import functools

import jax
import jax.numpy as jnp
from jax import lax
from jax.experimental import pallas as pl
from jax.experimental.pallas import tpu as pltpu
from jax.sharding import PartitionSpec as P

D = 512
HEADS = 8
HEAD = 64
SPAN = 128
LANE = 128
PAIRS = D // LANE
ROWS = 256
EPSILON = 1e-05
MASKED = -1e30
SCALE = HEAD**-0.5
FILL = 3
INV_ROOT = SPAN**-0.5
F32 = jnp.float32
BF16 = jnp.bfloat16

G1, S1, OB, G2, S2, DB, QB, UB = range(8)
SC_F, SC_C, SC_SLOT, SC_LEN = range(4)


def dot(a, b):
    return lax.dot_general(a, b, (((1,), (0,)), ((), ())), preferred_element_type=F32)


def dot_bt(a, b):
    return lax.dot_general(a, b, (((1,), (1,)), ((), ())), preferred_element_type=F32)


def dot_at(a, b):
    return lax.dot_general(a, b, (((0,), (0,)), ((), ())), preferred_element_type=F32)


def normalize(values):
    centre = values - jnp.mean(values, axis=-1, keepdims=True)
    spread = jnp.mean(centre * centre, axis=-1, keepdims=True)
    rstd = lax.rsqrt(spread + EPSILON)
    return centre * rstd, rstd


def norm_back(e, n, rstd):
    return rstd * (
        e - jnp.mean(e, axis=-1, keepdims=True) - n * jnp.mean(e * n, axis=-1, keepdims=True)
    )


def params(mib):
    return pltpu.CompilerParams(vmem_limit_bytes=mib * 1024 * 1024)


def in_vmem(count):
    return [pl.BlockSpec(memory_space=pltpu.VMEM) for _ in range(count)]


def cost(micros):
    return pl.CostEstimate(
        flops=int(micros * 1e9), transcendentals=0, bytes_accessed=int(micros * 1e6)
    )


def resident(kernel, name, micros, mib, scalars, arrays, outs, scratch=()):
    return pl.pallas_call(
        kernel,
        in_specs=[pl.BlockSpec(memory_space=pltpu.SMEM)] * len(scalars) + in_vmem(len(arrays)),
        out_specs=in_vmem(len(outs)),
        out_shape=[jax.ShapeDtypeStruct(shape, dtype) for shape, dtype in outs],
        scratch_shapes=list(scratch),
        compiler_params=params(mib),
        name=name,
        cost_estimate=cost(micros),
    )(*scalars, *arrays)


def block_rows(i, size=ROWS):
    if isinstance(i, int):
        return slice(i * size, (i + 1) * size)
    return pl.ds(pl.multiple_of(i * size, size), size)


def each_block(rows, body, size=ROWS, parts=1):
    each = rows // size // parts
    if parts == 1:
        for i in range(each):
            body(i)
        return

    def step(n, carry):
        for k in range(each):
            body(n * each + k)
        return carry

    lax.fori_loop(0, parts, step, 0)


def sums_kernel(x_ref, o_ref):
    spans = x_ref.shape[0] // SPAN
    sums = []
    for s in range(spans):
        n, _ = normalize(x_ref[s * SPAN : (s + 1) * SPAN, :].astype(F32))
        sums.append(jnp.sum(n, axis=0, keepdims=True))
    table = jnp.concatenate(sums, axis=0)
    for k in range(o_ref.shape[0]):
        o_ref[k] = table


def span_sums(x, copies):
    spans = x.shape[0] // SPAN
    return resident(sums_kernel, "span_sums", 3, 16, (), (x,), [((copies, spans, D), F32)])[0]


def pack_kernel(qkv_ref, out_ref, *refs):
    o_ref = refs[-1]
    rows, width = qkv_ref.shape
    o_ref[:rows, :width] = qkv_ref[...]
    o_ref[:rows, width:] = out_ref[...]
    parts = [ref[...].astype(F32) for ref in refs[:-1]]
    used = sum(part.shape[0] for part in parts)
    parts.append(jnp.zeros((16 - used, LANE), F32))
    o_ref[rows:, :LANE] = jnp.concatenate(parts, axis=0).astype(BF16)
    o_ref[rows:, LANE:] = jnp.zeros((16, o_ref.shape[1] - LANE), BF16)


def packed_params(qkv, out, vectors):
    shape = (qkv.shape[0] + 16, qkv.shape[1] + out.shape[1])
    vectors = [v.reshape(-1, LANE) for v in vectors]
    arrays = [qkv, out] + vectors
    return pl.pallas_call(
        pack_kernel,
        out_shape=jax.ShapeDtypeStruct(shape, BF16),
        compiler_params=params(58),
        name="pack",
        cost_estimate=cost(1),
    )(*arrays)


def attend_kernel(sc, x_ref, order_ref, nsum_ref, *refs, nf, seqs):
    param_refs = refs[:nf]
    (packed_ref, p_ref, att_ref, h1_ref, wqkv, wout, vec, tabs) = refs[nf:]
    nspan = nsum_ref.shape[0]
    block = D // nf

    vec[...] = jnp.zeros_like(vec)
    for q in range(nf):
        fq = sc[SC_F] ^ q
        at = pl.ds(pl.multiple_of(fq * block, block), block)
        wqkv[at, :] = param_refs[q][:block, : 3 * D]
        wout[at, :] = param_refs[q][:block, 3 * D :]
        sm = param_refs[q][block:, :LANE].astype(F32)
        for row, src in ((G1, 0), (S1, 1), (OB, 5), (G2, 6), (S2, 7), (DB, 12)):
            vec[row : row + 1, at] = sm[src : src + 1]
        for t in range(3):
            at3 = pl.ds(pl.multiple_of(fq * 3 * block + t * block, block), block)
            vec[QB : QB + 1, at3] = sm[2 + t : 3 + t]
        for t in range(4):
            at4 = pl.ds(pl.multiple_of(fq * 4 * block + t * block, block), block)
            vec[UB : UB + 1, at4] = sm[8 + t : 9 + t]
    hs = nsum_ref[...] * vec[G1 : G1 + 1, :D] + SPAN * vec[S1 : S1 + 1, :D]
    hi = hs.astype(BF16)
    lo = (hs - hi.astype(F32)).astype(BF16)
    both = dot(jnp.concatenate([hi, lo], axis=0), wqkv[:, D:])
    t = both[:nspan] + both[nspan:] + SPAN * vec[QB : QB + 1, D : 3 * D]
    tabs[...] = (t * INV_ROOT).astype(BF16)
    prompt = lax.div(sc[SC_LEN], SPAN)
    spans = ROWS // SPAN

    def body(i):
        rows = block_rows(i)
        n1, _ = normalize(x_ref[rows, :].astype(F32))
        h1 = (n1 * vec[G1 : G1 + 1, :D] + vec[S1 : S1 + 1, :D]).astype(BF16)
        h1_ref[rows, :] = h1
        packed_ref[rows, :] = (dot(h1, wqkv[...]) + vec[QB : QB + 1, : 3 * D]).astype(BF16)

        lane = lax.broadcasted_iota(jnp.int32, (SPAN, LANE), 1)
        low = lane < HEAD
        causal = jnp.where(
            lane <= lax.broadcasted_iota(jnp.int32, (SPAN, LANE), 0), 0.0, MASKED
        ).astype(F32)
        order = order_ref[...]
        for s in range(spans):
            a = sc[SC_LEN + seqs + sc[SC_SLOT] + i * spans + s]
            start, begin = 0, 0
            for k in range(seqs):
                begin = jnp.where(start <= a, start, begin)
                start = start + lax.div(sc[SC_LEN + k], SPAN)
            seen = (order < a) & ((order >= begin) | (order < prompt))
            far = jnp.where(seen, 0.0, MASKED).astype(F32)
            bias = jnp.concatenate([causal, jnp.broadcast_to(far, (SPAN, nspan))], axis=1)
            bias = jnp.concatenate([bias, bias], axis=0)
            at = block_rows(i * spans + s, SPAN)
            for p in range(PAIRS):
                cq, ck, cv = (slice(t * D + p * LANE, t * D + (p + 1) * LANE) for t in range(3))
                q = packed_ref[at, cq] * SCALE
                zero = jnp.zeros_like(q)
                q2 = jnp.concatenate([jnp.where(low, q, zero), jnp.where(low, zero, q)], axis=0)
                kc = jnp.concatenate([packed_ref[at, ck], tabs[:, cq]], axis=0)
                vc = jnp.concatenate([packed_ref[at, cv], tabs[:, ck]], axis=0)
                scores = dot_bt(q2, kc) + bias
                peak = jnp.max(scores, axis=1, keepdims=True)
                e = jnp.exp(scores - peak)
                w = (e * (1.0 / jnp.sum(e, axis=1, keepdims=True))).astype(BF16)
                p_ref[(i * spans + s) * PAIRS + p, :SPAN] = w[:, :SPAN].T
                p_ref[(i * spans + s) * PAIRS + p, SPAN:] = w[:, SPAN:].T
                o2 = dot(w, vc)
                att_ref[at, cq] = jnp.where(low, o2[:SPAN], o2[SPAN:]).astype(BF16)

    each_block(x_ref.shape[0], body, parts=2)


def proj_kernel(x_ref, att_ref, wout, vec, r1_ref, h2_ref):
    def body(i):
        at = block_rows(i)
        r1 = x_ref[at, :].astype(F32) + (dot(att_ref[at, :], wout[...]) + vec[OB : OB + 1, :D])
        r1_ref[at, :] = r1
        n2, _ = normalize(r1)
        h2_ref[at, :] = (n2 * vec[G2 : G2 + 1, :D] + vec[S2 : S2 + 1, :D]).astype(BF16)

    each_block(x_ref.shape[0], body)


def proj(x, att, wout, vec):
    outs = [(x.shape, F32), (x.shape, BF16)]
    return resident(proj_kernel, "proj", 3, 8, (), (x, att, wout, vec), outs)


def attend(sc, x, order, nsum, weights, seqs):
    rows = x.shape[0]
    nspan = nsum.shape[0]
    outs = [
        ((rows, 3 * D), BF16),
        ((rows // SPAN * PAIRS, SPAN + nspan, 2 * SPAN), BF16),
        ((rows, D), BF16),
        ((rows, D), BF16),
        ((D, 3 * D), BF16),
        ((D, D), BF16),
        ((8, 4 * D), F32),
        ((nspan, 2 * D), BF16),
    ]
    kernel = functools.partial(attend_kernel, nf=len(weights), seqs=seqs)
    arrays = (x, order, nsum, *weights)
    return resident(kernel, "attend", 12, 12, (sc,), arrays, outs)


def relative(step, nf):
    half = nf // 2
    return jnp.where(step < half, 2 * step + 1, 2 * (step - half))


def up_kernel(sc, h2_ref, vec_ref, *refs, nf):
    up_refs = refs[:nf]
    g_ref, gp_ref, w_ref = refs[nf:]
    block = D // nf
    width = w_ref.shape[1] // nf
    k0 = 0.7978845608028654
    for q in range(nf):
        at = pl.ds(pl.multiple_of((sc[SC_F] ^ q) * block, block), block)
        w_ref[at, :] = up_refs[q][...]
    rows = h2_ref.shape[0]

    def body(j):
        cols = pl.ds(pl.multiple_of(j * width, width), width)
        for i in range(rows // ROWS):
            at = block_rows(i)
            u = dot(h2_ref[at, :], w_ref[:, cols]) + vec_ref[UB : UB + 1, cols]
            u2 = u * u
            t = jnp.tanh(u * (k0 + (k0 * 0.044715) * u2))
            half = 0.5 + 0.5 * t
            g_ref[at, cols] = (u * half).astype(BF16)
            slope = u * (k0 + (3 * k0 * 0.044715) * u2)
            gp_ref[at, cols] = (half + (0.5 - 0.5 * t * t) * slope).astype(BF16)

    each_block(nf, body, 1, parts=2)


def ffn_up(sc, h2, vec, up):
    rows, ff = h2.shape[0], up[0].shape[1]
    outs = [((rows, ff), BF16), ((rows, ff), BF16), ((D, ff), BF16)]
    kernel = functools.partial(up_kernel, nf=len(up))
    return resident(kernel, "ffn_up", 8, 12, (sc,), (h2, vec, *up), outs)


def down_grad_kernel(sc, g_ref, c_ref, send_ref, keep_ref, *, nf):
    width = g_ref.shape[1] // nf
    for q in range(nf):
        at = pl.ds(pl.multiple_of((sc[SC_F] ^ q) * width, width), width)
        grad = dot_at(g_ref[:, at], c_ref[...]).astype(BF16)
        ref = send_ref if q % 2 else keep_ref
        for j in range(D // LANE):
            ref[q // 2, j * width : (j + 1) * width, :] = grad[:, j * LANE : (j + 1) * LANE]


def down_gradient(sc, g, c, nf):
    piece = g.shape[1] // nf * D // LANE
    outs = [((nf // 2, piece, LANE), BF16)] * 2
    kernel = functools.partial(down_grad_kernel, nf=nf)
    return resident(kernel, "down_grad", 4, 12, (sc,), (g, c), outs)


def down_kernel(sc, h2_ref, c_ref, gp_ref, w_ref, *refs, nf):
    down_refs = refs[:nf]
    dh2_ref, dub_ref, send_ref, keep_ref, du_ref, grad_ref = refs[nf:]
    width = w_ref.shape[1] // nf
    block = D // nf
    rows = h2_ref.shape[0]
    for s in range(nf):
        f = sc[SC_F] ^ s
        cols = pl.ds(pl.multiple_of(f * width, width), width)
        dub_ref[:, cols] = jnp.zeros((1, width), F32)

        def body(i):
            at = block_rows(i, 2 * ROWS)
            dg = dot_bt(c_ref[at, :], down_refs[s][...])
            du = (dg * gp_ref[at, cols].astype(F32)).astype(BF16)
            du_ref[at, :] = du
            dub_ref[:, cols] += jnp.sum(du.astype(F32), axis=0, keepdims=True)
            dh2 = dot_bt(du, w_ref[:, cols])
            if s == 0:
                dh2_ref[at, :] = dh2
            else:
                dh2_ref[at, :] += dh2

        each_block(rows, body, 2 * ROWS)
        grad_ref[...] = dot_at(h2_ref[...], du_ref[...])
        for q in range(nf):
            ref = send_ref if q % 2 else keep_ref
            piece = grad_ref[pl.ds(pl.multiple_of((sc[SC_F] ^ q) * block, block), block), :]
            piece = piece.astype(BF16)
            for j in range(width // LANE):
                to = pl.multiple_of((f * (width // LANE) + j) * block, block)
                ref[q // 2, pl.ds(to, block), :] = piece[:, j * LANE : (j + 1) * LANE]


def ffn_down(sc, h2, c, gp, w, down):
    nf = len(down)
    rows = h2.shape[0]
    ff = w.shape[1]
    piece = ff // LANE * (D // nf)
    outs = [((rows, D), F32), ((1, ff), F32)] + [((nf // 2, piece, LANE), BF16)] * 2
    scratch = [pltpu.VMEM((rows, ff // nf), BF16), pltpu.VMEM((D, ff // nf), F32)]
    kernel = functools.partial(down_kernel, nf=nf)
    arrays = (h2, c, gp, w, *down)
    return resident(kernel, "ffn_down", 8, 14, (sc,), arrays, outs, scratch)


def mid_kernel(c_ref, dh2_ref, r1_ref, att_ref, wout, vec, dr1_ref, da_ref, gout_ref, gvec_ref):
    gout_ref[...] = jnp.zeros_like(gout_ref)
    gvec_ref[...] = jnp.zeros_like(gvec_ref)

    def add(row, values):
        gvec_ref[row : row + 1, :] += jnp.sum(values, axis=0, keepdims=True)

    def body(i):
        at = block_rows(i)
        c = c_ref[at, :].astype(F32)
        dh2 = dh2_ref[at, :]
        n2, rstd2 = normalize(r1_ref[at, :])
        add(G2, dh2 * n2)
        add(S2, dh2)
        add(DB, c)
        dr1 = c + norm_back(dh2 * vec[G2 : G2 + 1, :D], n2, rstd2)
        dr1_ref[at, :] = dr1
        dy = dr1.astype(BF16)
        add(OB, dy.astype(F32))
        gout_ref[...] += dot_at(att_ref[at, :], dy)
        da_ref[at, :] = dot_bt(dy, wout[...]).astype(BF16)

    each_block(c_ref.shape[0], body)


def mid(c, dh2, r1, att, wout, vec):
    rows = c.shape[0]
    outs = [((rows, D), F32), ((rows, D), BF16), ((D, D), F32), ((8, D), F32)]
    return resident(mid_kernel, "mid", 5, 12, (), (c, dh2, r1, att, wout, vec), outs)


def tiles_kernel(packed_ref, tabs, q2_ref, kc_ref, vc_ref):
    low = lax.broadcasted_iota(jnp.int32, (SPAN, LANE), 1) < HEAD

    def body(i):
        at = block_rows(i, SPAN)
        for p in range(PAIRS):
            cq, ck, cv = (slice(t * D + p * LANE, t * D + (p + 1) * LANE) for t in range(3))
            n = i * PAIRS + p
            q = packed_ref[at, cq] * SCALE
            zero = jnp.zeros_like(q)
            q2_ref[n, :SPAN] = jnp.where(low, q, zero)
            q2_ref[n, SPAN:] = jnp.where(low, zero, q)
            kc_ref[n, :SPAN] = packed_ref[at, ck]
            kc_ref[n, SPAN:] = tabs[:, cq]
            vc_ref[n, :SPAN] = packed_ref[at, cv]
            vc_ref[n, SPAN:] = tabs[:, ck]

    spans = packed_ref.shape[0] // SPAN
    each_block(spans, body, 1, parts=spans // 2)


def tiles(packed, tabs):
    n = packed.shape[0] // SPAN * PAIRS
    keys = SPAN + tabs.shape[0]
    outs = [((n, 2 * SPAN, LANE), BF16)] + [((n, keys, LANE), BF16)] * 2
    return resident(tiles_kernel, "tiles", 1, 8, (), (packed, tabs), outs)


def piece_rows(used, parts):
    return -(-used // (16 * parts)) * 16 * parts


def columns_of(half):
    wide = PAIRS // 2 * LANE
    return [slice(t * D + half * wide, t * D + (half + 1) * wide) for t in range(3)]


def back_kernel(sc, x_ref, da_ref, h1_ref, q2_ref, kc_ref, vc_ref, p_ref, wqkv, vec, nsum_ref, *refs, nf, copies, half, first, last):
    if half:
        (dub_ref, gvec_ref, before_ref, sums_ref), refs = refs[:4], refs[4:]
    else:
        (gout_ref,), refs = refs[:1], refs[1:]
    olds, refs = ((), refs) if first else (refs[:3], refs[3:])
    (dh1_ref, acc, acc_span, accv), refs = refs[:4], refs[4:]
    if last:
        (sum_ref, far_send, far_keep, send_ref, keep_ref), refs = refs[:5], refs[5:]
    (dp_ref,) = refs
    wide = PAIRS // 2 * LANE
    columns = columns_of(half)
    for k, ref in enumerate((acc, acc_span, accv)):
        ref[...] = jnp.zeros_like(ref) if first else olds[k][...]

    def add(row, values):
        accv[row : row + 1, : values.shape[1]] += jnp.sum(values, axis=0, keepdims=True)

    def body(i):
        rows = block_rows(i)
        low = lax.broadcasted_iota(jnp.int32, (SPAN, LANE), 1) < HEAD
        for s in range(ROWS // SPAN):
            at = block_rows(i * (ROWS // SPAN) + s, SPAN)
            to = slice(s * SPAN, (s + 1) * SPAN)
            for k in range(PAIRS // 2):
                p = half * (PAIRS // 2) + k
                cq, ck, cv = (slice(t * D + p * LANE, t * D + (p + 1) * LANE) for t in range(3))
                oq, ok, ov = (slice(t * wide + k * LANE, t * wide + (k + 1) * LANE) for t in range(3))
                n = (i * (ROWS // SPAN) + s) * PAIRS + p
                do = da_ref[at, cq]
                zero = jnp.zeros_like(do)
                do2 = jnp.concatenate([jnp.where(low, do, zero), jnp.where(low, zero, do)], axis=0)
                q2, kc, vc, w = q2_ref[n], kc_ref[n], vc_ref[n], p_ref[n]
                wf = w.astype(F32)
                dp = dot_bt(vc, do2)
                delta = jnp.sum(wf * dp, axis=0, keepdims=True)
                ds = (wf * (dp - delta)).astype(BF16)
                dq2 = dot_at(ds, kc)
                dq = jnp.where(low, dq2[:SPAN], dq2[SPAN:]) * SCALE
                dk = dot(ds, q2)
                dv = dot(w, do2)
                acc_span[:, oq] += dk[SPAN:]
                acc_span[:, ok] += dv[SPAN:]
                dp_ref[to, oq] = dq.astype(BF16)
                dp_ref[to, ok] = dk[:SPAN].astype(BF16)
                dp_ref[to, ov] = dv[:SPAN].astype(BF16)
        dpk = dp_ref[...]
        add(QB, dpk.astype(F32))
        acc[...] += dot_at(h1_ref[rows, :], dpk)
        dh1 = dot_bt(dpk[:, :wide], wqkv[:, columns[0]])
        for t in (1, 2):
            dh1 = dh1 + dot_bt(dpk[:, t * wide : (t + 1) * wide], wqkv[:, columns[t]])
        if half:
            dh1 = dh1 + before_ref[rows, :]
            n1, _ = normalize(x_ref[rows, :].astype(F32))
            add(G1, dh1 * n1)
            add(S1, dh1)
        dh1_ref[block_rows(i - start), :] = dh1

    blocks = dh1_ref.shape[0] // ROWS
    start = 0 if first else x_ref.shape[0] // ROWS - blocks
    each_block(blocks * ROWS, lambda i: body(i + start), parts=max(blocks // 2, 1))
    if not last:
        return

    span = acc_span[...]
    bit = sc[SC_C] & 1
    each = span.shape[0] // copies
    for k in range(copies):
        code = code_of(k, copies)
        part = span[k * each : (k + 1) * each]
        hold = jnp.concatenate(
            [part[:, t * LANE : (t + 1) * LANE] for t in range(2 * wide // LANE)], axis=0
        ).astype(BF16)
        to = slice(code % (copies // 2) * hold.shape[0], (code % (copies // 2) + 1) * hold.shape[0])
        mine = bit == code // (copies // 2)

        @pl.when(mine)
        def _():
            far_keep[to, :] = hold

        @pl.when(jnp.logical_not(mine))
        def _():
            far_send[to, :] = hold

    span = span * INV_ROOT
    low_span = span.astype(BF16)
    nsum = nsum_ref[...]
    hs = (nsum * vec[G1 : G1 + 1, :D] + SPAN * vec[S1 : S1 + 1, :D]).astype(BF16)
    acc[:, wide:] += dot_at(hs, low_span)
    accv[QB : QB + 1, wide : 3 * wide] += SPAN * jnp.sum(span, axis=0, keepdims=True)
    de = dot_bt(low_span[:, :wide], wqkv[:, columns[1]])
    de = de + dot_bt(low_span[:, wide:], wqkv[:, columns[2]])
    block = D // nf
    if half:
        de = de + sums_ref[: de.shape[0], :]
        add(G1, de * nsum)
        accv[S1 : S1 + 1, :D] += SPAN * jnp.sum(de, axis=0, keepdims=True)
        bias = sums_ref[de.shape[0] : de.shape[0] + 8, :]
    else:
        sum_ref[: de.shape[0], :] = de
        tail = [accv[QB : QB + 1, t * wide : (t + 1) * wide] for t in range(3)]
        bias = jnp.concatenate(tail + [jnp.zeros((5, wide), F32)], axis=0)
        sum_ref[de.shape[0] : de.shape[0] + 8, :] = jnp.concatenate([bias, bias], axis=1)

    for q in range(nf):
        ref = send_ref if q % 2 else keep_ref
        fq = sc[SC_F] ^ q
        at = pl.ds(pl.multiple_of(fq * block, block), block)
        base = 0
        pieces = [acc[at, :].astype(BF16)]
        if not half:
            pieces.append(gout_ref[at, :].astype(BF16))
        for piece in pieces:
            for j in range(piece.shape[1] // LANE):
                ref[q // 2, base : base + block, :] = piece[:, j * LANE : (j + 1) * LANE]
                base += block
        if half:
            whole = jnp.concatenate(
                [
                    part
                    for t in range(3)
                    for part in (bias[t : t + 1, :wide], accv[QB : QB + 1, t * wide : (t + 1) * wide])
                ],
                axis=1,
            )
            accv[QB + 1 : QB + 2, : 3 * D] = whole
            three = [
                accv[QB + 1 : QB + 2, pl.ds(pl.multiple_of((fq * 3 + t) * block, block), block)]
                for t in range(3)
            ]
            four = [
                dub_ref[0:1, pl.ds(pl.multiple_of((fq * 4 + t) * block, block), block)]
                for t in range(4)
            ]
            small = jnp.concatenate(
                [accv[G1 : G1 + 1, at], accv[S1 : S1 + 1, at]]
                + three
                + [gvec_ref[OB : OB + 1, at], gvec_ref[G2 : G2 + 1, at], gvec_ref[S2 : S2 + 1, at]]
                + four
                + [gvec_ref[DB : DB + 1, at], jnp.zeros((3, LANE), F32)],
                axis=0,
            ).astype(BF16)
            ref[q // 2, base : base + 16, :] = small
            base += 16
        left = ref.shape[1] - base
        if left:
            ref[q // 2, base:, :] = jnp.zeros((left, LANE), BF16)


def back(sc, fixed, more, half, nf, copies, old=None, last=True):
    x, nsum = fixed[0], fixed[-1]
    rows = x.shape[0] if last and old is None else x.shape[0] // 2
    nspan = nsum.shape[0]
    wide = PAIRS // 2 * LANE
    block = D // nf
    used = 3 * wide // LANE * block + (16 if half else D // LANE * block)
    piece = piece_rows(used, copies)
    far = nspan // 2 * 2 * wide // LANE
    sums = [((D, 3 * wide), F32), ((nspan, 2 * wide), F32), ((16, 3 * D), F32)]
    outs = [((rows, D), F32)]
    scratch = [pltpu.VMEM((ROWS, 3 * wide), BF16)]
    if last:
        scratch = [pltpu.VMEM(*a) for a in sums] + scratch
        outs += [((nspan + 8, D), F32)]
        outs += [((far, LANE), BF16)] * 2 + [((nf // 2, piece, LANE), BF16)] * 2
    else:
        outs += sums
    kernel = functools.partial(
        back_kernel, nf=nf, copies=copies, half=half, first=old is None, last=last
    )

    def ordered(*refs):
        if not last:
            return kernel(*refs)
        at = len(refs) - len(scratch)
        return kernel(
            *refs[: at - len(outs) + 1], *refs[at:-1], *refs[at - len(outs) + 1 : at], refs[-1]
        )

    arrays = (*fixed, *more, *(old or ()))
    return resident(ordered, f"back_{half}", 9, 18, (sc,), arrays, outs, scratch)


def first_kernel(x_ref, dr1_ref, upper_ref, lower_ref, own_ref, wqkv, vec, o_ref, e_ref):
    i = pl.program_id(0)
    spans = ROWS // SPAN

    @pl.when(i == 0)
    def _():
        each = e_ref.shape[0]
        wide = PAIRS // 2 * LANE
        total = jnp.zeros((each, D), F32)
        for half in range(2):
            for k, columns in enumerate(columns_of(half)[1:]):
                for t in range(wide // LANE):
                    row = ((half * 2 + k) * (wide // LANE) + t) * each
                    own = own_ref[row : row + each, :].astype(F32) * INV_ROOT
                    cols = slice(columns.start + t * LANE, columns.start + (t + 1) * LANE)
                    total = total + dot_bt(own.astype(BF16), wqkv[:, cols])
        e_ref[...] = total

    at = block_rows(i)
    n1, rstd1 = normalize(x_ref[at, :].astype(F32))
    extra = jnp.concatenate(
        [jnp.broadcast_to(e_ref[pl.ds(i * spans + s, 1), :], (SPAN, D)) for s in range(spans)],
        axis=0,
    )
    half = pl.num_programs(0) // 2

    def write(ref, k):
        dh1 = ref[block_rows(k), :] + extra
        o_ref[...] = dr1_ref[at, :] + norm_back(dh1 * vec[G1 : G1 + 1, :D], n1, rstd1)

    @pl.when(i < half)
    def _():
        write(upper_ref, i)

    @pl.when(i >= half)
    def _():
        write(lower_ref, i - half)


def first_back(x, dr1, upper, lower, own, wqkv, vec):
    rows = x.shape[0]
    return pl.pallas_call(
        first_kernel,
        grid=(rows // ROWS,),
        in_specs=in_vmem(7),
        out_specs=pl.BlockSpec((ROWS, D), lambda i: (i, 0)),
        out_shape=jax.ShapeDtypeStruct((rows, D), F32),
        scratch_shapes=[pltpu.VMEM((rows // SPAN, D), F32)],
        compiler_params=params(8),
        name="first_back",
        cost_estimate=cost(3),
    )(x, dr1, upper, lower, own, wqkv, vec)


def mixed_kernel(sc, r1_ref, g_ref, vec, *refs):
    w_refs, o_ref = refs[:-1], refs[-1]
    at = block_rows(pl.program_id(0))
    total = r1_ref[at, :] + vec[DB : DB + 1, :D]
    width = w_refs[0].shape[0]
    for q, w_ref in enumerate(w_refs):
        cols = pl.ds(pl.multiple_of((sc[SC_F] ^ q) * width, width), width)
        total = total + dot(g_ref[at, cols], w_ref[...])
    o_ref[...] = total.astype(BF16)


def block_output(sc, r1, g, vec, down):
    rows = r1.shape[0]
    return pl.pallas_call(
        mixed_kernel,
        grid=(rows // ROWS,),
        in_specs=[pl.BlockSpec(memory_space=pltpu.SMEM)] + in_vmem(3 + len(down)),
        out_specs=pl.BlockSpec((ROWS, D), lambda i: (i, 0)),
        out_shape=jax.ShapeDtypeStruct((rows, D), BF16),
        compiler_params=params(8),
        name="block_output",
        cost_estimate=cost(4),
    )(sc, r1, g, vec, *down)


def swap(array, axis, bit):
    n = lax.axis_size(axis)
    return lax.ppermute(array, axis, [(k, k ^ bit) for k in range(n)])


def after(array, *others):
    return lax.optimization_barrier((array, others))[0]


def first_gather(array, axis):
    return swap(array, axis, lax.axis_size(axis) // 2)


def gathered(array, far, axis):
    n = lax.axis_size(axis)
    bit = n // 2
    held = {0: array, bit: far}
    bit //= 2
    while bit:
        for r in sorted(held):
            held[r ^ bit] = swap(held[r], axis, bit)
        bit //= 2
    return [held[r] for r in range(n)]


def total_of(values):
    total = values[0].astype(F32)
    for value in values[1:]:
        total = total + value.astype(F32)
    return total.astype(BF16)


def fold_kernel(sc, *refs, bit, counts):
    own = lax.div(sc[SC_C], bit) & 1 if bit else 0
    arrays, (send_ref, own_ref) = refs[:-2], refs[-2:]
    at = 0
    for count in counts:
        group, arrays = arrays[:count], arrays[count:]
        a, _, h, _ = group[0].shape
        for ref, half in ((send_ref, 1 - own), (own_ref, own)):
            for k in range(a):
                ref[k, at : at + h, :] = total_of([g[k, half] for g in group])
        at += h


def fold(sc, bit, *groups, micros=1):
    a = groups[0][0].shape[0]
    h = sum(group[0].shape[2] for group in groups)
    arrays = [array for group in groups for array in group]
    counts = tuple(len(group) for group in groups)
    kernel = functools.partial(fold_kernel, bit=bit, counts=counts)
    return resident(kernel, "fold", micros, 8, (sc,), arrays, [((a, h, LANE), BF16)] * 2)


def quad_kernel(sc, keep_ref, got_ref, *refs, bit, beside):
    pairs, (own_ref, ctx_ref, near_ref, both_ref) = refs[:-4], refs[-4:]
    own = lax.div(sc[SC_C], bit) & 1
    at = keep_ref.shape[2]
    own_ref[:at, :] = total_of((keep_ref[0, own], got_ref[0, own]))
    ctx_ref[:at, :] = total_of((keep_ref[0, 1 - own], got_ref[0, 1 - own]))
    near_ref[:at, :] = total_of((keep_ref[1, own], got_ref[1, own]))
    both_ref[...] = total_of((keep_ref[1, 1 - own], got_ref[1, 1 - own]))
    ends = {True: at, False: at}
    for n, (kept, sent) in enumerate(zip(pairs[0::2], pairs[1::2])):
        rows = kept.shape[0]
        own_ref[at : at + rows, :] = kept[...]
        at += rows
        ref, end = (near_ref if n < beside else ctx_ref), ends[n < beside]
        ref[end : end + rows, :] = sent[...]
        ends[n < beside] += rows


def quad(sc, bit, keep, got, with_near, with_ctx):
    kernel = functools.partial(quad_kernel, bit=bit, beside=len(with_near))
    arrays = (keep, got, *(a for pair in (*with_near, *with_ctx) for a in pair))
    h = keep.shape[2]
    near = h + sum(kept.shape[0] for kept, _ in with_near)
    ctx = h + sum(kept.shape[0] for kept, _ in with_ctx)
    outs = [((n, LANE), BF16) for n in (near + ctx - h, ctx, near, h)]
    return resident(kernel, "quad", 1, 8, (sc,), arrays, outs)


def swap_both(array, ctx_bit, near_bit):
    n, nf = lax.axis_size("ctx"), lax.axis_size("fsdp")
    pairs = [
        (a * nf + b, (a ^ ctx_bit) * nf + (b ^ near_bit)) for a in range(n) for b in range(nf)
    ]
    return lax.ppermute(array, ("ctx", "fsdp"), pairs)


def refold_kernel(sc, *refs, bit, sizes, sources):
    arrays, (send_ref, own_ref) = refs[:-2], refs[-2:]
    own = lax.div(sc[SC_C], bit) & 1
    at = 0
    for h, source in zip(sizes, sources):
        for ref, half in ((send_ref, 1 - own), (own_ref, own)):
            values = [
                arrays[k][pl.ds(pl.multiple_of(base + half * h, 16), h), :] for k, base in source
            ]
            ref[at : at + h, :] = total_of(values)
        at += h


def refold(sc, bit, arrays, sizes, micros=1, sources=None):
    if sources is None:
        starts = [2 * sum(sizes[:n]) for n in range(len(sizes))]
        sources = [[(k, start) for k in range(len(arrays))] for start in starts]
    outs = [((sum(sizes), LANE), BF16)] * 2
    kernel = functools.partial(refold_kernel, bit=bit, sizes=sizes, sources=sources)
    return resident(kernel, "fold", micros, 8, (sc,), arrays, outs)


def last_kernel(keep_ref, got_ref, o_ref, *rest):
    used = o_ref.shape[0]
    total = keep_ref[:used, :].astype(F32) + got_ref[:used, :].astype(F32)
    o_ref[...] = total.astype(BF16)
    for ref in rest:
        total = keep_ref[used:, :].astype(F32) + got_ref[used:, :].astype(F32)
        ref[...] = total.astype(BF16)


def last_sum(keep, got, used):
    outs = [((used, LANE), BF16)]
    if used < keep.shape[0]:
        outs.append(((keep.shape[0] - used, LANE), BF16))
    return resident(last_kernel, "last", 1, 8, (), (keep, got), outs)


class Sequence:
    def __init__(self):
        self.last = ()

    def next(self, array):
        return after(array, *self.last) if self.last else array

    def made(self, *arrays):
        self.last = arrays


class Part:
    def __init__(self, sc, seq, keep, send):
        self.sc, self.seq, self.keep, self.send = sc, seq, keep, send
        self.count, self.rows = keep.shape[0], keep.shape[1]
        self.total = self.rows
        self.move("fsdp", 1)

    def move(self, axis, bit):
        self.gots = (swap(self.send, axis, bit),)

    def view(self, axis):
        if axis == "fsdp":
            self.count //= 2
            return 1, 2, self.count * self.rows, LANE
        self.rows //= 2
        return self.count, 2, self.rows, LANE

    def pair(self, axis):
        view = self.view(axis)
        return tuple(a.reshape(view) for a in (self.keep, *self.gots))

    def split(self, axis, bit, micros=1):
        keep, got = self.pair(axis)
        pair = (self.seq.next(keep), got)
        self.send, self.keep = fold(self.sc, bit if axis == "ctx" else 0, pair, micros=micros)
        self.seq.made(self.keep, self.send)

    def step(self, axis, bit, micros=1):
        self.split(axis, bit, micros)
        self.move(axis, bit)


def ctx_bits():
    n = lax.axis_size("ctx")
    return [1 << k for k in range(n.bit_length() - 1)]


def united(sc, seq, parts):
    groups = [part.pair("ctx") for part in parts]
    groups[0] = (seq.next(groups[0][0]), *groups[0][1:])
    sizes = [group[0].shape[2] for group in groups]
    return Union(sc, seq, [a[0] for a in fold(sc, ctx_bits()[1], *groups)], sizes, len(sizes))


class Union:
    def __init__(self, sc, seq, halves, sizes, few):
        self.sc, self.seq, self.sizes = sc, seq, sizes
        self.bits = ctx_bits()
        self.used = sum(sizes[:few]) * 2 // self.bits[-1]
        self.received(self.bits[1], *halves)
        self.at = 2

    def received(self, bit, send, keep):
        self.keep = keep
        self.seq.made(keep, send)
        self.got = swap(send, "ctx", bit)

    def more(self):
        return self.at < len(self.bits)

    def step(self, micros=1):
        bit = self.bits[self.at]
        self.at += 1
        self.sizes = [size // 2 for size in self.sizes]
        keep = self.seq.next(self.keep)
        self.received(bit, *refold(self.sc, bit, (keep, self.got), self.sizes, micros))

    def end(self):
        own, *rest = last_sum(self.seq.next(self.keep), self.got, self.used)
        self.received(self.bits[-1], own, own)
        self.at = len(self.bits) - 1
        return rest[0] if rest else None

    def gathering(self):
        return self.at > 0

    def join(self):
        both = jnp.concatenate([self.seq.next(self.keep), self.got], axis=0)
        self.at -= 1
        self.received(self.bits[self.at], both, both)

    def rows(self):
        both = jnp.concatenate([self.seq.next(self.keep), self.got], axis=0)
        return both.reshape(lax.axis_size("ctx"), -1, LANE)


def code_of(index, n):
    code = 0
    for k in range(n.bit_length() - 1):
        bit = index >> k if isinstance(index, int) else lax.div(index, 1 << k)
        code = 2 * code + (bit & 1)
    return code


def finish_kernel(sc, got_ref, *refs, heights, plan):
    outs, rows = refs[:-1], refs[-1]
    n = got_ref.shape[0]
    code = code_of(sc[SC_C], n)
    for k in range(n):
        at, base = 0, 0
        for height in heights:
            h = height // n
            to = pl.multiple_of(base + (code ^ k) * h, 16)
            rows[pl.ds(to, h), :] = got_ref[k, at : at + h, :].astype(F32)
            at, base = at + h, base + height
    for ref, places in zip(outs, plan):
        if len(ref.shape) == 1:
            for j, place in enumerate(places):
                ref[j * LANE : (j + 1) * LANE] = rows[place, :]
            continue
        height = ref.shape[0]
        for j, place in enumerate(places):
            ref[:, j * LANE : (j + 1) * LANE] = rows[place : place + height, :]


def finish(sc, got, heights, shapes, plan):
    return pl.pallas_call(
        functools.partial(finish_kernel, heights=heights, plan=plan),
        in_specs=[pl.BlockSpec(memory_space=pltpu.SMEM)] + in_vmem(1),
        out_shape=[jax.ShapeDtypeStruct(shape, F32) for shape in shapes],
        scratch_shapes=[pltpu.VMEM((sum(heights), LANE), F32)],
        compiler_params=params(16),
        name="finish",
        cost_estimate=cost(2),
    )(sc, got)


def local(
    tokens, ln1_gain, ln1_shift, qkv_weight, qkv_bias, out_weight, out_bias, ln2_gain, ln2_shift,
    up_weight, up_bias, down_weight, down_bias, seq_lengths, span_order, cotangent,
):
    nf = lax.axis_size("fsdp")
    nc = lax.axis_size("ctx")
    x, c = tokens[0], cotangent[0]
    spans = x.shape[0] // SPAN
    seqs = seq_lengths.shape[1]
    weights = packed_params(
        qkv_weight, out_weight,
        (ln1_gain, ln1_shift, qkv_bias, out_bias, ln2_gain, ln2_shift, up_bias, down_bias),
    )
    scalars = jnp.concatenate(
        [
            lax.axis_index("fsdp").reshape(1),
            lax.axis_index("ctx").reshape(1),
            (lax.axis_index("ctx") * spans).reshape(1),
            seq_lengths[0],
            span_order[0],
        ]
    ).astype(jnp.int32)
    far_weights = first_gather(weights, "fsdp")
    sums = span_sums(x, nc)
    nsum = lax.all_to_all(sums, "ctx", 0, 0, tiled=True).reshape(nc * spans, D)
    far_weights = after(far_weights, nsum)
    weights = gathered(weights, far_weights, "fsdp")
    up_weight = after(up_weight, far_weights)
    far_up = first_gather(up_weight, "fsdp")
    down_weight = after(down_weight, far_weights)
    far_down = first_gather(down_weight, "fsdp")

    packed, p, att, h1, wqkv, wout, vec, tabs = attend(
        scalars, x, span_order, nsum, weights, seqs
    )
    up = gathered(up_weight, after(far_up, att), "fsdp")
    r1, h2 = proj(x, att, wout, vec)
    g, gp, wup = ffn_up(scalars, h2, vec, up)
    dsend, dkeep = down_gradient(scalars, g, c, nf)
    down = gathered(down_weight, after(far_down, dkeep), "fsdp")
    queries, keys, values = tiles(after(packed, dkeep), tabs)
    gp = after(gp, queries)
    dh2, dub, usend, ukeep = ffn_down(scalars, h2, c, gp, wup, down)
    bits = ctx_bits()
    near = [("fsdp", 1 << k) for k in range(1, nf.bit_length() - 1)]

    seq = Sequence()
    from_down = Part(scalars, seq, dkeep, dsend)
    from_down.step(*near[0])
    dr1, da, gout, gvec = mid(c, seq.next(dh2), r1, att, wout, vec)
    seq.made(da)
    from_up = Part(scalars, seq, ukeep, usend)
    from_up.step("ctx", bits[0])
    da = seq.next(da)
    fixed = (x, da, h1, queries, keys, values, p, wqkv, vec, nsum)
    dh1, sums, fsend0, fkeep0, send, keep = back(scalars, fixed, (gout,), 0, nf, nc)
    seq.made(dh1)
    first = Part(scalars, seq, keep, send)
    from_down.step("ctx", bits[0])
    from_up.step(*near[0])
    dh1 = seq.next(dh1)
    upper, *old = back(scalars, fixed, (dub, gvec, dh1, sums), 1, nf, nc, last=False)
    seq.made(old[0])
    first.step("ctx", bits[0])
    feed = united(scalars, seq, [from_down, from_up])
    old[0] = seq.next(old[0])
    lower, _, fsend1, fkeep1, send, keep = back(
        scalars, fixed, (dub, gvec, dh1, sums), 1, nf, nc, old=old
    )
    seq.made(lower)
    second = Part(scalars, seq, keep, send)
    while feed.more():
        feed.step(FILL)
    first.split(*near[0], FILL)
    with_near = ((first.keep[0], first.send[0]),)
    with_ctx = ((fkeep0, fsend0), (fkeep1, fsend1))
    view = (2, 2, second.rows // 2, LANE)
    keep, got = (a.reshape(view) for a in (second.keep, *second.gots))
    own, to_ctx, to_near, to_both = quad(
        scalars, bits[0], seq.next(keep), got, with_near, with_ctx
    )
    seq.made(own)
    arrays = (
        own,
        swap(to_ctx, "ctx", bits[0]),
        swap(to_near, *near[0]),
        swap_both(to_both, bits[0], near[0][1]),
    )
    feed.end()
    heights = [second.total // 2] + [kept.shape[0] for kept, _ in (*with_near, *with_ctx)]
    sources, at, ends = [[(k, 0) for k in range(4)]], heights[0], {1: heights[0], 2: heights[0]}
    for n, rows in enumerate(heights[1:]):
        where = 2 if n < len(with_near) else 1
        sources.append([(0, at), (where, ends[where])])
        at += rows
        ends[where] += rows
    sizes = [rows // 2 for rows in heights]
    arrays = (seq.next(arrays[0]), *arrays[1:])
    halves = refold(scalars, bits[1], arrays, sizes, sources=sources)
    rest = Union(scalars, seq, halves, sizes, 2)
    mixed = block_output(scalars, seq.next(r1), g, vec, down)
    seq.made(mixed)
    while feed.at > 1:
        feed.join()
    while rest.more():
        rest.step()
    feed.join()
    own_span = rest.end()
    rest.join()
    tokens_grad = first_back(seq.next(x), dr1, upper, lower, own_span, wqkv, vec)
    seq.made(tokens_grad)
    while rest.gathering():
        rest.join()
    block = D // nf
    height, width = down_weight.shape[0], up_weight.shape[1]
    heights = (from_down.total, from_up.total)
    grad_down, grad_up = finish(
        scalars,
        feed.rows(),
        heights,
        [(height, D), (block, width)],
        [
            [height * j for j in range(D // LANE)],
            [heights[0] + block * j for j in range(width // LANE)],
        ],
    )
    seq.made(grad_down)
    half = PAIRS // 2
    plan = [
        [
            (second.total if p < half else 0) + block * (t * half + p % half)
            for t in range(3)
            for p in range(PAIRS)
        ],
        [second.total + block * (3 * half + j) for j in range(D // LANE)],
    ]
    shapes = [(block, 3 * D), (block, D)]
    at = 3 * half * block
    for wide in (block, block, 3 * block, block, block, block, 4 * block, block):
        shapes.append((wide,))
        plan.append([at + j for j in range(wide // LANE)])
        at += wide // LANE
    grad_qkv, grad_out, *vectors = finish(
        scalars, rest.rows(), (second.total, first.total), shapes, plan
    )
    g1, s1, qb, ob, g2, s2, ub, db = vectors
    return (
        mixed[None], tokens_grad[None], g1, s1, grad_qkv, qb, grad_out, ob, g2, s2,
        grad_up, ub, grad_down, db,
    )


def solution(mesh):
    rows, one, two = P("fsdp", "ctx", None), P("fsdp"), P("fsdp", None)
    return jax.shard_map(
        local,
        mesh=mesh,
        in_specs=(
            rows, one, one, two, one, two, one, one, one, two, one, two, one, two, two, rows,
        ),
        out_specs=(rows, rows, one, one, two, one, two, one, one, one, two, one, two, one),
        check_vma=False,
    )
```

```python
import functools

import jax
import jax.numpy as jnp
from jax import lax
from jax.experimental import pallas as pl
from jax.experimental.pallas import tpu as pltpu
from jax.sharding import PartitionSpec as P

D = 512
HEADS = 8
HEAD = 64
SPAN = 128
LANE = 128
PAIRS = D // LANE
ROWS = 256
EPSILON = 1e-05
MASKED = -1e30
SCALE = HEAD**-0.5
FILL = 3
INV_ROOT = SPAN**-0.5
F32 = jnp.float32
BF16 = jnp.bfloat16

G1, S1, OB, G2, S2, DB, QB, UB = range(8)
SC_F, SC_C, SC_SLOT, SC_LEN = range(4)


def dot(a, b):
    return lax.dot_general(a, b, (((1,), (0,)), ((), ())), preferred_element_type=F32)


def dot_bt(a, b):
    return lax.dot_general(a, b, (((1,), (1,)), ((), ())), preferred_element_type=F32)


def dot_at(a, b):
    return lax.dot_general(a, b, (((0,), (0,)), ((), ())), preferred_element_type=F32)


def normalize(values):
    centre = values - jnp.mean(values, axis=-1, keepdims=True)
    spread = jnp.mean(centre * centre, axis=-1, keepdims=True)
    rstd = lax.rsqrt(spread + EPSILON)
    return centre * rstd, rstd


def norm_back(e, n, rstd):
    return rstd * (
        e - jnp.mean(e, axis=-1, keepdims=True) - n * jnp.mean(e * n, axis=-1, keepdims=True)
    )


def params(mib):
    return pltpu.CompilerParams(vmem_limit_bytes=mib * 1024 * 1024)


def in_vmem(count):
    return [pl.BlockSpec(memory_space=pltpu.VMEM) for _ in range(count)]


def cost(micros):
    return pl.CostEstimate(
        flops=int(micros * 1e9), transcendentals=0, bytes_accessed=int(micros * 1e6)
    )


def resident(kernel, name, micros, mib, scalars, arrays, outs, scratch=()):
    return pl.pallas_call(
        kernel,
        in_specs=[pl.BlockSpec(memory_space=pltpu.SMEM)] * len(scalars) + in_vmem(len(arrays)),
        out_specs=in_vmem(len(outs)),
        out_shape=[jax.ShapeDtypeStruct(shape, dtype) for shape, dtype in outs],
        scratch_shapes=list(scratch),
        compiler_params=params(mib),
        name=name,
        cost_estimate=cost(micros),
    )(*scalars, *arrays)


def block_rows(i, size=ROWS):
    if isinstance(i, int):
        return slice(i * size, (i + 1) * size)
    return pl.ds(pl.multiple_of(i * size, size), size)


def each_block(rows, body, size=ROWS, parts=1):
    each = rows // size // parts
    if parts == 1:
        for i in range(each):
            body(i)
        return

    def step(n, carry):
        for k in range(each):
            body(n * each + k)
        return carry

    lax.fori_loop(0, parts, step, 0)


def sums_kernel(x_ref, o_ref):
    spans = x_ref.shape[0] // SPAN
    sums = []
    for s in range(spans):
        n, _ = normalize(x_ref[s * SPAN : (s + 1) * SPAN, :].astype(F32))
        sums.append(jnp.sum(n, axis=0, keepdims=True))
    table = jnp.concatenate(sums, axis=0)
    for k in range(o_ref.shape[0]):
        o_ref[k] = table


def span_sums(x, copies):
    spans = x.shape[0] // SPAN
    return resident(sums_kernel, "span_sums", 3, 16, (), (x,), [((copies, spans, D), F32)])[0]


def pack_kernel(qkv_ref, out_ref, *refs):
    o_ref = refs[-1]
    rows, width = qkv_ref.shape
    o_ref[:rows, :width] = qkv_ref[...]
    o_ref[:rows, width:] = out_ref[...]
    parts = [ref[...].astype(F32) for ref in refs[:-1]]
    used = sum(part.shape[0] for part in parts)
    parts.append(jnp.zeros((16 - used, LANE), F32))
    o_ref[rows:, :LANE] = jnp.concatenate(parts, axis=0).astype(BF16)
    o_ref[rows:, LANE:] = jnp.zeros((16, o_ref.shape[1] - LANE), BF16)


def packed_params(qkv, out, vectors):
    shape = (qkv.shape[0] + 16, qkv.shape[1] + out.shape[1])
    vectors = [v.reshape(-1, LANE) for v in vectors]
    arrays = [qkv, out] + vectors
    return pl.pallas_call(
        pack_kernel,
        out_specs=pl.BlockSpec(memory_space=pltpu.VMEM),
        out_shape=jax.ShapeDtypeStruct(shape, BF16),
        compiler_params=params(58),
        name="pack",
        cost_estimate=cost(1),
    )(*arrays)


def attend_kernel(sc, x_ref, order_ref, nsum_ref, *refs, nf, seqs):
    param_refs = refs[:nf]
    (packed_ref, p_ref, att_ref, h1_ref, wqkv, wout, vec, tabs) = refs[nf:]
    nspan = nsum_ref.shape[0]
    block = D // nf

    vec[...] = jnp.zeros_like(vec)
    for q in range(nf):
        fq = sc[SC_F] ^ q
        at = pl.ds(pl.multiple_of(fq * block, block), block)
        wqkv[at, :] = param_refs[q][:block, : 3 * D]
        wout[at, :] = param_refs[q][:block, 3 * D :]
        sm = param_refs[q][block:, :LANE].astype(F32)
        for row, src in ((G1, 0), (S1, 1), (OB, 5), (G2, 6), (S2, 7), (DB, 12)):
            vec[row : row + 1, at] = sm[src : src + 1]
        for t in range(3):
            at3 = pl.ds(pl.multiple_of(fq * 3 * block + t * block, block), block)
            vec[QB : QB + 1, at3] = sm[2 + t : 3 + t]
        for t in range(4):
            at4 = pl.ds(pl.multiple_of(fq * 4 * block + t * block, block), block)
            vec[UB : UB + 1, at4] = sm[8 + t : 9 + t]
    hs = nsum_ref[...] * vec[G1 : G1 + 1, :D] + SPAN * vec[S1 : S1 + 1, :D]
    hi = hs.astype(BF16)
    lo = (hs - hi.astype(F32)).astype(BF16)
    both = dot(jnp.concatenate([hi, lo], axis=0), wqkv[:, D:])
    t = both[:nspan] + both[nspan:] + SPAN * vec[QB : QB + 1, D : 3 * D]
    tabs[...] = (t * INV_ROOT).astype(BF16)
    prompt = lax.div(sc[SC_LEN], SPAN)
    spans = ROWS // SPAN

    def body(i):
        rows = block_rows(i)
        n1, _ = normalize(x_ref[rows, :].astype(F32))
        h1 = (n1 * vec[G1 : G1 + 1, :D] + vec[S1 : S1 + 1, :D]).astype(BF16)
        h1_ref[rows, :] = h1
        packed_ref[rows, :] = (dot(h1, wqkv[...]) + vec[QB : QB + 1, : 3 * D]).astype(BF16)

        lane = lax.broadcasted_iota(jnp.int32, (SPAN, LANE), 1)
        low = lane < HEAD
        causal = jnp.where(
            lane <= lax.broadcasted_iota(jnp.int32, (SPAN, LANE), 0), 0.0, MASKED
        ).astype(F32)
        order = order_ref[...]
        for s in range(spans):
            a = sc[SC_LEN + seqs + sc[SC_SLOT] + i * spans + s]
            start, begin = 0, 0
            for k in range(seqs):
                begin = jnp.where(start <= a, start, begin)
                start = start + lax.div(sc[SC_LEN + k], SPAN)
            seen = (order < a) & ((order >= begin) | (order < prompt))
            far = jnp.where(seen, 0.0, MASKED).astype(F32)
            bias = jnp.concatenate([causal, jnp.broadcast_to(far, (SPAN, nspan))], axis=1)
            bias = jnp.concatenate([bias, bias], axis=0)
            at = block_rows(i * spans + s, SPAN)
            for p in range(PAIRS):
                cq, ck, cv = (slice(t * D + p * LANE, t * D + (p + 1) * LANE) for t in range(3))
                q = packed_ref[at, cq] * SCALE
                zero = jnp.zeros_like(q)
                q2 = jnp.concatenate([jnp.where(low, q, zero), jnp.where(low, zero, q)], axis=0)
                kc = jnp.concatenate([packed_ref[at, ck], tabs[:, cq]], axis=0)
                vc = jnp.concatenate([packed_ref[at, cv], tabs[:, ck]], axis=0)
                scores = dot_bt(q2, kc) + bias
                peak = jnp.max(scores, axis=1, keepdims=True)
                e = jnp.exp(scores - peak)
                w = (e * (1.0 / jnp.sum(e, axis=1, keepdims=True))).astype(BF16)
                p_ref[(i * spans + s) * PAIRS + p, :SPAN] = w[:, :SPAN].T
                p_ref[(i * spans + s) * PAIRS + p, SPAN:] = w[:, SPAN:].T
                o2 = dot(w, vc)
                att_ref[at, cq] = jnp.where(low, o2[:SPAN], o2[SPAN:]).astype(BF16)

    each_block(x_ref.shape[0], body, parts=2)


def proj_kernel(x_ref, att_ref, wout, vec, r1_ref, h2_ref):
    def body(i):
        at = block_rows(i)
        r1 = x_ref[at, :].astype(F32) + (dot(att_ref[at, :], wout[...]) + vec[OB : OB + 1, :D])
        r1_ref[at, :] = r1
        n2, _ = normalize(r1)
        h2_ref[at, :] = (n2 * vec[G2 : G2 + 1, :D] + vec[S2 : S2 + 1, :D]).astype(BF16)

    each_block(x_ref.shape[0], body)


def proj(x, att, wout, vec):
    outs = [(x.shape, F32), (x.shape, BF16)]
    return resident(proj_kernel, "proj", 3, 8, (), (x, att, wout, vec), outs)


def attend(sc, x, order, nsum, weights, seqs):
    rows = x.shape[0]
    nspan = nsum.shape[0]
    outs = [
        ((rows, 3 * D), BF16),
        ((rows // SPAN * PAIRS, SPAN + nspan, 2 * SPAN), BF16),
        ((rows, D), BF16),
        ((rows, D), BF16),
        ((D, 3 * D), BF16),
        ((D, D), BF16),
        ((8, 4 * D), F32),
        ((nspan, 2 * D), BF16),
    ]
    kernel = functools.partial(attend_kernel, nf=len(weights), seqs=seqs)
    arrays = (x, order, nsum, *weights)
    return resident(kernel, "attend", 12, 12, (sc,), arrays, outs)


def relative(step, nf):
    half = nf // 2
    return jnp.where(step < half, 2 * step + 1, 2 * (step - half))


def up_kernel(sc, h2_ref, vec_ref, *refs, nf):
    up_refs = refs[:nf]
    g_ref, gp_ref, w_ref = refs[nf:]
    block = D // nf
    width = w_ref.shape[1] // nf
    k0 = 0.7978845608028654
    for q in range(nf):
        at = pl.ds(pl.multiple_of((sc[SC_F] ^ q) * block, block), block)
        w_ref[at, :] = up_refs[q][...]
    rows = h2_ref.shape[0]

    def body(j):
        cols = pl.ds(pl.multiple_of(j * width, width), width)
        for i in range(rows // ROWS):
            at = block_rows(i)
            u = dot(h2_ref[at, :], w_ref[:, cols]) + vec_ref[UB : UB + 1, cols]
            u2 = u * u
            t = jnp.tanh(u * (k0 + (k0 * 0.044715) * u2))
            half = 0.5 + 0.5 * t
            g_ref[at, cols] = (u * half).astype(BF16)
            slope = u * (k0 + (3 * k0 * 0.044715) * u2)
            gp_ref[at, cols] = (half + (0.5 - 0.5 * t * t) * slope).astype(BF16)

    each_block(nf, body, 1, parts=2)


def ffn_up(sc, h2, vec, up):
    rows, ff = h2.shape[0], up[0].shape[1]
    outs = [((rows, ff), BF16), ((rows, ff), BF16), ((D, ff), BF16)]
    kernel = functools.partial(up_kernel, nf=len(up))
    return resident(kernel, "ffn_up", 8, 12, (sc,), (h2, vec, *up), outs)


def down_grad_kernel(sc, g_ref, c_ref, send_ref, keep_ref, *, nf):
    width = g_ref.shape[1] // nf
    for q in range(nf):
        at = pl.ds(pl.multiple_of((sc[SC_F] ^ q) * width, width), width)
        grad = dot_at(g_ref[:, at], c_ref[...]).astype(BF16)
        ref = send_ref if q % 2 else keep_ref
        for j in range(D // LANE):
            ref[q // 2, j * width : (j + 1) * width, :] = grad[:, j * LANE : (j + 1) * LANE]


def down_gradient(sc, g, c, nf):
    piece = g.shape[1] // nf * D // LANE
    outs = [((nf // 2, piece, LANE), BF16)] * 2
    kernel = functools.partial(down_grad_kernel, nf=nf)
    return resident(kernel, "down_grad", 4, 12, (sc,), (g, c), outs)


def down_kernel(sc, h2_ref, c_ref, gp_ref, w_ref, *refs, nf):
    down_refs = refs[:nf]
    dh2_ref, dub_ref, send_ref, keep_ref, du_ref, grad_ref = refs[nf:]
    width = w_ref.shape[1] // nf
    block = D // nf
    rows = h2_ref.shape[0]
    for s in range(nf):
        f = sc[SC_F] ^ s
        cols = pl.ds(pl.multiple_of(f * width, width), width)
        dub_ref[:, cols] = jnp.zeros((1, width), F32)

        def body(i):
            at = block_rows(i, 2 * ROWS)
            dg = dot_bt(c_ref[at, :], down_refs[s][...])
            du = (dg * gp_ref[at, cols].astype(F32)).astype(BF16)
            du_ref[at, :] = du
            dub_ref[:, cols] += jnp.sum(du.astype(F32), axis=0, keepdims=True)
            dh2 = dot_bt(du, w_ref[:, cols])
            if s == 0:
                dh2_ref[at, :] = dh2
            else:
                dh2_ref[at, :] += dh2

        each_block(rows, body, 2 * ROWS)
        grad_ref[...] = dot_at(h2_ref[...], du_ref[...])
        for q in range(nf):
            ref = send_ref if q % 2 else keep_ref
            piece = grad_ref[pl.ds(pl.multiple_of((sc[SC_F] ^ q) * block, block), block), :]
            piece = piece.astype(BF16)
            for j in range(width // LANE):
                to = pl.multiple_of((f * (width // LANE) + j) * block, block)
                ref[q // 2, pl.ds(to, block), :] = piece[:, j * LANE : (j + 1) * LANE]


def ffn_down(sc, h2, c, gp, w, down):
    nf = len(down)
    rows = h2.shape[0]
    ff = w.shape[1]
    piece = ff // LANE * (D // nf)
    outs = [((rows, D), F32), ((1, ff), F32)] + [((nf // 2, piece, LANE), BF16)] * 2
    scratch = [pltpu.VMEM((rows, ff // nf), BF16), pltpu.VMEM((D, ff // nf), F32)]
    kernel = functools.partial(down_kernel, nf=nf)
    arrays = (h2, c, gp, w, *down)
    return resident(kernel, "ffn_down", 8, 14, (sc,), arrays, outs, scratch)


def mid_kernel(c_ref, dh2_ref, r1_ref, att_ref, wout, vec, dr1_ref, da_ref, gout_ref, gvec_ref):
    gout_ref[...] = jnp.zeros_like(gout_ref)
    gvec_ref[...] = jnp.zeros_like(gvec_ref)

    def add(row, values):
        gvec_ref[row : row + 1, :] += jnp.sum(values, axis=0, keepdims=True)

    def body(i):
        at = block_rows(i)
        c = c_ref[at, :].astype(F32)
        dh2 = dh2_ref[at, :]
        n2, rstd2 = normalize(r1_ref[at, :])
        add(G2, dh2 * n2)
        add(S2, dh2)
        add(DB, c)
        dr1 = c + norm_back(dh2 * vec[G2 : G2 + 1, :D], n2, rstd2)
        dr1_ref[at, :] = dr1
        dy = dr1.astype(BF16)
        add(OB, dy.astype(F32))
        gout_ref[...] += dot_at(att_ref[at, :], dy)
        da_ref[at, :] = dot_bt(dy, wout[...]).astype(BF16)

    each_block(c_ref.shape[0], body)


def mid(c, dh2, r1, att, wout, vec):
    rows = c.shape[0]
    outs = [((rows, D), F32), ((rows, D), BF16), ((D, D), F32), ((8, D), F32)]
    return resident(mid_kernel, "mid", 5, 12, (), (c, dh2, r1, att, wout, vec), outs)


def tiles_kernel(packed_ref, tabs, q2_ref, kc_ref, vc_ref):
    low = lax.broadcasted_iota(jnp.int32, (SPAN, LANE), 1) < HEAD

    def body(i):
        at = block_rows(i, SPAN)
        for p in range(PAIRS):
            cq, ck, cv = (slice(t * D + p * LANE, t * D + (p + 1) * LANE) for t in range(3))
            n = i * PAIRS + p
            q = packed_ref[at, cq] * SCALE
            zero = jnp.zeros_like(q)
            q2_ref[n, :SPAN] = jnp.where(low, q, zero)
            q2_ref[n, SPAN:] = jnp.where(low, zero, q)
            kc_ref[n, :SPAN] = packed_ref[at, ck]
            kc_ref[n, SPAN:] = tabs[:, cq]
            vc_ref[n, :SPAN] = packed_ref[at, cv]
            vc_ref[n, SPAN:] = tabs[:, ck]

    spans = packed_ref.shape[0] // SPAN
    each_block(spans, body, 1, parts=spans // 2)


def tiles(packed, tabs):
    n = packed.shape[0] // SPAN * PAIRS
    keys = SPAN + tabs.shape[0]
    outs = [((n, 2 * SPAN, LANE), BF16)] + [((n, keys, LANE), BF16)] * 2
    return resident(tiles_kernel, "tiles", 1, 8, (), (packed, tabs), outs)


def piece_rows(used, parts):
    return -(-used // (16 * parts)) * 16 * parts


def columns_of(half):
    wide = PAIRS // 2 * LANE
    return [slice(t * D + half * wide, t * D + (half + 1) * wide) for t in range(3)]


def back_kernel(sc, x_ref, da_ref, h1_ref, q2_ref, kc_ref, vc_ref, p_ref, wqkv, vec, nsum_ref, *refs, nf, copies, half, first, last):
    if half:
        (dub_ref, gvec_ref, before_ref, sums_ref), refs = refs[:4], refs[4:]
    else:
        (gout_ref,), refs = refs[:1], refs[1:]
    olds, refs = ((), refs) if first else (refs[:3], refs[3:])
    (dh1_ref, acc, acc_span, accv), refs = refs[:4], refs[4:]
    if last:
        (sum_ref, far_send, far_keep, send_ref, keep_ref), refs = refs[:5], refs[5:]
    (dp_ref,) = refs
    wide = PAIRS // 2 * LANE
    columns = columns_of(half)
    for k, ref in enumerate((acc, acc_span, accv)):
        ref[...] = jnp.zeros_like(ref) if first else olds[k][...]

    def add(row, values):
        accv[row : row + 1, : values.shape[1]] += jnp.sum(values, axis=0, keepdims=True)

    def body(i):
        rows = block_rows(i)
        low = lax.broadcasted_iota(jnp.int32, (SPAN, LANE), 1) < HEAD
        for s in range(ROWS // SPAN):
            at = block_rows(i * (ROWS // SPAN) + s, SPAN)
            to = slice(s * SPAN, (s + 1) * SPAN)
            for k in range(PAIRS // 2):
                p = half * (PAIRS // 2) + k
                cq, ck, cv = (slice(t * D + p * LANE, t * D + (p + 1) * LANE) for t in range(3))
                oq, ok, ov = (slice(t * wide + k * LANE, t * wide + (k + 1) * LANE) for t in range(3))
                n = (i * (ROWS // SPAN) + s) * PAIRS + p
                do = da_ref[at, cq]
                zero = jnp.zeros_like(do)
                do2 = jnp.concatenate([jnp.where(low, do, zero), jnp.where(low, zero, do)], axis=0)
                q2, kc, vc, w = q2_ref[n], kc_ref[n], vc_ref[n], p_ref[n]
                wf = w.astype(F32)
                dp = dot_bt(vc, do2)
                delta = jnp.sum(wf * dp, axis=0, keepdims=True)
                ds = (wf * (dp - delta)).astype(BF16)
                dq2 = dot_at(ds, kc)
                dq = jnp.where(low, dq2[:SPAN], dq2[SPAN:]) * SCALE
                dk = dot(ds, q2)
                dv = dot(w, do2)
                acc_span[:, oq] += dk[SPAN:]
                acc_span[:, ok] += dv[SPAN:]
                dp_ref[to, oq] = dq.astype(BF16)
                dp_ref[to, ok] = dk[:SPAN].astype(BF16)
                dp_ref[to, ov] = dv[:SPAN].astype(BF16)
        dpk = dp_ref[...]
        add(QB, dpk.astype(F32))
        acc[...] += dot_at(h1_ref[rows, :], dpk)
        dh1 = dot_bt(dpk[:, :wide], wqkv[:, columns[0]])
        for t in (1, 2):
            dh1 = dh1 + dot_bt(dpk[:, t * wide : (t + 1) * wide], wqkv[:, columns[t]])
        if half:
            dh1 = dh1 + before_ref[rows, :]
            n1, _ = normalize(x_ref[rows, :].astype(F32))
            add(G1, dh1 * n1)
            add(S1, dh1)
        dh1_ref[block_rows(i - start), :] = dh1

    blocks = dh1_ref.shape[0] // ROWS
    start = 0 if first else x_ref.shape[0] // ROWS - blocks
    each_block(blocks * ROWS, lambda i: body(i + start), parts=max(blocks // 2, 1))
    if not last:
        return

    span = acc_span[...]
    bit = sc[SC_C] & 1
    each = span.shape[0] // copies
    for k in range(copies):
        code = code_of(k, copies)
        part = span[k * each : (k + 1) * each]
        hold = jnp.concatenate(
            [part[:, t * LANE : (t + 1) * LANE] for t in range(2 * wide // LANE)], axis=0
        ).astype(BF16)
        to = slice(code % (copies // 2) * hold.shape[0], (code % (copies // 2) + 1) * hold.shape[0])
        mine = bit == code // (copies // 2)

        @pl.when(mine)
        def _():
            far_keep[to, :] = hold

        @pl.when(jnp.logical_not(mine))
        def _():
            far_send[to, :] = hold

    span = span * INV_ROOT
    low_span = span.astype(BF16)
    nsum = nsum_ref[...]
    hs = (nsum * vec[G1 : G1 + 1, :D] + SPAN * vec[S1 : S1 + 1, :D]).astype(BF16)
    acc[:, wide:] += dot_at(hs, low_span)
    accv[QB : QB + 1, wide : 3 * wide] += SPAN * jnp.sum(span, axis=0, keepdims=True)
    de = dot_bt(low_span[:, :wide], wqkv[:, columns[1]])
    de = de + dot_bt(low_span[:, wide:], wqkv[:, columns[2]])
    block = D // nf
    if half:
        de = de + sums_ref[: de.shape[0], :]
        add(G1, de * nsum)
        accv[S1 : S1 + 1, :D] += SPAN * jnp.sum(de, axis=0, keepdims=True)
        bias = sums_ref[de.shape[0] : de.shape[0] + 8, :]
    else:
        sum_ref[: de.shape[0], :] = de
        tail = [accv[QB : QB + 1, t * wide : (t + 1) * wide] for t in range(3)]
        bias = jnp.concatenate(tail + [jnp.zeros((5, wide), F32)], axis=0)
        sum_ref[de.shape[0] : de.shape[0] + 8, :] = jnp.concatenate([bias, bias], axis=1)

    for q in range(nf):
        ref = send_ref if q % 2 else keep_ref
        fq = sc[SC_F] ^ q
        at = pl.ds(pl.multiple_of(fq * block, block), block)
        base = 0
        pieces = [acc[at, :].astype(BF16)]
        if not half:
            pieces.append(gout_ref[at, :].astype(BF16))
        for piece in pieces:
            for j in range(piece.shape[1] // LANE):
                ref[q // 2, base : base + block, :] = piece[:, j * LANE : (j + 1) * LANE]
                base += block
        if half:
            whole = jnp.concatenate(
                [
                    part
                    for t in range(3)
                    for part in (bias[t : t + 1, :wide], accv[QB : QB + 1, t * wide : (t + 1) * wide])
                ],
                axis=1,
            )
            accv[QB + 1 : QB + 2, : 3 * D] = whole
            three = [
                accv[QB + 1 : QB + 2, pl.ds(pl.multiple_of((fq * 3 + t) * block, block), block)]
                for t in range(3)
            ]
            four = [
                dub_ref[0:1, pl.ds(pl.multiple_of((fq * 4 + t) * block, block), block)]
                for t in range(4)
            ]
            small = jnp.concatenate(
                [accv[G1 : G1 + 1, at], accv[S1 : S1 + 1, at]]
                + three
                + [gvec_ref[OB : OB + 1, at], gvec_ref[G2 : G2 + 1, at], gvec_ref[S2 : S2 + 1, at]]
                + four
                + [gvec_ref[DB : DB + 1, at], jnp.zeros((3, LANE), F32)],
                axis=0,
            ).astype(BF16)
            ref[q // 2, base : base + 16, :] = small
            base += 16
        left = ref.shape[1] - base
        if left:
            ref[q // 2, base:, :] = jnp.zeros((left, LANE), BF16)


def back(sc, fixed, more, half, nf, copies, old=None, last=True):
    x, nsum = fixed[0], fixed[-1]
    rows = x.shape[0] if last and old is None else x.shape[0] // 2
    nspan = nsum.shape[0]
    wide = PAIRS // 2 * LANE
    block = D // nf
    used = 3 * wide // LANE * block + (16 if half else D // LANE * block)
    piece = piece_rows(used, copies)
    far = nspan // 2 * 2 * wide // LANE
    sums = [((D, 3 * wide), F32), ((nspan, 2 * wide), F32), ((16, 3 * D), F32)]
    outs = [((rows, D), F32)]
    scratch = [pltpu.VMEM((ROWS, 3 * wide), BF16)]
    if last:
        scratch = [pltpu.VMEM(*a) for a in sums] + scratch
        outs += [((nspan + 8, D), F32)]
        outs += [((far, LANE), BF16)] * 2 + [((nf // 2, piece, LANE), BF16)] * 2
    else:
        outs += sums
    kernel = functools.partial(
        back_kernel, nf=nf, copies=copies, half=half, first=old is None, last=last
    )

    def ordered(*refs):
        if not last:
            return kernel(*refs)
        at = len(refs) - len(scratch)
        return kernel(
            *refs[: at - len(outs) + 1], *refs[at:-1], *refs[at - len(outs) + 1 : at], refs[-1]
        )

    arrays = (*fixed, *more, *(old or ()))
    return resident(ordered, f"back_{half}", 9, 18, (sc,), arrays, outs, scratch)


def first_kernel(x_ref, dr1_ref, upper_ref, lower_ref, own_ref, wqkv, vec, o_ref, e_ref):
    i = pl.program_id(0)
    spans = ROWS // SPAN

    @pl.when(i == 0)
    def _():
        each = e_ref.shape[0]
        wide = PAIRS // 2 * LANE
        total = jnp.zeros((each, D), F32)
        for half in range(2):
            for k, columns in enumerate(columns_of(half)[1:]):
                for t in range(wide // LANE):
                    row = ((half * 2 + k) * (wide // LANE) + t) * each
                    own = own_ref[row : row + each, :].astype(F32) * INV_ROOT
                    cols = slice(columns.start + t * LANE, columns.start + (t + 1) * LANE)
                    total = total + dot_bt(own.astype(BF16), wqkv[:, cols])
        e_ref[...] = total

    at = block_rows(i)
    n1, rstd1 = normalize(x_ref[at, :].astype(F32))
    extra = jnp.concatenate(
        [jnp.broadcast_to(e_ref[pl.ds(i * spans + s, 1), :], (SPAN, D)) for s in range(spans)],
        axis=0,
    )
    half = pl.num_programs(0) // 2

    def write(ref, k):
        dh1 = ref[block_rows(k), :] + extra
        o_ref[...] = dr1_ref[at, :] + norm_back(dh1 * vec[G1 : G1 + 1, :D], n1, rstd1)

    @pl.when(i < half)
    def _():
        write(upper_ref, i)

    @pl.when(i >= half)
    def _():
        write(lower_ref, i - half)


def first_back(x, dr1, upper, lower, own, wqkv, vec):
    rows = x.shape[0]
    return pl.pallas_call(
        first_kernel,
        grid=(rows // ROWS,),
        in_specs=in_vmem(7),
        out_specs=pl.BlockSpec((ROWS, D), lambda i: (i, 0)),
        out_shape=jax.ShapeDtypeStruct((rows, D), F32),
        scratch_shapes=[pltpu.VMEM((rows // SPAN, D), F32)],
        compiler_params=params(8),
        name="first_back",
        cost_estimate=cost(3),
    )(x, dr1, upper, lower, own, wqkv, vec)


def mixed_kernel(sc, r1_ref, g_ref, vec, *refs):
    w_refs, o_ref = refs[:-1], refs[-1]
    at = block_rows(pl.program_id(0))
    total = r1_ref[at, :] + vec[DB : DB + 1, :D]
    width = w_refs[0].shape[0]
    for q, w_ref in enumerate(w_refs):
        cols = pl.ds(pl.multiple_of((sc[SC_F] ^ q) * width, width), width)
        total = total + dot(g_ref[at, cols], w_ref[...])
    o_ref[...] = total.astype(BF16)


def block_output(sc, r1, g, vec, down):
    rows = r1.shape[0]
    return pl.pallas_call(
        mixed_kernel,
        grid=(rows // ROWS,),
        in_specs=[pl.BlockSpec(memory_space=pltpu.SMEM)] + in_vmem(3 + len(down)),
        out_specs=pl.BlockSpec((ROWS, D), lambda i: (i, 0)),
        out_shape=jax.ShapeDtypeStruct((rows, D), BF16),
        compiler_params=params(8),
        name="block_output",
        cost_estimate=cost(4),
    )(sc, r1, g, vec, *down)


def swap(array, axis, bit):
    n = lax.axis_size(axis)
    return lax.ppermute(array, axis, [(k, k ^ bit) for k in range(n)])


def after(array, *others):
    return lax.optimization_barrier((array, others))[0]


def first_gather(array, axis):
    return swap(array, axis, lax.axis_size(axis) // 2)


def gathered(array, far, axis):
    n = lax.axis_size(axis)
    bit = n // 2
    held = {0: array, bit: far}
    bit //= 2
    while bit:
        for r in sorted(held):
            held[r ^ bit] = swap(held[r], axis, bit)
        bit //= 2
    return [held[r] for r in range(n)]


def total_of(values):
    total = values[0].astype(F32)
    for value in values[1:]:
        total = total + value.astype(F32)
    return total.astype(BF16)


def fold_kernel(sc, *refs, bit, counts):
    own = lax.div(sc[SC_C], bit) & 1 if bit else 0
    arrays, (send_ref, own_ref) = refs[:-2], refs[-2:]
    at = 0
    for count in counts:
        group, arrays = arrays[:count], arrays[count:]
        a, _, h, _ = group[0].shape
        for ref, half in ((send_ref, 1 - own), (own_ref, own)):
            for k in range(a):
                ref[k, at : at + h, :] = total_of([g[k, half] for g in group])
        at += h


def fold(sc, bit, *groups, micros=1):
    a = groups[0][0].shape[0]
    h = sum(group[0].shape[2] for group in groups)
    arrays = [array for group in groups for array in group]
    counts = tuple(len(group) for group in groups)
    kernel = functools.partial(fold_kernel, bit=bit, counts=counts)
    return resident(kernel, "fold", micros, 8, (sc,), arrays, [((a, h, LANE), BF16)] * 2)


def quad_kernel(sc, keep_ref, got_ref, *refs, bit, beside):
    pairs, (own_ref, ctx_ref, near_ref, both_ref) = refs[:-4], refs[-4:]
    own = lax.div(sc[SC_C], bit) & 1
    at = keep_ref.shape[2]
    own_ref[:at, :] = total_of((keep_ref[0, own], got_ref[0, own]))
    ctx_ref[:at, :] = total_of((keep_ref[0, 1 - own], got_ref[0, 1 - own]))
    near_ref[:at, :] = total_of((keep_ref[1, own], got_ref[1, own]))
    both_ref[...] = total_of((keep_ref[1, 1 - own], got_ref[1, 1 - own]))
    ends = {True: at, False: at}
    for n, (kept, sent) in enumerate(zip(pairs[0::2], pairs[1::2])):
        rows = kept.shape[0]
        own_ref[at : at + rows, :] = kept[...]
        at += rows
        ref, end = (near_ref if n < beside else ctx_ref), ends[n < beside]
        ref[end : end + rows, :] = sent[...]
        ends[n < beside] += rows


def quad(sc, bit, keep, got, with_near, with_ctx):
    kernel = functools.partial(quad_kernel, bit=bit, beside=len(with_near))
    arrays = (keep, got, *(a for pair in (*with_near, *with_ctx) for a in pair))
    h = keep.shape[2]
    near = h + sum(kept.shape[0] for kept, _ in with_near)
    ctx = h + sum(kept.shape[0] for kept, _ in with_ctx)
    outs = [((n, LANE), BF16) for n in (near + ctx - h, ctx, near, h)]
    return resident(kernel, "quad", 1, 8, (sc,), arrays, outs)


def swap_both(array, ctx_bit, near_bit):
    n, nf = lax.axis_size("ctx"), lax.axis_size("fsdp")
    pairs = [
        (a * nf + b, (a ^ ctx_bit) * nf + (b ^ near_bit)) for a in range(n) for b in range(nf)
    ]
    return lax.ppermute(array, ("ctx", "fsdp"), pairs)


def refold_kernel(sc, *refs, bit, sizes, sources):
    arrays, (send_ref, own_ref) = refs[:-2], refs[-2:]
    own = lax.div(sc[SC_C], bit) & 1
    at = 0
    for h, source in zip(sizes, sources):
        for ref, half in ((send_ref, 1 - own), (own_ref, own)):
            values = [
                arrays[k][pl.ds(pl.multiple_of(base + half * h, 16), h), :] for k, base in source
            ]
            ref[at : at + h, :] = total_of(values)
        at += h


def refold(sc, bit, arrays, sizes, micros=1, sources=None):
    if sources is None:
        starts = [2 * sum(sizes[:n]) for n in range(len(sizes))]
        sources = [[(k, start) for k in range(len(arrays))] for start in starts]
    outs = [((sum(sizes), LANE), BF16)] * 2
    kernel = functools.partial(refold_kernel, bit=bit, sizes=sizes, sources=sources)
    return resident(kernel, "fold", micros, 8, (sc,), arrays, outs)


def last_kernel(keep_ref, got_ref, o_ref, *rest):
    used = o_ref.shape[0]
    total = keep_ref[:used, :].astype(F32) + got_ref[:used, :].astype(F32)
    o_ref[...] = total.astype(BF16)
    for ref in rest:
        total = keep_ref[used:, :].astype(F32) + got_ref[used:, :].astype(F32)
        ref[...] = total.astype(BF16)


def last_sum(keep, got, used):
    outs = [((used, LANE), BF16)]
    if used < keep.shape[0]:
        outs.append(((keep.shape[0] - used, LANE), BF16))
    return resident(last_kernel, "last", 1, 8, (), (keep, got), outs)


class Sequence:
    def __init__(self):
        self.last = ()

    def next(self, array):
        return after(array, *self.last) if self.last else array

    def made(self, *arrays):
        self.last = arrays


class Part:
    def __init__(self, sc, seq, keep, send):
        self.sc, self.seq, self.keep, self.send = sc, seq, keep, send
        self.count, self.rows = keep.shape[0], keep.shape[1]
        self.total = self.rows
        self.move("fsdp", 1)

    def move(self, axis, bit):
        self.gots = (swap(self.send, axis, bit),)

    def view(self, axis):
        if axis == "fsdp":
            self.count //= 2
            return 1, 2, self.count * self.rows, LANE
        self.rows //= 2
        return self.count, 2, self.rows, LANE

    def pair(self, axis):
        view = self.view(axis)
        return tuple(a.reshape(view) for a in (self.keep, *self.gots))

    def split(self, axis, bit, micros=1):
        keep, got = self.pair(axis)
        pair = (self.seq.next(keep), got)
        self.send, self.keep = fold(self.sc, bit if axis == "ctx" else 0, pair, micros=micros)
        self.seq.made(self.keep, self.send)

    def step(self, axis, bit, micros=1):
        self.split(axis, bit, micros)
        self.move(axis, bit)


def ctx_bits():
    n = lax.axis_size("ctx")
    return [1 << k for k in range(n.bit_length() - 1)]


def united(sc, seq, parts):
    groups = [part.pair("ctx") for part in parts]
    groups[0] = (seq.next(groups[0][0]), *groups[0][1:])
    sizes = [group[0].shape[2] for group in groups]
    return Union(sc, seq, [a[0] for a in fold(sc, ctx_bits()[1], *groups)], sizes, len(sizes))


class Union:
    def __init__(self, sc, seq, halves, sizes, few):
        self.sc, self.seq, self.sizes = sc, seq, sizes
        self.bits = ctx_bits()
        self.used = sum(sizes[:few]) * 2 // self.bits[-1]
        self.received(self.bits[1], *halves)
        self.at = 2

    def received(self, bit, send, keep):
        self.keep = keep
        self.seq.made(keep, send)
        self.got = swap(send, "ctx", bit)

    def more(self):
        return self.at < len(self.bits)

    def step(self, micros=1):
        bit = self.bits[self.at]
        self.at += 1
        self.sizes = [size // 2 for size in self.sizes]
        keep = self.seq.next(self.keep)
        self.received(bit, *refold(self.sc, bit, (keep, self.got), self.sizes, micros))

    def end(self):
        own, *rest = last_sum(self.seq.next(self.keep), self.got, self.used)
        self.received(self.bits[-1], own, own)
        self.at = len(self.bits) - 1
        return rest[0] if rest else None

    def gathering(self):
        return self.at > 0

    def join(self):
        both = jnp.concatenate([self.seq.next(self.keep), self.got], axis=0)
        self.at -= 1
        self.received(self.bits[self.at], both, both)

    def rows(self):
        both = jnp.concatenate([self.seq.next(self.keep), self.got], axis=0)
        return both.reshape(lax.axis_size("ctx"), -1, LANE)


def code_of(index, n):
    code = 0
    for k in range(n.bit_length() - 1):
        bit = index >> k if isinstance(index, int) else lax.div(index, 1 << k)
        code = 2 * code + (bit & 1)
    return code


def finish_kernel(sc, got_ref, *refs, heights, plan):
    outs, rows = refs[:-1], refs[-1]
    n = got_ref.shape[0]
    code = code_of(sc[SC_C], n)
    for k in range(n):
        at, base = 0, 0
        for height in heights:
            h = height // n
            to = pl.multiple_of(base + (code ^ k) * h, 16)
            rows[pl.ds(to, h), :] = got_ref[k, at : at + h, :].astype(F32)
            at, base = at + h, base + height
    for ref, places in zip(outs, plan):
        if len(ref.shape) == 1:
            for j, place in enumerate(places):
                ref[j * LANE : (j + 1) * LANE] = rows[place, :]
            continue
        height = ref.shape[0]
        for j, place in enumerate(places):
            ref[:, j * LANE : (j + 1) * LANE] = rows[place : place + height, :]


def finish(sc, got, heights, shapes, plan):
    return pl.pallas_call(
        functools.partial(finish_kernel, heights=heights, plan=plan),
        in_specs=[pl.BlockSpec(memory_space=pltpu.SMEM)] + in_vmem(1),
        out_shape=[jax.ShapeDtypeStruct(shape, F32) for shape in shapes],
        scratch_shapes=[pltpu.VMEM((sum(heights), LANE), F32)],
        compiler_params=params(16),
        name="finish",
        cost_estimate=cost(2),
    )(sc, got)


def local(
    tokens, ln1_gain, ln1_shift, qkv_weight, qkv_bias, out_weight, out_bias, ln2_gain, ln2_shift,
    up_weight, up_bias, down_weight, down_bias, seq_lengths, span_order, cotangent,
):
    nf = lax.axis_size("fsdp")
    nc = lax.axis_size("ctx")
    x, c = tokens[0], cotangent[0]
    spans = x.shape[0] // SPAN
    seqs = seq_lengths.shape[1]
    weights = packed_params(
        qkv_weight, out_weight,
        (ln1_gain, ln1_shift, qkv_bias, out_bias, ln2_gain, ln2_shift, up_bias, down_bias),
    )
    scalars = jnp.concatenate(
        [
            lax.axis_index("fsdp").reshape(1),
            lax.axis_index("ctx").reshape(1),
            (lax.axis_index("ctx") * spans).reshape(1),
            seq_lengths[0],
            span_order[0],
        ]
    ).astype(jnp.int32)
    far_weights = first_gather(weights, "fsdp")
    sums = span_sums(x, nc)
    nsum = lax.all_to_all(sums, "ctx", 0, 0, tiled=True).reshape(nc * spans, D)
    far_weights = after(far_weights, nsum)
    weights = gathered(weights, far_weights, "fsdp")
    up_weight = after(up_weight, far_weights)
    far_up = first_gather(up_weight, "fsdp")
    down_weight = after(down_weight, far_weights)
    far_down = first_gather(down_weight, "fsdp")

    packed, p, att, h1, wqkv, wout, vec, tabs = attend(
        scalars, x, span_order, nsum, weights, seqs
    )
    up = gathered(up_weight, after(far_up, att), "fsdp")
    r1, h2 = proj(x, att, wout, vec)
    g, gp, wup = ffn_up(scalars, h2, vec, up)
    dsend, dkeep = down_gradient(scalars, g, c, nf)
    down = gathered(down_weight, after(far_down, dkeep), "fsdp")
    queries, keys, values = tiles(after(packed, dkeep), tabs)
    gp = after(gp, queries)
    dh2, dub, usend, ukeep = ffn_down(scalars, h2, c, gp, wup, down)
    bits = ctx_bits()
    near = [("fsdp", 1 << k) for k in range(1, nf.bit_length() - 1)]

    seq = Sequence()
    from_down = Part(scalars, seq, dkeep, dsend)
    from_down.step(*near[0])
    dr1, da, gout, gvec = mid(c, seq.next(dh2), r1, att, wout, vec)
    seq.made(da)
    from_up = Part(scalars, seq, ukeep, usend)
    from_up.step("ctx", bits[0])
    da = seq.next(da)
    fixed = (x, da, h1, queries, keys, values, p, wqkv, vec, nsum)
    dh1, sums, fsend0, fkeep0, send, keep = back(scalars, fixed, (gout,), 0, nf, nc)
    seq.made(dh1)
    first = Part(scalars, seq, keep, send)
    from_down.step("ctx", bits[0])
    from_up.step(*near[0])
    dh1 = seq.next(dh1)
    upper, *old = back(scalars, fixed, (dub, gvec, dh1, sums), 1, nf, nc, last=False)
    seq.made(old[0])
    first.step("ctx", bits[0])
    feed = united(scalars, seq, [from_down, from_up])
    old[0] = seq.next(old[0])
    lower, _, fsend1, fkeep1, send, keep = back(
        scalars, fixed, (dub, gvec, dh1, sums), 1, nf, nc, old=old
    )
    seq.made(lower)
    second = Part(scalars, seq, keep, send)
    while feed.more():
        feed.step(FILL)
    first.split(*near[0], FILL)
    with_near = ((first.keep[0], first.send[0]),)
    with_ctx = ((fkeep0, fsend0), (fkeep1, fsend1))
    view = (2, 2, second.rows // 2, LANE)
    keep, got = (a.reshape(view) for a in (second.keep, *second.gots))
    own, to_ctx, to_near, to_both = quad(
        scalars, bits[0], seq.next(keep), got, with_near, with_ctx
    )
    seq.made(own)
    arrays = (
        own,
        swap(to_ctx, "ctx", bits[0]),
        swap(to_near, *near[0]),
        swap_both(to_both, bits[0], near[0][1]),
    )
    feed.end()
    heights = [second.total // 2] + [kept.shape[0] for kept, _ in (*with_near, *with_ctx)]
    sources, at, ends = [[(k, 0) for k in range(4)]], heights[0], {1: heights[0], 2: heights[0]}
    for n, rows in enumerate(heights[1:]):
        where = 2 if n < len(with_near) else 1
        sources.append([(0, at), (where, ends[where])])
        at += rows
        ends[where] += rows
    sizes = [rows // 2 for rows in heights]
    arrays = (seq.next(arrays[0]), *arrays[1:])
    halves = refold(scalars, bits[1], arrays, sizes, sources=sources)
    rest = Union(scalars, seq, halves, sizes, 2)
    mixed = block_output(scalars, seq.next(r1), g, vec, down)
    seq.made(mixed)
    while feed.at > 1:
        feed.join()
    while rest.more():
        rest.step()
    feed.join()
    own_span = rest.end()
    rest.join()
    tokens_grad = first_back(seq.next(x), dr1, upper, lower, own_span, wqkv, vec)
    seq.made(tokens_grad)
    while rest.gathering():
        rest.join()
    block = D // nf
    height, width = down_weight.shape[0], up_weight.shape[1]
    heights = (from_down.total, from_up.total)
    grad_down, grad_up = finish(
        scalars,
        feed.rows(),
        heights,
        [(height, D), (block, width)],
        [
            [height * j for j in range(D // LANE)],
            [heights[0] + block * j for j in range(width // LANE)],
        ],
    )
    seq.made(grad_down)
    half = PAIRS // 2
    plan = [
        [
            (second.total if p < half else 0) + block * (t * half + p % half)
            for t in range(3)
            for p in range(PAIRS)
        ],
        [second.total + block * (3 * half + j) for j in range(D // LANE)],
    ]
    shapes = [(block, 3 * D), (block, D)]
    at = 3 * half * block
    for wide in (block, block, 3 * block, block, block, block, 4 * block, block):
        shapes.append((wide,))
        plan.append([at + j for j in range(wide // LANE)])
        at += wide // LANE
    grad_qkv, grad_out, *vectors = finish(
        scalars, rest.rows(), (second.total, first.total), shapes, plan
    )
    g1, s1, qb, ob, g2, s2, ub, db = vectors
    return (
        mixed[None], tokens_grad[None], g1, s1, grad_qkv, qb, grad_out, ob, g2, s2,
        grad_up, ub, grad_down, db,
    )


def solution(mesh):
    rows, one, two = P("fsdp", "ctx", None), P("fsdp"), P("fsdp", None)
    return jax.shard_map(
        local,
        mesh=mesh,
        in_specs=(
            rows, one, one, two, one, two, one, one, one, two, one, two, one, two, two, rows,
        ),
        out_specs=(rows, rows, one, one, two, one, two, one, one, one, two, one, two, one),
        check_vma=False,
    )
```
